32 devices in a mesh: band: 8 (over y, x, core), samp: 4 (over z).
Axes of the slice: x: 2, y: 2, z: 4, core: 2. Of those that a mesh axis runs over, the one named last changes fastest.
Arguments:
- dosage: bfloat16 [8192, 4096], P('samp', 'band'), may hold values from -1 to 2, as said below
Outputs:
- linkage: float32 [4096, 2048], P(('band', 'samp'))
The draws below stay inside these ranges and needn't reach their ends.
Inputs may be any that keep to these rules, and one draw needn't show every extreme that they name: -1 marks a missing call; every other entry is an imputed dosage between 0 and 2.
All inputs are finite; a program needn't handle non-finite values.
Results may differ from the reference program's by a relative error of at most 0.0015.
Values may be sent and summed in bfloat16 or wider, within the bound.
A program may use at most 64 MiB of HBM per device.

```python
import jax
import jax.numpy as jnp
from jax import lax

TILE = 512
WIN = 2048
SAMPLES = 8192
SNPS = 4096


def draw_dosage(key, part):
    keys = jax.random.split(jax.random.fold_in(key, 17), 6)
    position = jnp.arange(SAMPLES, dtype=jnp.float32) / SAMPLES
    cohort = 0.5 + 1.5 * position
    freq = jax.random.uniform(keys[0], (SNPS,), jnp.float32, 0.05, 0.5)
    noise = 0.25 * jax.random.normal(keys[2], (SAMPLES, SNPS), jnp.float32)
    chance = jnp.clip(freq[None, :] * cohort[:, None], 0.0, 0.95)
    first = (jax.random.uniform(keys[1], (SAMPLES, SNPS), jnp.float32) < chance).astype(jnp.float32)
    second = (jax.random.uniform(keys[5], (SAMPLES, SNPS), jnp.float32) < chance).astype(jnp.float32)
    dose = jnp.clip(first + second + noise, 0.0, 2.0)
    rate = 0.02 + 0.1 * position
    missing = jax.random.uniform(keys[3], (SAMPLES, SNPS), jnp.float32) < rate[:, None]
    return jnp.where(missing, -1.0, dose).astype(jnp.bfloat16)


def setup_inputs(seed: int = 0) -> dict:
    key_of = jax.random.split(jax.random.key(seed), 2)
    return {
        "dosage": draw_dosage(jax.random.fold_in(key_of[1], 71), 0),
    }


def reference(dosage):
    raw = dosage.astype(jnp.float32)
    observed = (raw >= 0.0).astype(jnp.float32)
    values = observed * raw
    count = lax.optimization_barrier(jnp.sum(observed, axis=0))
    total = lax.optimization_barrier(jnp.sum(values, axis=0))
    square = lax.optimization_barrier(jnp.sum(values * values, axis=0))
    mean = (total + 1.0) / (count + 1.0)
    spread = (square - 2.0 * mean * total + count * mean * mean + 0.5) / (count + 1.0)
    scaled = (observed * (values - mean) * lax.rsqrt(spread)).astype(jnp.bfloat16)
    padded = jnp.pad(scaled, ((0, 0), (0, WIN - TILE)))

    def one_tile(index):
        rows = lax.dynamic_slice_in_dim(scaled, index * TILE, TILE, 1)
        columns = lax.dynamic_slice_in_dim(padded, index * TILE, WIN, 1)
        product = lax.dot_general(rows, columns, (((0,), (0,)), ((), ())), preferred_element_type=jnp.float32)
        return product / SAMPLES
    blocks = lax.map(one_tile, jnp.arange(SNPS // TILE, dtype=jnp.int32))
    return blocks.reshape(SNPS, WIN)
```

```python
import functools

import jax
import jax.numpy as jnp
from jax import lax
from jax.experimental import pallas as pl
from jax.experimental.pallas import tpu as pltpu
from jax.sharding import PartitionSpec as P

TILE = 512
WIN = 2048
PIECES = 4
MESH = pl.DeviceIdType.MESH


def remote(src, dst, send, recv, band, samp):
    return pltpu.make_async_remote_copy(
        src_ref=src, dst_ref=dst, send_sem=send, recv_sem=recv,
        device_id=(band, samp), device_id_type=MESH,
    )


def kernel(bands, shards, reach, samples, dosage_ref, out_ref, own_t, window, stats, stats_in, coef,
           coef_in, parts, far_parts, near_in, far_in, panel_s, panel_r, stat_s, stat_r, coef_s, coef_r,
           part_s, part_r, relay_s, work, raw_ref, load_s):
    band = lax.axis_index("band")
    samp = lax.axis_index("samp")
    depth, width = raw_ref.shape
    load = pltpu.make_async_copy(dosage_ref, raw_ref, load_s)
    load.start()
    rows = width // shards
    piece = width // PIECES
    half = shards // 2
    side, seat = samp // half, lax.rem(samp, half)
    near = [side * half + lax.rem(seat + d, half) for d in range(1, half)]
    far = [(1 - side) * half + lax.rem(seat + d, half) for d in range(half)]
    peers = far + near

    barrier = pltpu.get_barrier_semaphore()
    for peer in peers:
        pl.semaphore_signal(barrier, inc=1, device_id=(band, peer), device_id_type=MESH)
    expected = shards - 1
    for k in range(1, reach + 1):
        @pl.when(band >= k)
        def _():
            pl.semaphore_signal(barrier, inc=1, device_id=(band - k, samp), device_id_type=MESH)

        @pl.when(band + k < bands)
        def _():
            pl.semaphore_signal(barrier, inc=1, device_id=(band + k, samp), device_id_type=MESH)
    expected = expected + jnp.minimum(band, reach) + jnp.minimum(bands - 1 - band, reach)
    pl.semaphore_wait(barrier, expected)
    load.wait()

    def panel_copy(k, j):
        columns = pl.ds(pl.multiple_of(j * piece, piece), piece)
        return remote(raw_ref.at[:, columns], window.at[k - 1, :, columns],
                      panel_s.at[k - 1, j], panel_r.at[k - 1, j], jnp.maximum(band - k, 0), samp)

    even = lax.rem(band, 2) == 0
    turn = lax.rem(band, 4)

    def sends(k):
        if k == 1:
            return jnp.logical_not(even)
        if k == 2:
            return (band >= 2) & (turn != 0)
        return even & (band >= 3)

    def relay_copy(k, j):
        columns = pl.ds(pl.multiple_of(j * piece, piece), piece)
        onward = (k == 2) & jnp.logical_not(even)
        target = jnp.clip(jnp.where(onward, band - 1, band + 1), 0, bands - 1)
        slot = jnp.where(k == 3, 1, jnp.where(even, 0, 2))
        return remote(window.at[k - 1, :, columns], window.at[slot, :, columns],
                      relay_s.at[k - 2, j], panel_r.at[slot, j], target, samp)

    def coef_copy(k):
        return remote(coef, coef_in.at[k - 1], coef_s.at[k - 1], coef_r.at[k - 1],
                      jnp.maximum(band - k, 0), samp)

    def part_copy(k, j, d):
        columns = pl.ds(pl.multiple_of(k * width + j * piece, piece), piece)
        source, landing, slot = (far_parts, far_in, d) if d < half else (parts, near_in, d - half)
        return remote(source.at[pl.ds(pl.multiple_of(peers[d] * rows, rows), rows), columns],
                      landing.at[slot, :, columns],
                      part_s.at[k, j, d], part_r.at[k, j, d], band, peers[d])

    def start_panel(k, j):
        @pl.when(sends(k))
        def _():
            panel_copy(k, j).start()

    early = [(k, 0) for k in range(1, reach + 1)]
    later = [(k, j) for j in range(PIECES) for k in range(1, reach + 1) if (k, j) not in early]
    for k, j in early:
        start_panel(k, j)

    step = 64

    def add(i, carry):
        x = raw_ref[pl.ds(pl.multiple_of(i * step, step), step), :].astype(jnp.float32)
        seen = jnp.where(x >= 0.0, 1.0, 0.0)
        value = jnp.where(x >= 0.0, x, 0.0)
        fold = lambda a: jnp.sum(a.reshape(step // 8, 8, width), axis=0)
        return carry[0] + fold(seen), carry[1] + fold(value), carry[2] + fold(value * value)

    zero = jnp.zeros((8, width), jnp.float32)
    sums = lax.fori_loop(0, depth // step, add, (zero, zero, zero))
    stats[...] = jnp.concatenate(
        [jnp.sum(a, axis=0, keepdims=True) for a in sums] + [jnp.zeros((5, width), jnp.float32)], axis=0
    )
    stat_copies = [
        remote(stats, stats_in.at[d], stat_s.at[d], stat_r.at[d], band, peers[d])
        for d in range(shards - 1)
    ]
    for copy in stat_copies:
        copy.start()
    for copy in stat_copies:
        copy.wait()
    sums = stats[...]
    for d in range(shards - 1):
        sums = sums + stats_in[d]
    count, total, square = sums[0:1], sums[1:2], sums[2:3]
    mean = (total + 1.0) / (count + 1.0)
    spread = (square - 2.0 * mean * total + count * mean * mean + 0.5) / (count + 1.0)
    coef[...] = jnp.concatenate(
        [mean, lax.rsqrt(spread), jnp.zeros((6, width), jnp.float32)], axis=0
    )
    for k in range(1, reach + 1):
        @pl.when(band >= k)
        def _():
            coef_copy(k).start()
    for k, j in later:
        start_panel(k, j)

    chunk = 256

    def standard(x, mean, scale):
        x = x.astype(jnp.float32)
        return jnp.where(x >= 0.0, (x - mean) * scale, 0.0).astype(jnp.bfloat16)

    own = window.at[reach]

    def scale_own(i, _):
        span = pl.ds(pl.multiple_of(i * chunk, chunk), chunk)
        scaled = standard(raw_ref[span, :], coef[0:1, :], coef[1:2, :])
        own[span, :] = scaled
        own_t[:, span] = scaled.T
        return 0

    lax.fori_loop(0, depth // chunk, scale_own, 0)

    def correlate(k, j, panel):
        place = pl.ds(pl.multiple_of(k * width + j * piece, piece), piece)

        def block(i, _):
            span = pl.ds(pl.multiple_of(i * 256, 256), 256)
            total = jnp.dot(own_t[span, :], panel[...], preferred_element_type=jnp.float32)
            parts[span, place] = total
            far_parts[span, place] = total.astype(jnp.bfloat16)
            return 0

        lax.fori_loop(0, width // 256, block, 0)
        for d in range(shards - 1):
            part_copy(k, j, d).start()
        out_ref[:, place] = parts[pl.ds(pl.multiple_of(samp * rows, rows), rows), place]

    def finish(k, j):
        place = slice(k * width + j * piece, k * width + (j + 1) * piece)
        total = out_ref[:, place]
        for d in range(shards - 1):
            part_copy(k, j, d).wait()
            landed = far_in[d, :, place] if d < half else near_in[d - half, :, place]
            total = total + landed.astype(jnp.float32)
        out_ref[:, place] = total / samples

    for j in range(PIECES):
        correlate(0, j, own.at[:, pl.ds(j * piece, piece)])
    ahead = [(1, 0)]
    for j in range(PIECES):
        ahead += [(1, j + 1)] if j + 1 < PIECES else []
        ahead += [(k, j) for k in range(2, reach + 1)]
    level = [(k, j) for j in range(PIECES) for k in range(reach, 0, -1)]
    for (k_even, j_even), (k_odd, j_odd) in zip(ahead, level):
        k_last = k_odd if k_odd == 1 else reach + 2 - k_odd
        k = jnp.where(even, k_even, jnp.where(turn == 3, k_last, k_odd))
        j = jnp.where(even, j_even, j_odd)
        columns = pl.ds(pl.multiple_of(j * piece, piece), piece)

        @pl.when(band + k < bands)
        def _():
            panel_copy(k, j).wait_recv()

            @pl.when((k == 2) | ((k == 3) & (turn == 1)))
            def _():
                relay_copy(k, j).start()

            @pl.when(j == 0)
            def _():
                coef_copy(k).wait_recv()

            mean, scale = coef_in[k - 1, 0:1, columns], coef_in[k - 1, 1:2, columns]

            def rescale(i, _):
                span = pl.ds(pl.multiple_of(i * chunk, chunk), chunk)
                work[span, :] = standard(window[k - 1, span, columns], mean, scale)
                return 0

            lax.fori_loop(0, depth // chunk, rescale, 0)
            correlate(k, j, work)

    for j in range(PIECES):
        finish(0, j)
    for j in range(PIECES):
        for k in range(1, reach + 1):
            @pl.when(band + k < bands)
            def _():
                finish(k, j)

            @pl.when(band + k >= bands)
            def _():
                place = slice(k * width + j * piece, k * width + (j + 1) * piece)
                out_ref[:, place] = jnp.zeros((rows, piece), jnp.float32)
    for k in range(1, reach + 1):
        @pl.when(band >= k)
        def _():
            coef_copy(k).wait_send()

        for j in range(PIECES):
            @pl.when(sends(k))
            def _():
                panel_copy(k, j).wait_send()

            if k > 1:
                @pl.when((band + k < bands) & ((k == 2) | (turn == 1)))
                def _():
                    relay_copy(k, j).wait_send()


def general(bands, shards, dosage):
    depth, width = dosage.shape
    reach = (WIN - TILE + width - 1) // width
    rows = width // shards
    f32 = jnp.float32
    dma = pltpu.SemaphoreType.DMA
    return pl.pallas_call(
        functools.partial(kernel, bands, shards, reach, depth * shards),
        out_shape=jax.ShapeDtypeStruct((rows, WIN), f32),
        in_specs=[pl.BlockSpec(memory_space=pltpu.HBM)],
        out_specs=pl.BlockSpec(memory_space=pltpu.VMEM),
        scratch_shapes=[
            pltpu.VMEM((width, depth), jnp.bfloat16),
            pltpu.VMEM((reach + 1, depth, width), jnp.bfloat16),
            pltpu.VMEM((8, width), f32),
            pltpu.VMEM((shards - 1, 8, width), f32),
            pltpu.VMEM((8, width), f32),
            pltpu.VMEM((reach, 8, width), f32),
            pltpu.VMEM((width, WIN), f32),
            pltpu.VMEM((width, WIN), jnp.bfloat16),
            pltpu.VMEM((max(shards // 2 - 1, 1), rows, WIN), f32),
            pltpu.VMEM((shards // 2, rows, WIN), jnp.bfloat16),
            dma((reach, PIECES)), dma((reach, PIECES)),
            dma((shards - 1,)), dma((shards - 1,)),
            dma((reach,)), dma((reach,)),
            dma((reach + 1, PIECES, shards - 1)), dma((reach + 1, PIECES, shards - 1)),
            dma((reach - 1, PIECES)),
            pltpu.VMEM((depth, width // PIECES), jnp.bfloat16),
            pltpu.VMEM((depth, width), jnp.bfloat16),
            dma(()),
        ],
        compiler_params=pltpu.CompilerParams(
            collective_id=0, has_side_effects=True, vmem_limit_bytes=48 * 1024 * 1024
        ),
    )(dosage)


ORDER = (
    (4, 5, 0, 1, 2, 3),
    (0, 4, 1, 5, 2, 3),
    (0, 1, 2, 3, 15, 15),
    (0, 1, 2, 3, 15, 15),
    (15, 15, 15, 15, 15, 15),
    (15, 15, 15, 15, 15, 15),
    (0, 1, 2, 4, 3, 5),
    (4, 0, 5, 1, 2, 3),
)
RELAYS = (
    {0: 4, 3: 5},
    {5: 4, 7: 5},
    {4: 0, 5: 1},
    {},
    {},
    {4: 4, 5: 5},
    {},
    {0: 4, 1: 0, 4: 5, 5: 1, 7: 2, 9: 3},
)
SENDS = {
    2: [(0, 0, 0), (1, 0, 1), (2, 0, 2), (3, 0, 3)],
    3: [(2, 7, 4), (3, 7, 5), (0, 1, 0), (1, 1, 1), (0, 6, 4), (1, 6, 5)],
    4: [(0, 0, 4), (1, 0, 5), (2, 1, 4), (3, 1, 5), (2, 6, 2), (3, 6, 3)],
    5: [(0, 7, 0), (1, 7, 1), (2, 7, 2), (3, 7, 3)],
}
LATE = {3: {4: ((0,), (4, 5))}, 4: {1: ((0,), (2, 3)), 4: ((2,), (4, 5))}}
COEFS = {2: [(0, 0)], 3: [(1, 0), (6, 1), (7, 1)], 4: [(0, 1), (1, 1), (2, 0), (6, 0)], 5: [(7, 0), (3, 0)]}
SOURCES = ((0, 1, 0, 1), (0, 1, 0, 4), (0, 1, 0, 1), (0, 1, 0, 2), (0, 1, 2, 2), (0, 2, 2, 3), (0, 1, 3, 3), (0, 3, 3, 3))
NONE = 15


def ladder_kernel(bands, shards, samples, dosage_ref, out_ref, raw, rhs, lhs, window, parts, turned, total,
                  land, carry_in, stats, stats_in, coef, coef_in, load_s, panel_s, panel_r, relay_s, stat_s,
                  stat_r, coef_s, coef_r, twin_s, twin_r, part_s, part_r, carry_r, turned_s):
    band = lax.axis_index("band")
    samp = lax.axis_index("samp")
    pieces, depth, piece = raw.shape
    width = pieces * piece
    rows = width // shards
    core = lax.rem(band, 2)
    even = band - core
    twin = band + 1 - 2 * core
    upper = band >= 6
    outer = (samp == 0) | (samp == 3)
    inner = jnp.logical_not(outer)
    near = samp + 1 - 2 * lax.rem(samp, 2)
    middle = jnp.where(samp < 2, 2, 1)
    far = jnp.where(samp < 2, 3, 0)

    def pick(values):
        result = jnp.int32(values[0])
        for i, value in enumerate(values[1:], 1):
            result = jnp.where(band == i, jnp.int32(value), result)
        return result

    def among(*which):
        result = band == which[0]
        for i in which[1:]:
            result = result | (band == i)
        return result

    def lookup(table, n):
        result = jnp.int32(NONE)
        for b in range(bands):
            for i, value in (table[b].items() if isinstance(table[b], dict) else enumerate(table[b])):
                if value != NONE:
                    result = jnp.where((band == b) & (n == i), jnp.int32(value), result)
        return result

    loads = [
        pltpu.make_async_copy(dosage_ref.at[:, pl.ds(j * piece, piece)], raw.at[j], load_s.at[j])
        for j in range(pieces)
    ]
    for load in loads:
        load.start()
    barrier = pltpu.get_barrier_semaphore()
    for d in range(shards):
        for b in range(bands):
            if b or d:
                pl.semaphore_signal(
                    barrier, inc=1, device_id=(lax.rem(band + b, bands), lax.rem(samp + d, shards)),
                    device_id_type=MESH,
                )

    step = 256

    def measure(j, _):
        def add(i, carry):
            x = raw[j, pl.ds(pl.multiple_of(i * step, step), step), :].astype(jnp.float32)
            seen = jnp.where(x >= 0.0, 1.0, 0.0)
            value = jnp.maximum(x, 0.0)
            fold = lambda a: jnp.sum(a.reshape(step // 8, 8, piece), axis=0)
            return carry[0] + fold(seen), carry[1] + fold(value), carry[2] + fold(value * value)

        zero = jnp.zeros((8, piece), jnp.float32)
        sums = lax.fori_loop(0, depth // step, add, (zero, zero, zero))
        columns = pl.ds(pl.multiple_of(j * piece, piece), piece)
        stats[:, columns] = jnp.concatenate(
            [jnp.sum(a, axis=0, keepdims=True) for a in sums] + [jnp.zeros((5, piece), jnp.float32)], axis=0
        )
        return 0

    for load in loads:
        load.wait()
    lax.fori_loop(0, pieces, measure, 0)
    pl.semaphore_wait(barrier, bands * shards - 1)

    def panel_copy(source, i):
        j, target, slot = SENDS[source][i]
        return remote(raw.at[j], window.at[slot], panel_s.at[i], panel_r.at[slot], target, samp)

    late = {source: [i for _, (_, starts) in events.items() for i in starts] for source, events in LATE.items()}
    waited = {source: [i for _, (waits, _) in events.items() for i in waits] for source, events in LATE.items()}
    for source in SENDS:
        @pl.when(band == source)
        def _():
            for i in range(len(SENDS[source])):
                if i not in late.get(source, []):
                    panel_copy(source, i).start()

    stat_copies = [
        remote(stats, stats_in.at[d - 1], stat_s.at[d - 1], stat_r.at[d - 1], band, lax.rem(samp + d, shards))
        for d in range(1, shards)
    ]
    for copy in stat_copies:
        copy.start()
    for copy in stat_copies:
        copy.wait()
    sums = stats[...]
    for d in range(shards - 1):
        sums = sums + stats_in[d]
    count, sum1, square = sums[0:1], sums[1:2], sums[2:3]
    mean = (sum1 + 1.0) / (count + 1.0)
    spread = (square - 2.0 * mean * sum1 + count * mean * mean + 0.5) / (count + 1.0)
    coef[...] = jnp.concatenate([mean, lax.rsqrt(spread), jnp.zeros((6, width), jnp.float32)], axis=0)

    def coef_copy(source, i):
        target, slot = COEFS[source][i]
        return remote(coef, coef_in.at[slot], coef_s.at[i], coef_r.at[slot], target, samp)

    for source in COEFS:
        @pl.when(band == source)
        def _():
            for i in range(len(COEFS[source])):
                coef_copy(source, i).start()

    chunk = 256

    def standard(x, mean, scale):
        x = x.astype(jnp.float32)
        return jnp.where(x >= 0.0, (x - mean) * scale, 0.0).astype(jnp.bfloat16)

    def twin_copy(j):
        place = pl.ds(pl.multiple_of(core * width + j * piece, piece), piece)
        return remote(lhs.at[place, :], lhs.at[place, :], twin_s.at[j], twin_r.at[j], twin, samp)

    def twin_wait(j):
        place = pl.ds(pl.multiple_of((1 - core) * width + j * piece, piece), piece)
        return remote(lhs.at[place, :], lhs.at[place, :], twin_s.at[j], twin_r.at[j], twin, samp)

    def scale_own(j, _):
        columns = pl.ds(pl.multiple_of(j * piece, piece), piece)
        place = pl.ds(pl.multiple_of(core * width + j * piece, piece), piece)
        mean, scale = coef[0:1, columns], coef[1:2, columns]

        def part(i, _):
            span = pl.ds(pl.multiple_of(i * chunk, chunk), chunk)
            scaled = standard(raw[j, span, :], mean, scale)
            rhs[j, span, :] = scaled
            lhs[place, span] = scaled.T
            return 0

        lax.fori_loop(0, depth // chunk, part, 0)
        twin_copy(j).start()
        return 0

    lax.fori_loop(0, pieces, scale_own, 0)

    both_here = among(0, 1, 2, 3, 6, 7)
    single_here = among(0, 1, 6, 7)

    @pl.when(both_here)
    def _():
        remote(coef, coef_in.at[0], coef_s.at[0], coef_r.at[0], twin, samp).wait_recv()

    @pl.when(single_here)
    def _():
        remote(coef, coef_in.at[1], coef_s.at[0], coef_r.at[1], twin, samp).wait_recv()

    for j in range(pieces):
        twin_wait(j).wait_recv()

    def relay_copy(w):
        target = jnp.where(w < 4, pick((2, 2, 6, 0, 0, 1, 0, 3)), pick((2, 2, 6, 0, 0, 1, 0, 5)))
        slot = jnp.clip(w + pick((-4, -2, 0, 0, 0, -2, 0, 0)), 0, 5)
        return remote(window.at[w], window.at[slot], relay_s.at[w], panel_r.at[slot], target, samp)

    def arrival(w):
        return remote(window.at[w], window.at[w], relay_s.at[w], panel_r.at[w], twin, samp)

    def relayed(w):
        return (among(0, 1, 5) & (w >= 4)) | ((band == 2) & (w < 2)) | (band == 7)

    def job(n):
        w = lookup(ORDER, n - pieces)
        own = n < pieces
        active = own | (w != NONE)
        w = jnp.minimum(w, 5)
        both = jnp.logical_not(own) & (w < 4)
        single = jnp.logical_not(own) & (w >= 4)
        q = jnp.where(own, n, jnp.where(both, w, jnp.clip(2 * core + w - 4, 0, pieces - 1)))
        return w, own, both, single, active, q

    def spans(n, r):
        w, own, both, single, active, q = job(n)
        lower = active & (own | jnp.logical_not(upper))
        if r == 0:
            here = lower & jnp.logical_not(single)
        else:
            here = lower & (jnp.logical_not(own) | (core == 1))
        k = jnp.where(single, 3, jnp.where(own, 0, 2) + core - r)
        k = jnp.clip(k, 0, 3)
        return here, k, q

    def part_copy(n, r, k, q, i):
        columns = pl.ds(pl.multiple_of(k * width + q * piece, piece), piece)
        target = (near, middle, far, samp)[i]
        slot = (0, jnp.where(outer, 2, 1), 1, 3)[i]
        source = parts.at[n, pl.ds(pl.multiple_of(r * width + target * rows, rows), rows), :]
        return remote(source, land.at[slot, :, columns], part_s.at[n, r, i], part_r.at[k * pieces + q, slot],
                      even + r, target)

    def carry_copy(n, r):
        source = parts.at[n, pl.ds(pl.multiple_of(r * width + far * rows, rows), rows), :]
        return remote(source, carry_in.at[n, r], part_s.at[n, r, 2], carry_r.at[n, r], band, near)

    def turned_copy(n, w, single, q):
        cut = pl.ds(pl.multiple_of((2 - core) * width, width), 2 * width)
        whole = remote(turned.at[n - pieces], land.at[samp, :, cut], turned_s.at[n - pieces],
                       part_r.at[(2 - core) * pieces, samp], jnp.maximum(band - 2, 0), q)
        half = remote(turned.at[n - pieces, :, pl.ds(0, width)], land.at[samp, :, pl.ds(3 * width, width)],
                      turned_s.at[n - pieces], part_r.at[3 * pieces, samp], 3, q)
        return whole, half

    def carry_on(n):
        for r in range(2):
            here, k, q = spans(n, r)

            @pl.when(here & inner)
            def _():
                carry_copy(n, r).wait_recv()
                place = pl.ds(pl.multiple_of(r * width + far * rows, rows), rows)
                sent = total[lax.rem(n, 2), place, :] + carry_in[n, r].astype(jnp.float32)
                parts[n, place, :] = sent.astype(jnp.bfloat16)
                part_copy(n, r, k, q, 2).start()

    jobs = pieces + len(ORDER[0])
    block = 256

    def run(n, _):
        event = lookup(RELAYS, n)

        @pl.when(event != NONE)
        def _():
            w = jnp.minimum(event, 5)
            arrival(w).wait_recv()
            relay_copy(w).start()

        for source, events in LATE.items():
            for when, (waits, starts) in events.items():
                @pl.when((band == source) & (n == when))
                def _():
                    for i in waits:
                        panel_copy(source, i).wait_send()
                    for i in starts:
                        panel_copy(source, i).start()

        w, own, both, single, active, q = job(n)

        @pl.when(active)
        def _():
            @pl.when(jnp.logical_not(own))
            def _():
                @pl.when(jnp.logical_not(relayed(w)))
                def _():
                    arrival(w).wait_recv()

                slot = jnp.where(both, 0, 1)
                columns = pl.ds(pl.multiple_of(q * piece, piece), piece)
                mean, scale = coef_in[slot, 0:1, columns], coef_in[slot, 1:2, columns]

                def rescale(i, _):
                    span = pl.ds(pl.multiple_of(i * chunk, chunk), chunk)
                    rhs[pieces, span, :] = standard(window[w, span, :], mean, scale)
                    return 0

                lax.fori_loop(0, depth // chunk, rescale, 0)

            index = jnp.where(own, q, pieces)
            first = jnp.where(single & jnp.logical_not(upper), width // block, 0)
            short = (own & (core == 0)) | (single & upper)
            last = jnp.where(short, width // block, 2 * width // block)

            def multiply(i, _):
                place = pl.ds(pl.multiple_of(i * block, block), block)
                result = jnp.dot(lhs[place, :], rhs[index], preferred_element_type=jnp.float32)

                @pl.when(own | jnp.logical_not(upper))
                def _():
                    total[lax.rem(n, 2), place, :] = result
                    parts[n, place, :] = result.astype(jnp.bfloat16)

                @pl.when(jnp.logical_not(own) & upper)
                def _():
                    turned[n - pieces, :, place] = result.T.astype(jnp.bfloat16)

                return 0

            lax.fori_loop(first, last, multiply, 0)

            for r in range(2):
                here, k, q_ = spans(n, r)

                @pl.when(here)
                def _():
                    @pl.when(outer)
                    def _():
                        carry_copy(n, r).start()

                    part_copy(n, r, k, q, 1).start()
                    part_copy(n, r, k, q, 0).start()

                    @pl.when(core != r)
                    def _():
                        part_copy(n, r, k, q, 3).start()

                    @pl.when(core == r)
                    def _():
                        place = pl.ds(pl.multiple_of(r * width + samp * rows, rows), rows)
                        columns = pl.ds(pl.multiple_of(k * width + q * piece, piece), piece)
                        out_ref[:, columns] = total[lax.rem(n, 2), place, :]

            whole, half = turned_copy(jnp.maximum(n, pieces), w, single, q)

            @pl.when(both & upper)
            def _():
                whole.start()

            @pl.when(single & upper)
            def _():
                half.start()

        @pl.when(n > 0)
        def _():
            carry_on(jnp.maximum(n - 1, 0))

        return 0

    lax.fori_loop(0, jobs, run, 0)
    carry_on(jobs - 1)

    def finish(k):
        kind = pick([row[k] for row in SOURCES])
        for q in range(pieces):
            here = kind if k < 3 else jnp.where(kind == 4, 1 if q < pieces // 2 else 0, kind)
            place = slice(k * width + q * piece, k * width + (q + 1) * piece)

            def landed(slot):
                return remote(land.at[slot, :, place], land.at[slot, :, place], part_s.at[0, 0, 0],
                              part_r.at[k * pieces + q, slot], twin, samp)

            @pl.when(here < 2)
            def _():
                landed(0).wait_recv()
                landed(1).wait_recv()

                @pl.when(here == 1)
                def _():
                    landed(3).wait_recv()
                    out_ref[:, place] = land[3, :, place].astype(jnp.float32)

                @pl.when(inner)
                def _():
                    landed(2).wait_recv()
                    out_ref[:, place] += land[2, :, place].astype(jnp.float32)

                result = out_ref[:, place] + land[0, :, place].astype(jnp.float32)
                out_ref[:, place] = (result + land[1, :, place].astype(jnp.float32)) / samples

        @pl.when(kind == 3)
        def _():
            out_ref[:, k * width:(k + 1) * width] = jnp.zeros((rows, width), jnp.float32)

    def gather(k, span):
        place = slice(k * width, (k + span) * width)
        for z in range(shards):
            remote(land.at[z, :, place], land.at[z, :, place], part_s.at[0, 0, 0], part_r.at[k * pieces, z],
                   twin, samp).wait_recv()
        result = land[0, :, place].astype(jnp.float32)
        for z in range(1, shards):
            result = result + land[z, :, place].astype(jnp.float32)
        out_ref[:, place] = result / samples

    for k in range(4):
        finish(k)
    for b, k, span in ((3, 3, 1), (4, 2, 2), (5, 1, 2)):
        @pl.when(band == b)
        def _():
            gather(k, span)

    for source in SENDS:
        @pl.when(band == source)
        def _():
            for i in range(len(SENDS[source])):
                if i not in waited.get(source, []):
                    panel_copy(source, i).wait_send()
            for i in range(len(COEFS[source])):
                coef_copy(source, i).wait_send()
    for w in range(6):
        @pl.when(relayed(w))
        def _():
            relay_copy(jnp.int32(w)).wait_send()
    for j in range(pieces):
        twin_copy(j).wait_send()

    def settle(n, _):
        w, own, both, single, active, q = job(n)
        for r in range(2):
            here, k, q_ = spans(n, r)

            @pl.when(here)
            def _():
                part_copy(n, r, k, q, 0).wait_send()
                part_copy(n, r, k, q, 1).wait_send()
                part_copy(n, r, k, q, 2).wait_send()

                @pl.when(core != r)
                def _():
                    part_copy(n, r, k, q, 3).wait_send()

        whole, half = turned_copy(jnp.maximum(n, pieces), w, single, q)

        @pl.when(both & upper)
        def _():
            whole.wait_send()

        @pl.when(single & upper & active)
        def _():
            half.wait_send()

        return 0

    lax.fori_loop(0, jobs, settle, 0)


def ladder(bands, shards, dosage):
    depth, width = dosage.shape
    pieces = shards
    piece = width // pieces
    rows = width // shards
    jobs = pieces + len(ORDER[0])
    f32, b16 = jnp.float32, jnp.bfloat16
    dma = pltpu.SemaphoreType.DMA
    return pl.pallas_call(
        functools.partial(ladder_kernel, bands, shards, depth * shards),
        out_shape=jax.ShapeDtypeStruct((rows, WIN), f32),
        in_specs=[pl.BlockSpec(memory_space=pltpu.HBM)],
        out_specs=pl.BlockSpec(memory_space=pltpu.VMEM),
        scratch_shapes=[
            pltpu.VMEM((pieces, depth, piece), b16),
            pltpu.VMEM((pieces + 1, depth, piece), b16),
            pltpu.VMEM((2 * width, depth), b16),
            pltpu.VMEM((6, depth, piece), b16),
            pltpu.VMEM((jobs, 2 * width, piece), b16),
            pltpu.VMEM((jobs - pieces, rows, 2 * width), b16),
            pltpu.VMEM((2, 2 * width, piece), f32),
            pltpu.VMEM((4, rows, WIN), b16),
            pltpu.VMEM((jobs, 2, rows, piece), b16),
            pltpu.VMEM((8, width), f32),
            pltpu.VMEM((shards - 1, 8, width), f32),
            pltpu.VMEM((8, width), f32),
            pltpu.VMEM((2, 8, width), f32),
            dma((pieces,)),
            dma((6,)), dma((6,)), dma((6,)),
            dma((shards - 1,)), dma((shards - 1,)),
            dma((4,)), dma((2,)),
            dma((pieces,)), dma((pieces,)),
            dma((jobs, 2, 4)), dma((4 * pieces, 4)), dma((jobs, 2)),
            dma((jobs - pieces,)),
        ],
        compiler_params=pltpu.CompilerParams(
            collective_id=0, has_side_effects=True, vmem_limit_bytes=48 * 1024 * 1024
        ),
    )(dosage)


def on_device(bands, shards, dosage):
    if bands == len(ORDER) and shards == 4 and dosage.shape[1] == TILE:
        return ladder(bands, shards, dosage)
    return general(bands, shards, dosage)


def solution(mesh):
    return jax.shard_map(
        functools.partial(on_device, mesh.shape["band"], mesh.shape["samp"]),
        mesh=mesh,
        in_specs=(P("samp", "band"),),
        out_specs=P(("band", "samp"), None),
        check_vma=False,
    )
```

```python
import functools

import jax
import jax.numpy as jnp
from jax import lax
from jax.experimental import pallas as pl
from jax.experimental.pallas import tpu as pltpu
from jax.sharding import PartitionSpec as P

TILE = 512
WIN = 2048
PIECES = 4
MESH = pl.DeviceIdType.MESH


def remote(src, dst, send, recv, band, samp):
    return pltpu.make_async_remote_copy(
        src_ref=src, dst_ref=dst, send_sem=send, recv_sem=recv,
        device_id=(band, samp), device_id_type=MESH,
    )


def kernel(bands, shards, reach, samples, dosage_ref, out_ref, own_t, window, stats, stats_in, coef,
           coef_in, parts, far_parts, near_in, far_in, panel_s, panel_r, stat_s, stat_r, coef_s, coef_r,
           part_s, part_r, relay_s, work, raw_ref, load_s):
    band = lax.axis_index("band")
    samp = lax.axis_index("samp")
    depth, width = raw_ref.shape
    load = pltpu.make_async_copy(dosage_ref, raw_ref, load_s)
    load.start()
    rows = width // shards
    piece = width // PIECES
    half = shards // 2
    side, seat = samp // half, lax.rem(samp, half)
    near = [side * half + lax.rem(seat + d, half) for d in range(1, half)]
    far = [(1 - side) * half + lax.rem(seat + d, half) for d in range(half)]
    peers = far + near

    barrier = pltpu.get_barrier_semaphore()
    for peer in peers:
        pl.semaphore_signal(barrier, inc=1, device_id=(band, peer), device_id_type=MESH)
    expected = shards - 1
    for k in range(1, reach + 1):
        @pl.when(band >= k)
        def _():
            pl.semaphore_signal(barrier, inc=1, device_id=(band - k, samp), device_id_type=MESH)

        @pl.when(band + k < bands)
        def _():
            pl.semaphore_signal(barrier, inc=1, device_id=(band + k, samp), device_id_type=MESH)
    expected = expected + jnp.minimum(band, reach) + jnp.minimum(bands - 1 - band, reach)
    pl.semaphore_wait(barrier, expected)
    load.wait()

    def panel_copy(k, j):
        columns = pl.ds(pl.multiple_of(j * piece, piece), piece)
        return remote(raw_ref.at[:, columns], window.at[k - 1, :, columns],
                      panel_s.at[k - 1, j], panel_r.at[k - 1, j], jnp.maximum(band - k, 0), samp)

    even = lax.rem(band, 2) == 0
    turn = lax.rem(band, 4)

    def sends(k):
        if k == 1:
            return jnp.logical_not(even)
        if k == 2:
            return (band >= 2) & (turn != 0)
        return even & (band >= 3)

    def relay_copy(k, j):
        columns = pl.ds(pl.multiple_of(j * piece, piece), piece)
        onward = (k == 2) & jnp.logical_not(even)
        target = jnp.clip(jnp.where(onward, band - 1, band + 1), 0, bands - 1)
        slot = jnp.where(k == 3, 1, jnp.where(even, 0, 2))
        return remote(window.at[k - 1, :, columns], window.at[slot, :, columns],
                      relay_s.at[k - 2, j], panel_r.at[slot, j], target, samp)

    def coef_copy(k):
        return remote(coef, coef_in.at[k - 1], coef_s.at[k - 1], coef_r.at[k - 1],
                      jnp.maximum(band - k, 0), samp)

    def part_copy(k, j, d):
        columns = pl.ds(pl.multiple_of(k * width + j * piece, piece), piece)
        source, landing, slot = (far_parts, far_in, d) if d < half else (parts, near_in, d - half)
        return remote(source.at[pl.ds(pl.multiple_of(peers[d] * rows, rows), rows), columns],
                      landing.at[slot, :, columns],
                      part_s.at[k, j, d], part_r.at[k, j, d], band, peers[d])

    def start_panel(k, j):
        @pl.when(sends(k))
        def _():
            panel_copy(k, j).start()

    early = [(k, 0) for k in range(1, reach + 1)]
    later = [(k, j) for j in range(PIECES) for k in range(1, reach + 1) if (k, j) not in early]
    for k, j in early:
        start_panel(k, j)

    step = 64

    def add(i, carry):
        x = raw_ref[pl.ds(pl.multiple_of(i * step, step), step), :].astype(jnp.float32)
        seen = jnp.where(x >= 0.0, 1.0, 0.0)
        value = jnp.where(x >= 0.0, x, 0.0)
        fold = lambda a: jnp.sum(a.reshape(step // 8, 8, width), axis=0)
        return carry[0] + fold(seen), carry[1] + fold(value), carry[2] + fold(value * value)

    zero = jnp.zeros((8, width), jnp.float32)
    sums = lax.fori_loop(0, depth // step, add, (zero, zero, zero))
    stats[...] = jnp.concatenate(
        [jnp.sum(a, axis=0, keepdims=True) for a in sums] + [jnp.zeros((5, width), jnp.float32)], axis=0
    )
    stat_copies = [
        remote(stats, stats_in.at[d], stat_s.at[d], stat_r.at[d], band, peers[d])
        for d in range(shards - 1)
    ]
    for copy in stat_copies:
        copy.start()
    for copy in stat_copies:
        copy.wait()
    sums = stats[...]
    for d in range(shards - 1):
        sums = sums + stats_in[d]
    count, total, square = sums[0:1], sums[1:2], sums[2:3]
    mean = (total + 1.0) / (count + 1.0)
    spread = (square - 2.0 * mean * total + count * mean * mean + 0.5) / (count + 1.0)
    coef[...] = jnp.concatenate(
        [mean, lax.rsqrt(spread), jnp.zeros((6, width), jnp.float32)], axis=0
    )
    for k in range(1, reach + 1):
        @pl.when(band >= k)
        def _():
            coef_copy(k).start()
    for k, j in later:
        start_panel(k, j)

    chunk = 256

    def standard(x, mean, scale):
        x = x.astype(jnp.float32)
        return jnp.where(x >= 0.0, (x - mean) * scale, 0.0).astype(jnp.bfloat16)

    own = window.at[reach]

    def scale_own(i, _):
        span = pl.ds(pl.multiple_of(i * chunk, chunk), chunk)
        scaled = standard(raw_ref[span, :], coef[0:1, :], coef[1:2, :])
        own[span, :] = scaled
        own_t[:, span] = scaled.T
        return 0

    lax.fori_loop(0, depth // chunk, scale_own, 0)

    def correlate(k, j, panel):
        place = pl.ds(pl.multiple_of(k * width + j * piece, piece), piece)

        def block(i, _):
            span = pl.ds(pl.multiple_of(i * 256, 256), 256)
            total = jnp.dot(own_t[span, :], panel[...], preferred_element_type=jnp.float32)
            parts[span, place] = total
            far_parts[span, place] = total.astype(jnp.bfloat16)
            return 0

        lax.fori_loop(0, width // 256, block, 0)
        for d in range(shards - 1):
            part_copy(k, j, d).start()
        out_ref[:, place] = parts[pl.ds(pl.multiple_of(samp * rows, rows), rows), place]

    def finish(k, j):
        place = slice(k * width + j * piece, k * width + (j + 1) * piece)
        total = out_ref[:, place]
        for d in range(shards - 1):
            part_copy(k, j, d).wait()
            landed = far_in[d, :, place] if d < half else near_in[d - half, :, place]
            total = total + landed.astype(jnp.float32)
        out_ref[:, place] = total / samples

    for j in range(PIECES):
        correlate(0, j, own.at[:, pl.ds(j * piece, piece)])
    ahead = [(1, 0)]
    for j in range(PIECES):
        ahead += [(1, j + 1)] if j + 1 < PIECES else []
        ahead += [(k, j) for k in range(2, reach + 1)]
    level = [(k, j) for j in range(PIECES) for k in range(reach, 0, -1)]
    for (k_even, j_even), (k_odd, j_odd) in zip(ahead, level):
        k_last = k_odd if k_odd == 1 else reach + 2 - k_odd
        k = jnp.where(even, k_even, jnp.where(turn == 3, k_last, k_odd))
        j = jnp.where(even, j_even, j_odd)
        columns = pl.ds(pl.multiple_of(j * piece, piece), piece)

        @pl.when(band + k < bands)
        def _():
            panel_copy(k, j).wait_recv()

            @pl.when((k == 2) | ((k == 3) & (turn == 1)))
            def _():
                relay_copy(k, j).start()

            @pl.when(j == 0)
            def _():
                coef_copy(k).wait_recv()

            mean, scale = coef_in[k - 1, 0:1, columns], coef_in[k - 1, 1:2, columns]

            def rescale(i, _):
                span = pl.ds(pl.multiple_of(i * chunk, chunk), chunk)
                work[span, :] = standard(window[k - 1, span, columns], mean, scale)
                return 0

            lax.fori_loop(0, depth // chunk, rescale, 0)
            correlate(k, j, work)

    for j in range(PIECES):
        finish(0, j)
    for j in range(PIECES):
        for k in range(1, reach + 1):
            @pl.when(band + k < bands)
            def _():
                finish(k, j)

            @pl.when(band + k >= bands)
            def _():
                place = slice(k * width + j * piece, k * width + (j + 1) * piece)
                out_ref[:, place] = jnp.zeros((rows, piece), jnp.float32)
    for k in range(1, reach + 1):
        @pl.when(band >= k)
        def _():
            coef_copy(k).wait_send()

        for j in range(PIECES):
            @pl.when(sends(k))
            def _():
                panel_copy(k, j).wait_send()

            if k > 1:
                @pl.when((band + k < bands) & ((k == 2) | (turn == 1)))
                def _():
                    relay_copy(k, j).wait_send()


def general(bands, shards, dosage):
    depth, width = dosage.shape
    reach = (WIN - TILE + width - 1) // width
    rows = width // shards
    f32 = jnp.float32
    dma = pltpu.SemaphoreType.DMA
    return pl.pallas_call(
        functools.partial(kernel, bands, shards, reach, depth * shards),
        out_shape=jax.ShapeDtypeStruct((rows, WIN), f32),
        in_specs=[pl.BlockSpec(memory_space=pltpu.HBM)],
        out_specs=pl.BlockSpec(memory_space=pltpu.VMEM),
        scratch_shapes=[
            pltpu.VMEM((width, depth), jnp.bfloat16),
            pltpu.VMEM((reach + 1, depth, width), jnp.bfloat16),
            pltpu.VMEM((8, width), f32),
            pltpu.VMEM((shards - 1, 8, width), f32),
            pltpu.VMEM((8, width), f32),
            pltpu.VMEM((reach, 8, width), f32),
            pltpu.VMEM((width, WIN), f32),
            pltpu.VMEM((width, WIN), jnp.bfloat16),
            pltpu.VMEM((max(shards // 2 - 1, 1), rows, WIN), f32),
            pltpu.VMEM((shards // 2, rows, WIN), jnp.bfloat16),
            dma((reach, PIECES)), dma((reach, PIECES)),
            dma((shards - 1,)), dma((shards - 1,)),
            dma((reach,)), dma((reach,)),
            dma((reach + 1, PIECES, shards - 1)), dma((reach + 1, PIECES, shards - 1)),
            dma((reach - 1, PIECES)),
            pltpu.VMEM((depth, width // PIECES), jnp.bfloat16),
            pltpu.VMEM((depth, width), jnp.bfloat16),
            dma(()),
        ],
        compiler_params=pltpu.CompilerParams(
            collective_id=0, has_side_effects=True, vmem_limit_bytes=48 * 1024 * 1024
        ),
    )(dosage)


ORDER = (
    (4, 5, 0, 1, 2, 3),
    (0, 4, 1, 5, 2, 3),
    (0, 1, 2, 3, 15, 15),
    (0, 1, 2, 3, 15, 15),
    (15, 15, 15, 15, 15, 15),
    (15, 15, 15, 15, 15, 15),
    (4, 0, 2, 5, 1, 3),
    (4, 0, 5, 1, 2, 3),
)
RELAYS = (
    {0: 4, 3: 5},
    {5: 4, 7: 5},
    {4: 0, 5: 1},
    {},
    {},
    {7: 4, 8: 5},
    {},
    {0: 4, 1: 0, 4: 5, 5: 1, 7: 2, 9: 3},
)
SENDS = {
    2: [(0, 0, 0), (1, 0, 1), (2, 0, 2), (3, 0, 3)],
    3: [(2, 7, 4), (3, 7, 5), (0, 1, 0), (1, 1, 1), (0, 6, 4), (1, 6, 5)],
    4: [(0, 0, 4), (1, 0, 5), (2, 1, 4), (3, 1, 5), (2, 6, 2), (3, 6, 3)],
    5: [(0, 7, 0), (1, 7, 1), (2, 7, 2), (3, 7, 3)],
}
EARLY = {2: (0,), 3: (0, 2), 4: (0,), 5: (0,)}
LATE = {3: {1: ((0,), (4, 5))}, 4: {1: ((0,), (2, 3)), 3: ((2,), (4, 5))}}
COEFS = {2: [(0, 0)], 3: [(1, 0), (6, 1), (7, 1)], 4: [(0, 1), (1, 1), (2, 0), (6, 0)], 5: [(7, 0), (3, 0)]}
SOURCES = ((0, 1, 0, 1), (0, 1, 0, 4), (0, 1, 0, 1), (0, 1, 0, 2), (0, 1, 2, 2), (0, 2, 2, 3), (0, 1, 3, 3), (0, 3, 3, 3))
CROSS = {3: (6, 7), 4: (6,), 6: (3, 4), 7: (3,)}
HOLD = {6: 0, 7: 1, 8: 2, 9: 3}
LAG = 2
NONE = 15


def peers(bands):
    plane = {b: {b + 1 - 2 * (b % 2)} for b in range(bands)}
    pairs = [(b, target) for b in SENDS for _, target, _ in SENDS[b]] + [(b, target) for b in COEFS for target, _ in COEFS[b]]
    pairs += [(0, 2), (1, 2), (2, 6), (5, 1), (7, 3), (7, 5)] + [(b, target) for b in CROSS for target in CROSS[b]]
    for a, b in pairs:
        plane[a].add(b)
        plane[b].add(a)
    line = {b: {b, b + 1 - 2 * (b % 2), *CROSS.get(b, ())} for b in range(bands)}
    return plane, line


def ladder_kernel(bands, shards, samples, dosage_ref, out_ref, raw, rhs, lhs, window, parts, turned, total,
                  land, carry_in, stats, stats_in, coef, coef_in, load_s, panel_s, panel_r, relay_s, stat_s,
                  stat_r, coef_s, coef_r, twin_s, twin_r, part_s, part_r, carry_r, hold, hold_s, hold_r, keep):
    band = lax.axis_index("band")
    samp = lax.axis_index("samp")
    pieces, depth, piece = raw.shape
    width = pieces * piece
    rows = width // shards
    core = lax.rem(band, 2)
    even = band - core
    twin = band + 1 - 2 * core
    upper = band >= 6
    outer = (samp == 0) | (samp == 3)
    inner = jnp.logical_not(outer)
    near = samp + 1 - 2 * lax.rem(samp, 2)
    middle = jnp.where(samp < 2, 2, 1)
    far = jnp.where(samp < 2, 3, 0)

    def pick(values):
        result = jnp.int32(values[0])
        for i, value in enumerate(values[1:], 1):
            result = jnp.where(band == i, jnp.int32(value), result)
        return result

    def among(*which):
        result = band == which[0]
        for i in which[1:]:
            result = result | (band == i)
        return result

    def lookup(table, n):
        result = jnp.int32(NONE)
        for b in range(bands):
            for i, value in (table[b].items() if isinstance(table[b], dict) else enumerate(table[b])):
                if value != NONE:
                    result = jnp.where((band == b) & (n == i), jnp.int32(value), result)
        return result

    loads = [
        pltpu.make_async_copy(dosage_ref.at[:, pl.ds(j * piece, piece)], raw.at[j], load_s.at[j])
        for j in range(pieces)
    ]
    for load in loads:
        load.start()
    barrier = pltpu.get_barrier_semaphore()
    plane, line = peers(bands)
    for b in range(bands):
        @pl.when(band == b)
        def _():
            for peer in sorted(plane[b]):
                pl.semaphore_signal(barrier, inc=1, device_id=(peer, samp), device_id_type=MESH)
            for peer in sorted(line[b]):
                for d in range(1, shards):
                    pl.semaphore_signal(barrier, inc=1, device_id=(peer, lax.rem(samp + d, shards)),
                                        device_id_type=MESH)

    step = 256

    def measure(j, _):
        def add(i, carry):
            x = raw[j, pl.ds(pl.multiple_of(i * step, step), step), :].astype(jnp.float32)
            seen = jnp.where(x >= 0.0, 1.0, 0.0)
            value = jnp.maximum(x, 0.0)
            fold = lambda a: jnp.sum(a.reshape(step // 8, 8, piece), axis=0)
            return carry[0] + fold(seen), carry[1] + fold(value), carry[2] + fold(value * value)

        zero = jnp.zeros((8, piece), jnp.float32)
        sums = lax.fori_loop(0, depth // step, add, (zero, zero, zero))
        columns = pl.ds(pl.multiple_of(j * piece, piece), piece)
        stats[:, columns] = jnp.concatenate(
            [jnp.sum(a, axis=0, keepdims=True) for a in sums] + [jnp.zeros((5, piece), jnp.float32)], axis=0
        )
        return 0

    for load in loads:
        load.wait()
    lax.fori_loop(0, pieces, measure, 0)
    pl.semaphore_wait(barrier, pick([len(plane[b]) + (shards - 1) * len(line[b]) for b in range(bands)]))

    def panel_copy(source, i):
        j, target, slot = SENDS[source][i]
        return remote(raw.at[j], window.at[slot], panel_s.at[i], panel_r.at[slot], target, samp)

    late = {source: [i for _, (_, starts) in events.items() for i in starts] for source, events in LATE.items()}
    waited = {source: [i for _, (waits, _) in events.items() for i in waits] for source, events in LATE.items()}
    for source in SENDS:
        @pl.when(band == source)
        def _():
            for i in EARLY[source]:
                panel_copy(source, i).start()

    stat_copies = [
        remote(stats, stats_in.at[d - 1], stat_s, stat_r, band, lax.rem(samp + d, shards))
        for d in range(1, shards)
    ]
    for copy in stat_copies:
        copy.start()
    remote(stats_in, stats_in, stat_s, stat_r, twin, samp).wait()
    sums = stats[...]
    for d in range(shards - 1):
        sums = sums + stats_in[d]
    count, sum1, square = sums[0:1], sums[1:2], sums[2:3]
    mean = (sum1 + 1.0) / (count + 1.0)
    spread = (square - 2.0 * mean * sum1 + count * mean * mean + 0.5) / (count + 1.0)
    coef[...] = jnp.concatenate([mean, lax.rsqrt(spread), jnp.zeros((6, width), jnp.float32)], axis=0)

    def coef_copy(source, i):
        target, slot = COEFS[source][i]
        return remote(coef, coef_in.at[slot], coef_s.at[i], coef_r.at[slot], target, samp)

    for source in COEFS:
        @pl.when(band == source)
        def _():
            for i in range(len(COEFS[source])):
                coef_copy(source, i).start()
            for i in range(len(SENDS[source])):
                if i not in late.get(source, []) and i not in EARLY[source]:
                    panel_copy(source, i).start()

    chunk = 256

    def standard(x, mean, scale):
        x = x.astype(jnp.float32)
        return jnp.where(x >= 0.0, (x - mean) * scale, 0.0).astype(jnp.bfloat16)

    def twin_copy(j):
        place = pl.ds(pl.multiple_of(core * width + j * piece, piece), piece)
        return remote(lhs.at[place, :], lhs.at[place, :], twin_s, twin_r, twin, samp)

    def twin_wait():
        place = pl.ds(pl.multiple_of((1 - core) * width, width), width)
        return remote(lhs.at[place, :], lhs.at[place, :], twin_s, twin_r, twin, samp)

    def scale_own(j, _):
        columns = pl.ds(pl.multiple_of(j * piece, piece), piece)
        place = pl.ds(pl.multiple_of(core * width + j * piece, piece), piece)
        mean, scale = coef[0:1, columns], coef[1:2, columns]

        def part(i, _):
            span = pl.ds(pl.multiple_of(i * chunk, chunk), chunk)
            scaled = standard(raw[j, span, :], mean, scale)
            rhs[j, span, :] = scaled
            lhs[place, span] = scaled.T
            return 0

        lax.fori_loop(0, depth // chunk, part, 0)
        twin_copy(j).start()
        return 0

    lax.fori_loop(0, pieces, scale_own, 0)

    def relay_copy(w):
        target = jnp.where(w < 4, pick((2, 2, 6, 0, 0, 1, 0, 3)), pick((2, 2, 6, 0, 0, 1, 0, 5)))
        slot = jnp.clip(w + pick((-4, -2, 0, 0, 0, -2, 0, 0)), 0, 5)
        return remote(window.at[w], window.at[slot], relay_s.at[w], panel_r.at[slot], target, samp)

    def arrival(w):
        return remote(window.at[w], window.at[w], relay_s.at[w], panel_r.at[w], twin, samp)

    def relayed(w):
        return (among(0, 1, 5) & (w >= 4)) | ((band == 2) & (w < 2)) | (band == 7)

    def job(n):
        w = lookup(ORDER, n - pieces)
        own = n < pieces
        active = own | (w != NONE)
        w = jnp.minimum(w, 5)
        both = jnp.logical_not(own) & (w < 4)
        single = jnp.logical_not(own) & (w >= 4)
        q = jnp.where(own, n, jnp.where(both, w, jnp.clip(2 * core + w - 4, 0, pieces - 1)))
        return w, own, both, single, active, q

    def needs(n, r):
        w, own, both, single, active, q = job(n)
        return active & (both | (own & ((r == 0) | (core == 1))) | (single & (r == jnp.where(upper, 0, 1))))

    def block_of(n, r):
        w, own, both, single, active, q = job(n)
        return jnp.clip(jnp.where(single, 3, jnp.where(own, 0, 2) + core - r), 0, 3)

    def lower(n):
        return (n < pieces) | jnp.logical_not(upper)

    def part_copy(n, r, k, q, i):
        columns = pl.ds(pl.multiple_of(k * width + q * piece, piece), piece)
        target = (near, middle, far, samp)[i]
        slot = (0, jnp.where(outer, 2, 1), 1, 3)[i]
        source = parts.at[pl.ds(pl.multiple_of(n * 2 * width + r * width + target * rows, rows), rows), :]
        return remote(source, land.at[slot, :, columns], part_s, part_r.at[k, slot],
                      even + r, target)

    def carry_copy(n, r):
        source = parts.at[pl.ds(pl.multiple_of(n * 2 * width + r * width + far * rows, rows), rows), :]
        return remote(source, carry_in.at[n, r], part_s, carry_r.at[n], band, near)

    def turned_copy(n, r, single, q, held):
        k = jnp.clip(jnp.where(single, 3, 2 - core + r), 0, 3)
        source = turned.at[n - pieces, :, pl.ds(pl.multiple_of(r * width, width), width)]
        to = jnp.where(single, 3, jnp.maximum(band - 2, 0))
        if held:
            return remote(source, hold.at[q, r], part_s, hold_r.at[q], to, samp)
        return remote(source, land.at[samp, :, pl.ds(pl.multiple_of(k * width, width), width)],
                      part_s, part_r.at[k, samp], to, q)

    def hold_copy(r, q):
        return remote(hold.at[q, r], land.at[samp, :, (1 + r) * width:(2 + r) * width], hold_s,
                      part_r.at[1 + r, samp], band, q)

    def hold_wait(q):
        return remote(hold.at[q], hold.at[q], hold_s, hold_r.at[q], twin, samp)

    def is_held(both, q):
        return (band == 7) & both & (q != samp)

    def carry_on(n):
        first, second = needs(n, 0), needs(n, 1)

        @pl.when((first | second) & lower(n) & inner)
        def _():
            @pl.when(first & second)
            def _():
                remote(carry_in.at[n], carry_in.at[n], part_s, carry_r.at[n], twin, samp).wait_recv()

            @pl.when(jnp.logical_not(first & second))
            def _():
                remote(carry_in.at[n, 0], carry_in.at[n, 0], part_s, carry_r.at[n], twin, samp).wait_recv()

            def one(r, _):
                @pl.when(needs(n, r))
                def _():
                    w, own, both, single, active, q = job(n)
                    place = pl.ds(pl.multiple_of(n * 2 * width + r * width + far * rows, rows), rows)
                    parts[place, :] = (keep[n, r] + carry_in[n, r].astype(jnp.float32)).astype(jnp.bfloat16)
                    part_copy(n, r, block_of(n, r), q, 2).start()

                return 0

            lax.fori_loop(0, 2, one, 0)

    jobs = pieces + len(ORDER[0])

    def run(n, _):
        event = lookup(RELAYS, n)

        @pl.when(event != NONE)
        def _():
            w = jnp.minimum(event, 5)
            arrival(w).wait_recv()
            relay_copy(w).start()

        @pl.when((n == pieces) & (core == 0))
        def _():
            twin_wait().wait_recv()

        for when, q in HOLD.items():
            @pl.when((band == 5) & (n == when) & (samp != q))
            def _():
                hold_wait(q).wait_recv()
                for r in range(2):
                    hold_copy(r, q).start()

        for source, events in LATE.items():
            for when, (waits, starts) in events.items():
                @pl.when((band == source) & (n == when))
                def _():
                    for i in waits:
                        panel_copy(source, i).wait_send()
                    for i in starts:
                        panel_copy(source, i).start()

        w, own, both, single, active, q = job(n)

        @pl.when(active)
        def _():
            @pl.when(jnp.logical_not(own))
            def _():
                @pl.when(jnp.logical_not(relayed(w)))
                def _():
                    arrival(w).wait_recv()

                slot = jnp.where(both, 0, 1)

                @pl.when((w == 0) | (w == 4))
                def _():
                    remote(coef, coef_in.at[slot], coef_s.at[0], coef_r.at[slot], twin, samp).wait_recv()

                columns = pl.ds(pl.multiple_of(q * piece, piece), piece)
                mean, scale = coef_in[slot, 0:1, columns], coef_in[slot, 1:2, columns]

                def rescale(i, _):
                    span = pl.ds(pl.multiple_of(i * chunk, chunk), chunk)
                    rhs[pieces, span, :] = standard(window[w, span, :], mean, scale)
                    return 0

                lax.fori_loop(0, depth // chunk, rescale, 0)

            index = jnp.where(own, q, pieces)

            def multiply(i, _):
                r = lax.rem(core + i, 2)

                @pl.when(needs(n, r))
                def _():
                    @pl.when((i == 1) & (n == jnp.where(core == 1, 0, NONE)))
                    def _():
                        twin_wait().wait_recv()

                    place = pl.ds(pl.multiple_of(r * width, width), width)
                    total[...] = jnp.dot(lhs[place, :], rhs[index], preferred_element_type=jnp.float32)

                    @pl.when(lower(n))
                    def _():
                        k = block_of(n, r)
                        parts[pl.ds(pl.multiple_of(n * 2 * width + r * width, width), width), :] = total[...].astype(jnp.bfloat16)

                        @pl.when(outer)
                        def _():
                            carry_copy(n, r).start()

                        part_copy(n, r, k, q, 1).start()
                        part_copy(n, r, k, q, 0).start()

                        @pl.when(core != r)
                        def _():
                            part_copy(n, r, k, q, 3).start()

                        @pl.when(inner)
                        def _():
                            keep[n, r] = total[pl.ds(pl.multiple_of(far * rows, rows), rows), :]

                        @pl.when(core == r)
                        def _():
                            columns = pl.ds(pl.multiple_of(k * width + q * piece, piece), piece)
                            out_ref[:, columns] = total[pl.ds(pl.multiple_of(samp * rows, rows), rows), :]

                    @pl.when(jnp.logical_not(lower(n)))
                    def _():
                        m = jnp.maximum(n, pieces)
                        turned[m - pieces, :, place] = total[...].T.astype(jnp.bfloat16)

                        @pl.when(is_held(both, q))
                        def _():
                            turned_copy(m, r, single, q, True).start()

                        @pl.when(jnp.logical_not(is_held(both, q)))
                        def _():
                            turned_copy(m, r, single, q, False).start()

                return 0

            lax.fori_loop(0, 2, multiply, 0)

        @pl.when(n >= LAG)
        def _():
            carry_on(jnp.maximum(n - LAG, 0))

        return 0

    lax.fori_loop(0, jobs, run, 0)
    for n in range(jobs - LAG, jobs):
        carry_on(n)

    def landed(k, slot):
        place = slice(k * width, (k + 1) * width)
        remote(land.at[slot, :, place], land.at[slot, :, place], part_s, part_r.at[k, slot], twin, samp).wait_recv()

    def finish(k):
        kind = pick([row[k] for row in SOURCES])
        place = slice(k * width, (k + 1) * width)

        @pl.when((kind != 2) & (kind != 3))
        def _():
            landed(k, 0)
            landed(k, 1)

            @pl.when(inner)
            def _():
                landed(k, 2)

            def close(spot, slots):
                result = out_ref[:, spot] if 3 not in slots else land[3, :, spot].astype(jnp.float32)
                for slot in slots[:2]:
                    result = result + land[slot, :, spot].astype(jnp.float32)
                out_ref[:, spot] = result / samples

            @pl.when(kind == 0)
            def _():
                close(place, (0, 1))

            @pl.when(kind == 1)
            def _():
                landed(k, 3)
                close(place, (0, 1, 3))

            @pl.when(kind == 4)
            def _():
                mid = k * width + width // 2
                spot = slice(k * width, mid)
                remote(land.at[3, :, spot], land.at[3, :, spot], part_s, part_r.at[k, 3], twin, samp).wait_recv()
                close(spot, (0, 1, 3))
                close(slice(mid, (k + 1) * width), (0, 1))

            @pl.when(inner)
            def _():
                out_ref[:, place] += land[2, :, place].astype(jnp.float32) / samples

        @pl.when(kind == 3)
        def _():
            out_ref[:, place] = jnp.zeros((rows, width), jnp.float32)

    def gather(k):
        place = slice(k * width, (k + 1) * width)
        for z in range(shards):
            landed(k, z)
        result = land[0, :, place].astype(jnp.float32)
        for z in range(1, shards):
            result = result + land[z, :, place].astype(jnp.float32)
        out_ref[:, place] = result / samples

    for k in range(4):
        finish(k)
    for b, k in ((3, 3), (4, 2), (4, 3), (5, 1), (5, 2)):
        @pl.when(band == b)
        def _():
            gather(k)

    for source in SENDS:
        @pl.when(band == source)
        def _():
            for i in range(len(SENDS[source])):
                if i not in waited.get(source, []):
                    panel_copy(source, i).wait_send()
            for i in range(len(COEFS[source])):
                coef_copy(source, i).wait_send()
    for w in range(6):
        @pl.when(relayed(w))
        def _():
            relay_copy(jnp.int32(w)).wait_send()
    twin_wait().wait_send()

    @pl.when(band == 5)
    def _():
        remote(hold.at[0:shards - 1], hold.at[0:shards - 1], hold_s, hold_r.at[0], twin, samp).wait_send()

    for b in range(bands):
        odd = b % 2
        sent = pieces * (3 + 4 * odd)
        if b >= 6:
            sent += sum(pieces * (2 if w < 4 else 1) for w in ORDER[b])
        else:
            sent += sum(7 if w < 4 else 4 - odd for w in ORDER[b] if w != NONE)

        @pl.when(band == b)
        def _():
            span = pl.ds(0, sent * rows)
            remote(parts.at[span, :], parts.at[span, :], part_s, part_r.at[0, 0], twin, samp).wait_send()


def ladder(bands, shards, dosage):
    depth, width = dosage.shape
    pieces = shards
    piece = width // pieces
    rows = width // shards
    jobs = pieces + len(ORDER[0])
    f32, b16 = jnp.float32, jnp.bfloat16
    dma = pltpu.SemaphoreType.DMA
    return pl.pallas_call(
        functools.partial(ladder_kernel, bands, shards, depth * shards),
        out_shape=jax.ShapeDtypeStruct((rows, WIN), f32),
        in_specs=[pl.BlockSpec(memory_space=pltpu.HBM)],
        out_specs=pl.BlockSpec(memory_space=pltpu.VMEM),
        scratch_shapes=[
            pltpu.VMEM((pieces, depth, piece), b16),
            pltpu.VMEM((pieces + 1, depth, piece), b16),
            pltpu.VMEM((2 * width, depth), b16),
            pltpu.VMEM((6, depth, piece), b16),
            pltpu.VMEM((jobs * 2 * width, piece), b16),
            pltpu.VMEM((jobs - pieces, rows, 2 * width), b16),
            pltpu.VMEM((width, piece), f32),
            pltpu.VMEM((4, rows, WIN), b16),
            pltpu.VMEM((jobs, 2, rows, piece), b16),
            pltpu.VMEM((8, width), f32),
            pltpu.VMEM((shards - 1, 8, width), f32),
            pltpu.VMEM((8, width), f32),
            pltpu.VMEM((2, 8, width), f32),
            dma((pieces,)),
            dma((6,)), dma((6,)), dma((6,)),
            dma(()), dma(()),
            dma((4,)), dma((2,)),
            dma(()), dma(()),
            dma(()), dma((4, 4)), dma((jobs,)),
            pltpu.VMEM((pieces, 2, rows, width), b16),
            dma(()), dma((pieces,)),
            pltpu.VMEM((jobs, 2, rows, piece), f32),
        ],
        compiler_params=pltpu.CompilerParams(
            collective_id=0, has_side_effects=True, vmem_limit_bytes=48 * 1024 * 1024
        ),
    )(dosage)


def on_device(bands, shards, dosage):
    if bands == len(ORDER) and shards == 4 and dosage.shape[1] == TILE:
        return ladder(bands, shards, dosage)
    return general(bands, shards, dosage)


def solution(mesh):
    return jax.shard_map(
        functools.partial(on_device, mesh.shape["band"], mesh.shape["samp"]),
        mesh=mesh,
        in_specs=(P("samp", "band"),),
        out_specs=P(("band", "samp"), None),
        check_vma=False,
    )
```

```python
import functools

import jax
import jax.numpy as jnp
from jax import lax
from jax.experimental import pallas as pl
from jax.experimental.pallas import tpu as pltpu
from jax.sharding import PartitionSpec as P

TILE = 512
WIN = 2048
PIECES = 4
MESH = pl.DeviceIdType.MESH


def remote(src, dst, send, recv, band, samp):
    return pltpu.make_async_remote_copy(
        src_ref=src, dst_ref=dst, send_sem=send, recv_sem=recv,
        device_id=(band, samp), device_id_type=MESH,
    )


def kernel(bands, shards, reach, samples, dosage_ref, out_ref, own_t, window, stats, stats_in, coef,
           coef_in, parts, far_parts, near_in, far_in, panel_s, panel_r, stat_s, stat_r, coef_s, coef_r,
           part_s, part_r, relay_s, work, raw_ref, load_s):
    band = lax.axis_index("band")
    samp = lax.axis_index("samp")
    depth, width = raw_ref.shape
    load = pltpu.make_async_copy(dosage_ref, raw_ref, load_s)
    load.start()
    rows = width // shards
    piece = width // PIECES
    half = shards // 2
    side, seat = samp // half, lax.rem(samp, half)
    near = [side * half + lax.rem(seat + d, half) for d in range(1, half)]
    far = [(1 - side) * half + lax.rem(seat + d, half) for d in range(half)]
    peers = far + near

    barrier = pltpu.get_barrier_semaphore()
    for peer in peers:
        pl.semaphore_signal(barrier, inc=1, device_id=(band, peer), device_id_type=MESH)
    expected = shards - 1
    for k in range(1, reach + 1):
        @pl.when(band >= k)
        def _():
            pl.semaphore_signal(barrier, inc=1, device_id=(band - k, samp), device_id_type=MESH)

        @pl.when(band + k < bands)
        def _():
            pl.semaphore_signal(barrier, inc=1, device_id=(band + k, samp), device_id_type=MESH)
    expected = expected + jnp.minimum(band, reach) + jnp.minimum(bands - 1 - band, reach)
    pl.semaphore_wait(barrier, expected)
    load.wait()

    def panel_copy(k, j):
        columns = pl.ds(pl.multiple_of(j * piece, piece), piece)
        return remote(raw_ref.at[:, columns], window.at[k - 1, :, columns],
                      panel_s.at[k - 1, j], panel_r.at[k - 1, j], jnp.maximum(band - k, 0), samp)

    even = lax.rem(band, 2) == 0
    turn = lax.rem(band, 4)

    def sends(k):
        if k == 1:
            return jnp.logical_not(even)
        if k == 2:
            return (band >= 2) & (turn != 0)
        return even & (band >= 3)

    def relay_copy(k, j):
        columns = pl.ds(pl.multiple_of(j * piece, piece), piece)
        onward = (k == 2) & jnp.logical_not(even)
        target = jnp.clip(jnp.where(onward, band - 1, band + 1), 0, bands - 1)
        slot = jnp.where(k == 3, 1, jnp.where(even, 0, 2))
        return remote(window.at[k - 1, :, columns], window.at[slot, :, columns],
                      relay_s.at[k - 2, j], panel_r.at[slot, j], target, samp)

    def coef_copy(k):
        return remote(coef, coef_in.at[k - 1], coef_s.at[k - 1], coef_r.at[k - 1],
                      jnp.maximum(band - k, 0), samp)

    def part_copy(k, j, d):
        columns = pl.ds(pl.multiple_of(k * width + j * piece, piece), piece)
        source, landing, slot = (far_parts, far_in, d) if d < half else (parts, near_in, d - half)
        return remote(source.at[pl.ds(pl.multiple_of(peers[d] * rows, rows), rows), columns],
                      landing.at[slot, :, columns],
                      part_s.at[k, j, d], part_r.at[k, j, d], band, peers[d])

    def start_panel(k, j):
        @pl.when(sends(k))
        def _():
            panel_copy(k, j).start()

    early = [(k, 0) for k in range(1, reach + 1)]
    later = [(k, j) for j in range(PIECES) for k in range(1, reach + 1) if (k, j) not in early]
    for k, j in early:
        start_panel(k, j)

    step = 64

    def add(i, carry):
        x = raw_ref[pl.ds(pl.multiple_of(i * step, step), step), :].astype(jnp.float32)
        seen = jnp.where(x >= 0.0, 1.0, 0.0)
        value = jnp.where(x >= 0.0, x, 0.0)
        fold = lambda a: jnp.sum(a.reshape(step // 8, 8, width), axis=0)
        return carry[0] + fold(seen), carry[1] + fold(value), carry[2] + fold(value * value)

    zero = jnp.zeros((8, width), jnp.float32)
    sums = lax.fori_loop(0, depth // step, add, (zero, zero, zero))
    stats[...] = jnp.concatenate(
        [jnp.sum(a, axis=0, keepdims=True) for a in sums] + [jnp.zeros((5, width), jnp.float32)], axis=0
    )
    stat_copies = [
        remote(stats, stats_in.at[d], stat_s.at[d], stat_r.at[d], band, peers[d])
        for d in range(shards - 1)
    ]
    for copy in stat_copies:
        copy.start()
    for copy in stat_copies:
        copy.wait()
    sums = stats[...]
    for d in range(shards - 1):
        sums = sums + stats_in[d]
    count, total, square = sums[0:1], sums[1:2], sums[2:3]
    mean = (total + 1.0) / (count + 1.0)
    spread = (square - 2.0 * mean * total + count * mean * mean + 0.5) / (count + 1.0)
    coef[...] = jnp.concatenate(
        [mean, lax.rsqrt(spread), jnp.zeros((6, width), jnp.float32)], axis=0
    )
    for k in range(1, reach + 1):
        @pl.when(band >= k)
        def _():
            coef_copy(k).start()
    for k, j in later:
        start_panel(k, j)

    chunk = 256

    def standard(x, mean, scale):
        x = x.astype(jnp.float32)
        return jnp.where(x >= 0.0, (x - mean) * scale, 0.0).astype(jnp.bfloat16)

    own = window.at[reach]

    def scale_own(i, _):
        span = pl.ds(pl.multiple_of(i * chunk, chunk), chunk)
        scaled = standard(raw_ref[span, :], coef[0:1, :], coef[1:2, :])
        own[span, :] = scaled
        own_t[:, span] = scaled.T
        return 0

    lax.fori_loop(0, depth // chunk, scale_own, 0)

    def correlate(k, j, panel):
        place = pl.ds(pl.multiple_of(k * width + j * piece, piece), piece)

        def block(i, _):
            span = pl.ds(pl.multiple_of(i * 256, 256), 256)
            total = jnp.dot(own_t[span, :], panel[...], preferred_element_type=jnp.float32)
            parts[span, place] = total
            far_parts[span, place] = total.astype(jnp.bfloat16)
            return 0

        lax.fori_loop(0, width // 256, block, 0)
        for d in range(shards - 1):
            part_copy(k, j, d).start()
        out_ref[:, place] = parts[pl.ds(pl.multiple_of(samp * rows, rows), rows), place]

    def finish(k, j):
        place = slice(k * width + j * piece, k * width + (j + 1) * piece)
        total = out_ref[:, place]
        for d in range(shards - 1):
            part_copy(k, j, d).wait()
            landed = far_in[d, :, place] if d < half else near_in[d - half, :, place]
            total = total + landed.astype(jnp.float32)
        out_ref[:, place] = total / samples

    for j in range(PIECES):
        correlate(0, j, own.at[:, pl.ds(j * piece, piece)])
    ahead = [(1, 0)]
    for j in range(PIECES):
        ahead += [(1, j + 1)] if j + 1 < PIECES else []
        ahead += [(k, j) for k in range(2, reach + 1)]
    level = [(k, j) for j in range(PIECES) for k in range(reach, 0, -1)]
    for (k_even, j_even), (k_odd, j_odd) in zip(ahead, level):
        k_last = k_odd if k_odd == 1 else reach + 2 - k_odd
        k = jnp.where(even, k_even, jnp.where(turn == 3, k_last, k_odd))
        j = jnp.where(even, j_even, j_odd)
        columns = pl.ds(pl.multiple_of(j * piece, piece), piece)

        @pl.when(band + k < bands)
        def _():
            panel_copy(k, j).wait_recv()

            @pl.when((k == 2) | ((k == 3) & (turn == 1)))
            def _():
                relay_copy(k, j).start()

            @pl.when(j == 0)
            def _():
                coef_copy(k).wait_recv()

            mean, scale = coef_in[k - 1, 0:1, columns], coef_in[k - 1, 1:2, columns]

            def rescale(i, _):
                span = pl.ds(pl.multiple_of(i * chunk, chunk), chunk)
                work[span, :] = standard(window[k - 1, span, columns], mean, scale)
                return 0

            lax.fori_loop(0, depth // chunk, rescale, 0)
            correlate(k, j, work)

    for j in range(PIECES):
        finish(0, j)
    for j in range(PIECES):
        for k in range(1, reach + 1):
            @pl.when(band + k < bands)
            def _():
                finish(k, j)

            @pl.when(band + k >= bands)
            def _():
                place = slice(k * width + j * piece, k * width + (j + 1) * piece)
                out_ref[:, place] = jnp.zeros((rows, piece), jnp.float32)
    for k in range(1, reach + 1):
        @pl.when(band >= k)
        def _():
            coef_copy(k).wait_send()

        for j in range(PIECES):
            @pl.when(sends(k))
            def _():
                panel_copy(k, j).wait_send()

            if k > 1:
                @pl.when((band + k < bands) & ((k == 2) | (turn == 1)))
                def _():
                    relay_copy(k, j).wait_send()


def general(bands, shards, dosage):
    depth, width = dosage.shape
    reach = (WIN - TILE + width - 1) // width
    rows = width // shards
    f32 = jnp.float32
    dma = pltpu.SemaphoreType.DMA
    return pl.pallas_call(
        functools.partial(kernel, bands, shards, reach, depth * shards),
        out_shape=jax.ShapeDtypeStruct((rows, WIN), f32),
        in_specs=[pl.BlockSpec(memory_space=pltpu.HBM)],
        out_specs=pl.BlockSpec(memory_space=pltpu.VMEM),
        scratch_shapes=[
            pltpu.VMEM((width, depth), jnp.bfloat16),
            pltpu.VMEM((reach + 1, depth, width), jnp.bfloat16),
            pltpu.VMEM((8, width), f32),
            pltpu.VMEM((shards - 1, 8, width), f32),
            pltpu.VMEM((8, width), f32),
            pltpu.VMEM((reach, 8, width), f32),
            pltpu.VMEM((width, WIN), f32),
            pltpu.VMEM((width, WIN), jnp.bfloat16),
            pltpu.VMEM((max(shards // 2 - 1, 1), rows, WIN), f32),
            pltpu.VMEM((shards // 2, rows, WIN), jnp.bfloat16),
            dma((reach, PIECES)), dma((reach, PIECES)),
            dma((shards - 1,)), dma((shards - 1,)),
            dma((reach,)), dma((reach,)),
            dma((reach + 1, PIECES, shards - 1)), dma((reach + 1, PIECES, shards - 1)),
            dma((reach - 1, PIECES)),
            pltpu.VMEM((depth, width // PIECES), jnp.bfloat16),
            pltpu.VMEM((depth, width), jnp.bfloat16),
            dma(()),
        ],
        compiler_params=pltpu.CompilerParams(
            collective_id=0, has_side_effects=True, vmem_limit_bytes=48 * 1024 * 1024
        ),
    )(dosage)


ORDER = (
    (4, 5, 0, 1, 2, 3, 15, 15),
    (0, 4, 1, 5, 2, 3, 15, 15),
    (0, 1, 2, 3, 15, 15, 15, 15),
    (0, 1, 2, 3, 15, 15, 15, 15),
    (15, 15, 15, 15, 15, 15, 15, 15),
    (15, 15, 15, 15, 15, 15, 15, 15),
    (0, 2, 1, 3, 15, 15, 15, 15),
    (4, 0, 5, 1, 2, 3, 6, 7),
)
RELAYS = (
    {0: 4, 3: 5},
    {5: 4, 7: 5},
    {4: 0, 5: 1},
    {},
    {},
    {7: 4, 8: 5},
    {},
    {0: 4, 1: 0, 4: 5, 5: 1, 7: 2, 9: 3},
)
SENDS = {
    2: [(0, 0, 0), (1, 0, 1), (2, 0, 2), (3, 0, 3)],
    3: [(2, 7, 4), (3, 7, 5), (0, 1, 0), (1, 1, 1), (0, 7, 6), (1, 7, 7)],
    4: [(0, 0, 4), (1, 0, 5), (2, 1, 4), (3, 1, 5), (2, 6, 2), (3, 6, 3)],
    5: [(0, 7, 0), (1, 7, 1), (2, 7, 2), (3, 7, 3)],
}
EARLY = {2: (0,), 3: (0, 2), 4: (0,), 5: (0,)}
LATE = {3: {6: ((0,), (4, 5))}, 4: {0: ((0,), (2, 3)), 2: ((2,), (4, 5))}}
COEFS = {2: [(0, 0)], 3: [(1, 0), (7, 1)], 4: [(0, 1), (1, 1), (2, 0), (6, 0)], 5: [(7, 0), (3, 0)]}
SOURCES = ((0, 1, 0, 1), (0, 1, 0, 4), (0, 1, 0, 1), (0, 1, 0, 2), (0, 1, 2, 2), (0, 2, 2, 3), (0, 1, 3, 3), (0, 3, 3, 3))
CROSS = {3: (7,), 4: (6,), 6: (4,), 7: (3,)}
HOLD = {6: 0, 7: 1, 8: 2, 9: 3}
LAG = 3
NONE = 15


def peers(bands):
    plane = {b: {b + 1 - 2 * (b % 2)} for b in range(bands)}
    pairs = [(b, target) for b in SENDS for _, target, _ in SENDS[b]] + [(b, target) for b in COEFS for target, _ in COEFS[b]]
    pairs += [(0, 2), (1, 2), (2, 6), (5, 1), (7, 3), (7, 5)] + [(b, target) for b in CROSS for target in CROSS[b]]
    for a, b in pairs:
        plane[a].add(b)
        plane[b].add(a)
    line = {b: {b, b + 1 - 2 * (b % 2), *CROSS.get(b, ())} for b in range(bands)}
    return plane, line


def ladder_kernel(bands, shards, samples, dosage_ref, out_ref, raw, rhs, lhs, window, parts, turned, total,
                  land, carry_in, stats, stats_in, coef, coef_in, load_s, panel_s, panel_r, relay_s, stat_s,
                  stat_r, coef_s, coef_r, twin_s, twin_r, part_s, part_r, carry_r, hold, hold_s, hold_r, keep):
    band = lax.axis_index("band")
    samp = lax.axis_index("samp")
    pieces, depth, piece = raw.shape
    width = pieces * piece
    rows = width // shards
    core = lax.rem(band, 2)
    even = band - core
    twin = band + 1 - 2 * core
    upper = band >= 6
    outer = (samp == 0) | (samp == 3)
    inner = jnp.logical_not(outer)
    near = samp + 1 - 2 * lax.rem(samp, 2)
    middle = jnp.where(samp < 2, 2, 1)
    far = jnp.where(samp < 2, 3, 0)

    def pick(values):
        result = jnp.int32(values[0])
        for i, value in enumerate(values[1:], 1):
            result = jnp.where(band == i, jnp.int32(value), result)
        return result

    def among(*which):
        result = band == which[0]
        for i in which[1:]:
            result = result | (band == i)
        return result

    def lookup(table, n):
        result = jnp.int32(NONE)
        for b in range(bands):
            for i, value in (table[b].items() if isinstance(table[b], dict) else enumerate(table[b])):
                if value != NONE:
                    result = jnp.where((band == b) & (n == i), jnp.int32(value), result)
        return result

    loads = [
        pltpu.make_async_copy(dosage_ref.at[:, pl.ds(j * piece, piece)], raw.at[j], load_s.at[j])
        for j in range(pieces)
    ]
    for load in loads:
        load.start()
    barrier = pltpu.get_barrier_semaphore()
    plane, line = peers(bands)
    for b in range(bands):
        @pl.when(band == b)
        def _():
            for peer in sorted(plane[b]):
                pl.semaphore_signal(barrier, inc=1, device_id=(peer, samp), device_id_type=MESH)
            for peer in sorted(line[b]):
                for d in range(1, shards):
                    pl.semaphore_signal(barrier, inc=1, device_id=(peer, lax.rem(samp + d, shards)),
                                        device_id_type=MESH)

    step = 256

    def measure(j, _):
        def add(i, carry):
            x = raw[j, pl.ds(pl.multiple_of(i * step, step), step), :].astype(jnp.float32)
            seen = jnp.where(x >= 0.0, 1.0, 0.0)
            value = jnp.maximum(x, 0.0)
            fold = lambda a: jnp.sum(a.reshape(step // 8, 8, piece), axis=0)
            return carry[0] + fold(seen), carry[1] + fold(value), carry[2] + fold(value * value)

        zero = jnp.zeros((8, piece), jnp.float32)
        sums = lax.fori_loop(0, depth // step, add, (zero, zero, zero))
        for i, a in enumerate(sums):
            stats[pl.ds(pieces * i + j, 1), :] = jnp.sum(a, axis=0, keepdims=True)
        return 0

    for load in loads:
        load.wait()
    stats[3 * pieces:, :] = jnp.zeros((pieces, piece), jnp.float32)
    lax.fori_loop(0, pieces, measure, 0)
    pl.semaphore_wait(barrier, pick([len(plane[b]) + (shards - 1) * len(line[b]) for b in range(bands)]))

    def panel_copy(source, i):
        j, target, slot = SENDS[source][i]
        return remote(raw.at[j], window.at[slot], panel_s.at[i], panel_r.at[slot], target, samp)

    late = {source: [i for _, (_, starts) in events.items() for i in starts] for source, events in LATE.items()}
    waited = {source: [i for _, (waits, _) in events.items() for i in waits] for source, events in LATE.items()}
    for source in SENDS:
        @pl.when(band == source)
        def _():
            for i in EARLY[source]:
                panel_copy(source, i).start()

    stat_copies = [
        remote(stats, stats_in.at[d - 1], stat_s, stat_r, band, lax.rem(samp + d, shards))
        for d in range(1, shards)
    ]
    for copy in stat_copies:
        copy.start()
    remote(stats_in, stats_in, stat_s, stat_r, twin, samp).wait()
    sums = stats[...]
    for d in range(shards - 1):
        sums = sums + stats_in[d]
    count, sum1, square = (sums[pieces * i:pieces * (i + 1)] for i in range(3))
    mean = (sum1 + 1.0) / (count + 1.0)
    spread = (square - 2.0 * mean * sum1 + count * mean * mean + 0.5) / (count + 1.0)
    coef[0:pieces, :] = mean
    coef[pieces:2 * pieces, :] = lax.rsqrt(spread)

    def coef_copy(source, i):
        target, slot = COEFS[source][i]
        return remote(coef, coef_in.at[slot], coef_s.at[i], coef_r.at[slot], target, samp)

    for source in COEFS:
        @pl.when(band == source)
        def _():
            for i in range(len(COEFS[source])):
                coef_copy(source, i).start()
            for i in range(len(SENDS[source])):
                if i not in late.get(source, []) and i not in EARLY[source]:
                    panel_copy(source, i).start()

    chunk = 256

    def standard(x, mean, scale):
        x = x.astype(jnp.float32)
        return jnp.where(x >= 0.0, (x - mean) * scale, 0.0).astype(jnp.bfloat16)

    def twin_copy(j):
        place = pl.ds(pl.multiple_of(core * width + j * piece, piece), piece)
        return remote(lhs.at[place, :], lhs.at[place, :], twin_s, twin_r, twin, samp)

    def twin_wait():
        place = pl.ds(pl.multiple_of((1 - core) * width, width), width)
        return remote(lhs.at[place, :], lhs.at[place, :], twin_s, twin_r, twin, samp)

    def scale_own(j, _):
        place = pl.ds(pl.multiple_of(core * width + j * piece, piece), piece)
        mean, scale = coef[pl.ds(j, 1), :], coef[pl.ds(pieces + j, 1), :]

        def part(i, _):
            span = pl.ds(pl.multiple_of(i * chunk, chunk), chunk)
            scaled = standard(raw[j, span, :], mean, scale)
            rhs[j, span, :] = scaled
            lhs[place, span] = scaled.T
            return 0

        lax.fori_loop(0, depth // chunk, part, 0)
        twin_copy(j).start()
        return 0

    lax.fori_loop(0, pieces, scale_own, 0)

    def relay_copy(w):
        target = jnp.where(w < 4, pick((2, 2, 6, 0, 0, 1, 0, 3)), pick((2, 2, 6, 0, 0, 1, 0, 5)))
        slot = jnp.clip(w + pick((-4, -2, 0, 0, 0, -2, 0, 0)), 0, 5)
        return remote(window.at[w], window.at[slot], relay_s.at[w], panel_r.at[slot], target, samp)

    def arrival(w):
        return remote(window.at[w], window.at[w], relay_s.at[w], panel_r.at[w], twin, samp)

    def relayed(w):
        return (among(0, 1, 5) & (w >= 4)) | ((band == 2) & (w < 2)) | ((band == 7) & (w < 6))

    def job(n):
        w = lookup(ORDER, n - pieces)
        own = n < pieces
        active = own | (w != NONE)
        w = jnp.minimum(w, 7)
        both = jnp.logical_not(own) & (w < 4)
        single = jnp.logical_not(own) & (w >= 4)
        q = jnp.where(own, n, jnp.where(both, w, lax.rem(jnp.maximum(2 * core + w - 4, 0), pieces)))
        return w, own, both, single, active, q

    def needs(n, r):
        w, own, both, single, active, q = job(n)
        return active & (both | (own & ((r == 0) | (core == 1))) | (single & (r == jnp.where(upper, 0, 1))))

    def block_of(n, r):
        w, own, both, single, active, q = job(n)
        return jnp.clip(jnp.where(single, 3, jnp.where(own, 0, 2) + core - r), 0, 3)

    def lower(n):
        return (n < pieces) | jnp.logical_not(upper)

    def part_copy(n, r, k, q, i):
        columns = pl.ds(pl.multiple_of(k * width + q * piece, piece), piece)
        target = (near, middle, far, samp)[i]
        slot = (0, jnp.where(outer, 2, 1), 1, 3)[i]
        source = parts.at[pl.ds(pl.multiple_of(n * 2 * width + r * width + target * rows, rows), rows), :]
        return remote(source, land.at[slot, :, columns], part_s, part_r.at[k, slot],
                      even + r, target)

    def carry_copy(n, r):
        source = parts.at[pl.ds(pl.multiple_of(n * 2 * width + r * width + far * rows, rows), rows), :]
        return remote(source, carry_in.at[n, r], part_s, carry_r.at[n], band, near)

    def turned_copy(n, r, single, q, held):
        k = jnp.clip(jnp.where(single, 3, 2 - core + r), 0, 3)
        source = turned.at[n - pieces, :, pl.ds(pl.multiple_of(r * width, width), width)]
        to = jnp.where(single, 3, jnp.maximum(band - 2, 0))
        if held:
            return remote(source, hold.at[q, r], part_s, hold_r.at[q], to, samp)
        return remote(source, land.at[samp, :, pl.ds(pl.multiple_of(k * width, width), width)],
                      part_s, part_r.at[k, samp], to, q)

    def hold_copy(r, q):
        return remote(hold.at[q, r], land.at[samp, :, (1 + r) * width:(2 + r) * width], hold_s,
                      part_r.at[1 + r, samp], band, q)

    def hold_wait(q):
        return remote(hold.at[q], hold.at[q], hold_s, hold_r.at[q], twin, samp)

    def is_held(both, q):
        return (band == 7) & both & (q != samp)

    def carry_on(n):
        first, second = needs(n, 0), needs(n, 1)

        @pl.when((first | second) & lower(n) & inner)
        def _():
            @pl.when(first & second)
            def _():
                remote(carry_in.at[n], carry_in.at[n], part_s, carry_r.at[n], twin, samp).wait_recv()

            @pl.when(jnp.logical_not(first & second))
            def _():
                remote(carry_in.at[n, 0], carry_in.at[n, 0], part_s, carry_r.at[n], twin, samp).wait_recv()

            def one(r, _):
                @pl.when(needs(n, r))
                def _():
                    w, own, both, single, active, q = job(n)
                    place = pl.ds(pl.multiple_of(n * 2 * width + r * width + far * rows, rows), rows)
                    parts[place, :] = (keep[n, r] + carry_in[n, r].astype(jnp.float32)).astype(jnp.bfloat16)
                    part_copy(n, r, block_of(n, r), q, 2).start()

                return 0

            lax.fori_loop(0, 2, one, 0)

    jobs = pieces + len(ORDER[0])

    def run(n, _):
        event = lookup(RELAYS, n)

        @pl.when(event != NONE)
        def _():
            w = jnp.minimum(event, 5)
            arrival(w).wait_recv()
            relay_copy(w).start()

        @pl.when((n == pieces) & (core == 0))
        def _():
            twin_wait().wait_recv()

        for when, q in HOLD.items():
            @pl.when((band == 5) & (n == when) & (samp != q))
            def _():
                hold_wait(q).wait_recv()
                for r in range(2):
                    hold_copy(r, q).start()

        for source, events in LATE.items():
            for when, (waits, starts) in events.items():
                @pl.when((band == source) & (n == when))
                def _():
                    for i in waits:
                        panel_copy(source, i).wait_send()
                    for i in starts:
                        panel_copy(source, i).start()

        w, own, both, single, active, q = job(n)

        @pl.when(active)
        def _():
            @pl.when(jnp.logical_not(own))
            def _():
                @pl.when(jnp.logical_not(relayed(w)))
                def _():
                    arrival(w).wait_recv()

                slot = jnp.where(both, 0, 1)

                @pl.when((w == 0) | (w == 4))
                def _():
                    remote(coef, coef_in.at[slot], coef_s.at[0], coef_r.at[slot], twin, samp).wait_recv()

                mean, scale = coef_in[slot, pl.ds(q, 1), :], coef_in[slot, pl.ds(pieces + q, 1), :]

                def rescale(i, _):
                    span = pl.ds(pl.multiple_of(i * chunk, chunk), chunk)
                    rhs[pieces, span, :] = standard(window[w, span, :], mean, scale)
                    return 0

                lax.fori_loop(0, depth // chunk, rescale, 0)

            index = jnp.where(own, q, pieces)

            def multiply(i, _):
                r = lax.rem(core + i, 2)

                @pl.when(needs(n, r))
                def _():
                    @pl.when((i == 1) & (n == jnp.where(core == 1, 0, NONE)))
                    def _():
                        twin_wait().wait_recv()

                    place = pl.ds(pl.multiple_of(r * width, width), width)
                    total[...] = jnp.dot(lhs[place, :], rhs[index], preferred_element_type=jnp.float32)

                    @pl.when(lower(n))
                    def _():
                        k = block_of(n, r)
                        parts[pl.ds(pl.multiple_of(n * 2 * width + r * width, width), width), :] = total[...].astype(jnp.bfloat16)

                        @pl.when(outer)
                        def _():
                            carry_copy(n, r).start()

                        part_copy(n, r, k, q, 1).start()
                        part_copy(n, r, k, q, 0).start()

                        @pl.when(core != r)
                        def _():
                            part_copy(n, r, k, q, 3).start()

                        @pl.when(inner)
                        def _():
                            keep[n, r] = total[pl.ds(pl.multiple_of(far * rows, rows), rows), :]

                        @pl.when(core == r)
                        def _():
                            columns = pl.ds(pl.multiple_of(k * width + q * piece, piece), piece)
                            out_ref[:, columns] = total[pl.ds(pl.multiple_of(samp * rows, rows), rows), :]

                    @pl.when(jnp.logical_not(lower(n)))
                    def _():
                        m = jnp.maximum(n, pieces)
                        turned[m - pieces, :, place] = total[...].T.astype(jnp.bfloat16)

                        @pl.when(is_held(both, q))
                        def _():
                            turned_copy(m, r, single, q, True).start()

                        @pl.when(jnp.logical_not(is_held(both, q)))
                        def _():
                            turned_copy(m, r, single, q, False).start()

                return 0

            lax.fori_loop(0, 2, multiply, 0)

        @pl.when(n >= LAG)
        def _():
            carry_on(jnp.maximum(n - LAG, 0))

        return 0

    lax.fori_loop(0, jobs, run, 0)
    for n in range(jobs - LAG, jobs):
        carry_on(n)

    def landed(k, slot):
        place = slice(k * width, (k + 1) * width)
        remote(land.at[slot, :, place], land.at[slot, :, place], part_s, part_r.at[k, slot], twin, samp).wait_recv()

    def finish(k):
        kind = pick([row[k] for row in SOURCES])
        place = slice(k * width, (k + 1) * width)

        @pl.when((kind != 2) & (kind != 3))
        def _():
            landed(k, 0)
            landed(k, 1)

            @pl.when(inner)
            def _():
                landed(k, 2)

            def close(spot, slots):
                result = out_ref[:, spot] if 3 not in slots else land[3, :, spot].astype(jnp.float32)
                for slot in slots[:2]:
                    result = result + land[slot, :, spot].astype(jnp.float32)
                out_ref[:, spot] = result / samples

            @pl.when(kind == 0)
            def _():
                close(place, (0, 1))

            @pl.when(kind == 1)
            def _():
                landed(k, 3)
                close(place, (0, 1, 3))

            @pl.when(kind == 4)
            def _():
                mid = k * width + width // 2
                spot = slice(k * width, mid)
                remote(land.at[3, :, spot], land.at[3, :, spot], part_s, part_r.at[k, 3], twin, samp).wait_recv()
                close(spot, (0, 1, 3))
                close(slice(mid, (k + 1) * width), (0, 1))

            @pl.when(inner)
            def _():
                out_ref[:, place] += land[2, :, place].astype(jnp.float32) / samples

        @pl.when(kind == 3)
        def _():
            out_ref[:, place] = jnp.zeros((rows, width), jnp.float32)

    def gather(k):
        place = slice(k * width, (k + 1) * width)
        for z in range(shards):
            landed(k, z)
        result = land[0, :, place].astype(jnp.float32)
        for z in range(1, shards):
            result = result + land[z, :, place].astype(jnp.float32)
        out_ref[:, place] = result / samples

    for k in range(4):
        finish(k)
    for b, k in ((3, 3), (4, 2), (4, 3), (5, 1), (5, 2)):
        @pl.when(band == b)
        def _():
            gather(k)

    for source in SENDS:
        @pl.when(band == source)
        def _():
            for i in range(len(SENDS[source])):
                if i not in waited.get(source, []):
                    panel_copy(source, i).wait_send()
            for i in range(len(COEFS[source])):
                coef_copy(source, i).wait_send()
    for w in range(6):
        @pl.when(relayed(w))
        def _():
            relay_copy(jnp.int32(w)).wait_send()
    twin_wait().wait_send()

    @pl.when(band == 5)
    def _():
        remote(hold.at[0:shards - 1], hold.at[0:shards - 1], hold_s, hold_r.at[0], twin, samp).wait_send()

    for b in range(bands):
        odd = b % 2
        sent = pieces * (3 + 4 * odd)
        if b >= 6:
            sent += sum(pieces * (2 if w < 4 else 1) for w in ORDER[b] if w != NONE)
        else:
            sent += sum(7 if w < 4 else 4 - odd for w in ORDER[b] if w != NONE)

        @pl.when(band == b)
        def _():
            span = pl.ds(0, sent * rows)
            remote(parts.at[span, :], parts.at[span, :], part_s, part_r.at[0, 0], twin, samp).wait_send()


def ladder(bands, shards, dosage):
    depth, width = dosage.shape
    pieces = shards
    piece = width // pieces
    rows = width // shards
    jobs = pieces + len(ORDER[0])
    f32, b16 = jnp.float32, jnp.bfloat16
    dma = pltpu.SemaphoreType.DMA
    return pl.pallas_call(
        functools.partial(ladder_kernel, bands, shards, depth * shards),
        out_shape=jax.ShapeDtypeStruct((rows, WIN), f32),
        in_specs=[pl.BlockSpec(memory_space=pltpu.HBM)],
        out_specs=pl.BlockSpec(memory_space=pltpu.VMEM),
        scratch_shapes=[
            pltpu.VMEM((pieces, depth, piece), b16),
            pltpu.VMEM((pieces + 1, depth, piece), b16),
            pltpu.VMEM((2 * width, depth), b16),
            pltpu.VMEM((8, depth, piece), b16),
            pltpu.VMEM((jobs * 2 * width, piece), b16),
            pltpu.VMEM((jobs - pieces, rows, 2 * width), b16),
            pltpu.VMEM((width, piece), f32),
            pltpu.VMEM((4, rows, WIN), b16),
            pltpu.VMEM((jobs, 2, rows, piece), b16),
            pltpu.VMEM((4 * pieces, piece), f32),
            pltpu.VMEM((shards - 1, 4 * pieces, piece), f32),
            pltpu.VMEM((2 * pieces, piece), f32),
            pltpu.VMEM((2, 2 * pieces, piece), f32),
            dma((pieces,)),
            dma((6,)), dma((8,)), dma((6,)),
            dma(()), dma(()),
            dma((4,)), dma((2,)),
            dma(()), dma(()),
            dma(()), dma((4, 4)), dma((jobs,)),
            pltpu.VMEM((pieces, 2, rows, width), b16),
            dma(()), dma((pieces,)),
            pltpu.VMEM((jobs, 2, rows, piece), f32),
        ],
        compiler_params=pltpu.CompilerParams(
            collective_id=0, has_side_effects=True, vmem_limit_bytes=52 * 1024 * 1024
        ),
    )(dosage)


def on_device(bands, shards, dosage):
    if bands == len(ORDER) and shards == 4 and dosage.shape[1] == TILE:
        return ladder(bands, shards, dosage)
    return general(bands, shards, dosage)


def solution(mesh):
    return jax.shard_map(
        functools.partial(on_device, mesh.shape["band"], mesh.shape["samp"]),
        mesh=mesh,
        in_specs=(P("samp", "band"),),
        out_specs=P(("band", "samp"), None),
        check_vma=False,
    )
```

```python
import functools

import jax
import jax.numpy as jnp
from jax import lax
from jax.experimental import pallas as pl
from jax.experimental.pallas import tpu as pltpu
from jax.sharding import PartitionSpec as P

TILE = 512
WIN = 2048
PIECES = 4
MESH = pl.DeviceIdType.MESH


def remote(src, dst, send, recv, band, samp):
    return pltpu.make_async_remote_copy(
        src_ref=src, dst_ref=dst, send_sem=send, recv_sem=recv,
        device_id=(band, samp), device_id_type=MESH,
    )


def kernel(bands, shards, reach, samples, dosage_ref, out_ref, own_t, window, stats, stats_in, coef,
           coef_in, parts, far_parts, near_in, far_in, panel_s, panel_r, stat_s, stat_r, coef_s, coef_r,
           part_s, part_r, relay_s, work, raw_ref, load_s):
    band = lax.axis_index("band")
    samp = lax.axis_index("samp")
    depth, width = raw_ref.shape
    load = pltpu.make_async_copy(dosage_ref, raw_ref, load_s)
    load.start()
    rows = width // shards
    piece = width // PIECES
    half = shards // 2
    side, seat = samp // half, lax.rem(samp, half)
    near = [side * half + lax.rem(seat + d, half) for d in range(1, half)]
    far = [(1 - side) * half + lax.rem(seat + d, half) for d in range(half)]
    peers = far + near

    barrier = pltpu.get_barrier_semaphore()
    for peer in peers:
        pl.semaphore_signal(barrier, inc=1, device_id=(band, peer), device_id_type=MESH)
    expected = shards - 1
    for k in range(1, reach + 1):
        @pl.when(band >= k)
        def _():
            pl.semaphore_signal(barrier, inc=1, device_id=(band - k, samp), device_id_type=MESH)

        @pl.when(band + k < bands)
        def _():
            pl.semaphore_signal(barrier, inc=1, device_id=(band + k, samp), device_id_type=MESH)
    expected = expected + jnp.minimum(band, reach) + jnp.minimum(bands - 1 - band, reach)
    pl.semaphore_wait(barrier, expected)
    load.wait()

    def panel_copy(k, j):
        columns = pl.ds(pl.multiple_of(j * piece, piece), piece)
        return remote(raw_ref.at[:, columns], window.at[k - 1, :, columns],
                      panel_s.at[k - 1, j], panel_r.at[k - 1, j], jnp.maximum(band - k, 0), samp)

    even = lax.rem(band, 2) == 0
    turn = lax.rem(band, 4)

    def sends(k):
        if k == 1:
            return jnp.logical_not(even)
        if k == 2:
            return (band >= 2) & (turn != 0)
        return even & (band >= 3)

    def relay_copy(k, j):
        columns = pl.ds(pl.multiple_of(j * piece, piece), piece)
        onward = (k == 2) & jnp.logical_not(even)
        target = jnp.clip(jnp.where(onward, band - 1, band + 1), 0, bands - 1)
        slot = jnp.where(k == 3, 1, jnp.where(even, 0, 2))
        return remote(window.at[k - 1, :, columns], window.at[slot, :, columns],
                      relay_s.at[k - 2, j], panel_r.at[slot, j], target, samp)

    def coef_copy(k):
        return remote(coef, coef_in.at[k - 1], coef_s.at[k - 1], coef_r.at[k - 1],
                      jnp.maximum(band - k, 0), samp)

    def part_copy(k, j, d):
        columns = pl.ds(pl.multiple_of(k * width + j * piece, piece), piece)
        source, landing, slot = (far_parts, far_in, d) if d < half else (parts, near_in, d - half)
        return remote(source.at[pl.ds(pl.multiple_of(peers[d] * rows, rows), rows), columns],
                      landing.at[slot, :, columns],
                      part_s.at[k, j, d], part_r.at[k, j, d], band, peers[d])

    def start_panel(k, j):
        @pl.when(sends(k))
        def _():
            panel_copy(k, j).start()

    early = [(k, 0) for k in range(1, reach + 1)]
    later = [(k, j) for j in range(PIECES) for k in range(1, reach + 1) if (k, j) not in early]
    for k, j in early:
        start_panel(k, j)

    step = 64

    def add(i, carry):
        x = raw_ref[pl.ds(pl.multiple_of(i * step, step), step), :].astype(jnp.float32)
        seen = jnp.where(x >= 0.0, 1.0, 0.0)
        value = jnp.where(x >= 0.0, x, 0.0)
        fold = lambda a: jnp.sum(a.reshape(step // 8, 8, width), axis=0)
        return carry[0] + fold(seen), carry[1] + fold(value), carry[2] + fold(value * value)

    zero = jnp.zeros((8, width), jnp.float32)
    sums = lax.fori_loop(0, depth // step, add, (zero, zero, zero))
    stats[...] = jnp.concatenate(
        [jnp.sum(a, axis=0, keepdims=True) for a in sums] + [jnp.zeros((5, width), jnp.float32)], axis=0
    )
    stat_copies = [
        remote(stats, stats_in.at[d], stat_s.at[d], stat_r.at[d], band, peers[d])
        for d in range(shards - 1)
    ]
    for copy in stat_copies:
        copy.start()
    for copy in stat_copies:
        copy.wait()
    sums = stats[...]
    for d in range(shards - 1):
        sums = sums + stats_in[d]
    count, total, square = sums[0:1], sums[1:2], sums[2:3]
    mean = (total + 1.0) / (count + 1.0)
    spread = (square - 2.0 * mean * total + count * mean * mean + 0.5) / (count + 1.0)
    coef[...] = jnp.concatenate(
        [mean, lax.rsqrt(spread), jnp.zeros((6, width), jnp.float32)], axis=0
    )
    for k in range(1, reach + 1):
        @pl.when(band >= k)
        def _():
            coef_copy(k).start()
    for k, j in later:
        start_panel(k, j)

    chunk = 256

    def standard(x, mean, scale):
        x = x.astype(jnp.float32)
        return jnp.where(x >= 0.0, (x - mean) * scale, 0.0).astype(jnp.bfloat16)

    own = window.at[reach]

    def scale_own(i, _):
        span = pl.ds(pl.multiple_of(i * chunk, chunk), chunk)
        scaled = standard(raw_ref[span, :], coef[0:1, :], coef[1:2, :])
        own[span, :] = scaled
        own_t[:, span] = scaled.T
        return 0

    lax.fori_loop(0, depth // chunk, scale_own, 0)

    def correlate(k, j, panel):
        place = pl.ds(pl.multiple_of(k * width + j * piece, piece), piece)

        def block(i, _):
            span = pl.ds(pl.multiple_of(i * 256, 256), 256)
            total = jnp.dot(own_t[span, :], panel[...], preferred_element_type=jnp.float32)
            parts[span, place] = total
            far_parts[span, place] = total.astype(jnp.bfloat16)
            return 0

        lax.fori_loop(0, width // 256, block, 0)
        for d in range(shards - 1):
            part_copy(k, j, d).start()
        out_ref[:, place] = parts[pl.ds(pl.multiple_of(samp * rows, rows), rows), place]

    def finish(k, j):
        place = slice(k * width + j * piece, k * width + (j + 1) * piece)
        total = out_ref[:, place]
        for d in range(shards - 1):
            part_copy(k, j, d).wait()
            landed = far_in[d, :, place] if d < half else near_in[d - half, :, place]
            total = total + landed.astype(jnp.float32)
        out_ref[:, place] = total / samples

    for j in range(PIECES):
        correlate(0, j, own.at[:, pl.ds(j * piece, piece)])
    ahead = [(1, 0)]
    for j in range(PIECES):
        ahead += [(1, j + 1)] if j + 1 < PIECES else []
        ahead += [(k, j) for k in range(2, reach + 1)]
    level = [(k, j) for j in range(PIECES) for k in range(reach, 0, -1)]
    for (k_even, j_even), (k_odd, j_odd) in zip(ahead, level):
        k_last = k_odd if k_odd == 1 else reach + 2 - k_odd
        k = jnp.where(even, k_even, jnp.where(turn == 3, k_last, k_odd))
        j = jnp.where(even, j_even, j_odd)
        columns = pl.ds(pl.multiple_of(j * piece, piece), piece)

        @pl.when(band + k < bands)
        def _():
            panel_copy(k, j).wait_recv()

            @pl.when((k == 2) | ((k == 3) & (turn == 1)))
            def _():
                relay_copy(k, j).start()

            @pl.when(j == 0)
            def _():
                coef_copy(k).wait_recv()

            mean, scale = coef_in[k - 1, 0:1, columns], coef_in[k - 1, 1:2, columns]

            def rescale(i, _):
                span = pl.ds(pl.multiple_of(i * chunk, chunk), chunk)
                work[span, :] = standard(window[k - 1, span, columns], mean, scale)
                return 0

            lax.fori_loop(0, depth // chunk, rescale, 0)
            correlate(k, j, work)

    for j in range(PIECES):
        finish(0, j)
    for j in range(PIECES):
        for k in range(1, reach + 1):
            @pl.when(band + k < bands)
            def _():
                finish(k, j)

            @pl.when(band + k >= bands)
            def _():
                place = slice(k * width + j * piece, k * width + (j + 1) * piece)
                out_ref[:, place] = jnp.zeros((rows, piece), jnp.float32)
    for k in range(1, reach + 1):
        @pl.when(band >= k)
        def _():
            coef_copy(k).wait_send()

        for j in range(PIECES):
            @pl.when(sends(k))
            def _():
                panel_copy(k, j).wait_send()

            if k > 1:
                @pl.when((band + k < bands) & ((k == 2) | (turn == 1)))
                def _():
                    relay_copy(k, j).wait_send()


def general(bands, shards, dosage):
    depth, width = dosage.shape
    reach = (WIN - TILE + width - 1) // width
    rows = width // shards
    f32 = jnp.float32
    dma = pltpu.SemaphoreType.DMA
    return pl.pallas_call(
        functools.partial(kernel, bands, shards, reach, depth * shards),
        out_shape=jax.ShapeDtypeStruct((rows, WIN), f32),
        in_specs=[pl.BlockSpec(memory_space=pltpu.HBM)],
        out_specs=pl.BlockSpec(memory_space=pltpu.VMEM),
        scratch_shapes=[
            pltpu.VMEM((width, depth), jnp.bfloat16),
            pltpu.VMEM((reach + 1, depth, width), jnp.bfloat16),
            pltpu.VMEM((8, width), f32),
            pltpu.VMEM((shards - 1, 8, width), f32),
            pltpu.VMEM((8, width), f32),
            pltpu.VMEM((reach, 8, width), f32),
            pltpu.VMEM((width, WIN), f32),
            pltpu.VMEM((width, WIN), jnp.bfloat16),
            pltpu.VMEM((max(shards // 2 - 1, 1), rows, WIN), f32),
            pltpu.VMEM((shards // 2, rows, WIN), jnp.bfloat16),
            dma((reach, PIECES)), dma((reach, PIECES)),
            dma((shards - 1,)), dma((shards - 1,)),
            dma((reach,)), dma((reach,)),
            dma((reach + 1, PIECES, shards - 1)), dma((reach + 1, PIECES, shards - 1)),
            dma((reach - 1, PIECES)),
            pltpu.VMEM((depth, width // PIECES), jnp.bfloat16),
            pltpu.VMEM((depth, width), jnp.bfloat16),
            dma(()),
        ],
        compiler_params=pltpu.CompilerParams(
            collective_id=0, has_side_effects=True, vmem_limit_bytes=48 * 1024 * 1024
        ),
    )(dosage)


ORDER = (
    (4, 5, 0, 1, 2, 3, 15, 15),
    (0, 4, 1, 5, 2, 3, 15, 15),
    (0, 1, 2, 3, 15, 15, 15, 15),
    (0, 1, 2, 3, 15, 15, 15, 15),
    (15, 15, 15, 15, 15, 15, 15, 15),
    (15, 15, 15, 15, 15, 15, 15, 15),
    (0, 2, 1, 3, 15, 15, 15, 15),
    (4, 0, 5, 1, 2, 3, 6, 7),
)
RELAYS = (
    {0: 4, 3: 5},
    {5: 4, 7: 5},
    {4: 0, 5: 1},
    {},
    {},
    {7: 4, 8: 5},
    {},
    {0: 4, 1: 0, 3: 5, 4: 1, 6: 2, 9: 3},
)
SENDS = {
    2: [(0, 0, 0), (1, 0, 1), (2, 0, 2), (3, 0, 3)],
    3: [(2, 7, 4), (3, 7, 5), (0, 1, 0), (1, 1, 1), (0, 7, 6), (1, 7, 7)],
    4: [(0, 0, 4), (1, 0, 5), (2, 1, 4), (3, 1, 5), (2, 6, 2), (3, 6, 3)],
    5: [(0, 7, 0), (1, 7, 1), (2, 7, 2), (3, 7, 3)],
}
EARLY = {2: (0,), 3: (0, 2), 4: (0,), 5: (0,)}
LATE = {3: {6: ((0,), (4, 5))}, 4: {0: ((0,), (2, 3)), 2: ((2,), (4, 5))}}
COEFS = {2: [(0, 0)], 3: [(1, 0), (7, 1)], 4: [(0, 1), (1, 1), (2, 0), (6, 0)], 5: [(7, 0), (3, 0)]}
SOURCES = ((0, 1, 0, 1), (0, 1, 0, 4), (0, 1, 0, 1), (0, 1, 0, 2), (0, 1, 2, 2), (0, 2, 2, 3), (0, 1, 3, 3), (0, 3, 3, 3))
CROSS = {3: (7,), 4: (6,), 6: (4,), 7: (3,)}
HOLD = {6: 0, 7: 1, 8: 2, 9: 3}
LAG = 3
NONE = 15


def peers(bands):
    plane = {b: {b + 1 - 2 * (b % 2)} for b in range(bands)}
    pairs = [(b, target) for b in SENDS for _, target, _ in SENDS[b]] + [(b, target) for b in COEFS for target, _ in COEFS[b]]
    pairs += [(0, 2), (1, 2), (2, 6), (5, 1), (7, 3), (7, 5)] + [(b, target) for b in CROSS for target in CROSS[b]]
    for a, b in pairs:
        plane[a].add(b)
        plane[b].add(a)
    line = {b: {b, b + 1 - 2 * (b % 2), *CROSS.get(b, ())} for b in range(bands)}
    return plane, line


def ladder_kernel(bands, shards, samples, dosage_ref, out_ref, raw, rhs, lhs, window, parts, turned, total,
                  land, carry_in, stats, stats_in, coef, coef_in, load_s, panel_s, panel_r, relay_s, stat_s,
                  stat_r, coef_s, coef_r, twin_s, twin_r, part_s, part_r, carry_r, hold, hold_s, hold_r, keep):
    band = lax.axis_index("band")
    samp = lax.axis_index("samp")
    pieces, depth, piece = raw.shape
    width = pieces * piece
    rows = width // shards
    core = lax.rem(band, 2)
    even = band - core
    twin = band + 1 - 2 * core
    upper = band >= 6
    outer = (samp == 0) | (samp == 3)
    inner = jnp.logical_not(outer)
    near = samp + 1 - 2 * lax.rem(samp, 2)
    middle = jnp.where(samp < 2, 2, 1)
    far = jnp.where(samp < 2, 3, 0)

    def pick(values):
        result = jnp.int32(values[0])
        for i, value in enumerate(values[1:], 1):
            result = jnp.where(band == i, jnp.int32(value), result)
        return result

    def among(*which):
        result = band == which[0]
        for i in which[1:]:
            result = result | (band == i)
        return result

    def lookup(table, n):
        result = jnp.int32(NONE)
        for b in range(bands):
            for i, value in (table[b].items() if isinstance(table[b], dict) else enumerate(table[b])):
                if value != NONE:
                    result = jnp.where((band == b) & (n == i), jnp.int32(value), result)
        return result

    loads = [
        pltpu.make_async_copy(dosage_ref.at[:, pl.ds(j * piece, piece)], raw.at[j], load_s.at[j])
        for j in range(pieces)
    ]
    for load in loads:
        load.start()
    barrier = pltpu.get_barrier_semaphore()
    plane, line = peers(bands)
    for b in range(bands):
        @pl.when(band == b)
        def _():
            for peer in sorted(plane[b]):
                pl.semaphore_signal(barrier, inc=1, device_id=(peer, samp), device_id_type=MESH)
            for peer in sorted(line[b]):
                for d in range(1, shards):
                    pl.semaphore_signal(barrier, inc=1, device_id=(peer, lax.rem(samp + d, shards)),
                                        device_id_type=MESH)

    step = 256

    def measure(j, _):
        def add(i, carry):
            x = raw[j, pl.ds(pl.multiple_of(i * step, step), step), :].astype(jnp.float32)
            seen = jnp.where(x >= 0.0, 1.0, 0.0)
            value = jnp.maximum(x, 0.0)
            fold = lambda a: jnp.sum(a.reshape(step // 8, 8, piece), axis=0)
            return carry[0] + fold(seen), carry[1] + fold(value), carry[2] + fold(value * value)

        zero = jnp.zeros((8, piece), jnp.float32)
        sums = lax.fori_loop(0, depth // step, add, (zero, zero, zero))
        for i, a in enumerate(sums):
            stats[pl.ds(pieces * i + j, 1), :] = jnp.sum(a, axis=0, keepdims=True)
        return 0

    for load in loads:
        load.wait()
    stats[3 * pieces:, :] = jnp.zeros((pieces, piece), jnp.float32)
    lax.fori_loop(0, pieces, measure, 0)
    pl.semaphore_wait(barrier, pick([len(plane[b]) + (shards - 1) * len(line[b]) for b in range(bands)]))

    def panel_copy(source, i):
        j, target, slot = SENDS[source][i]
        return remote(raw.at[j], window.at[slot], panel_s.at[i], panel_r.at[slot], target, samp)

    late = {source: [i for _, (_, starts) in events.items() for i in starts] for source, events in LATE.items()}
    waited = {source: [i for _, (waits, _) in events.items() for i in waits] for source, events in LATE.items()}
    for source in SENDS:
        @pl.when(band == source)
        def _():
            for i in EARLY[source]:
                panel_copy(source, i).start()

    stat_copies = [
        remote(stats, stats_in.at[d - 1], stat_s, stat_r, band, lax.rem(samp + d, shards))
        for d in range(1, shards)
    ]
    for copy in stat_copies:
        copy.start()
    remote(stats_in, stats_in, stat_s, stat_r, twin, samp).wait()
    sums = stats[...]
    for d in range(shards - 1):
        sums = sums + stats_in[d]
    count, sum1, square = (sums[pieces * i:pieces * (i + 1)] for i in range(3))
    mean = (sum1 + 1.0) / (count + 1.0)
    spread = (square - 2.0 * mean * sum1 + count * mean * mean + 0.5) / (count + 1.0)
    coef[0:pieces, :] = mean
    coef[pieces:2 * pieces, :] = lax.rsqrt(spread)

    def coef_copy(source, i):
        target, slot = COEFS[source][i]
        return remote(coef, coef_in.at[slot], coef_s.at[i], coef_r.at[slot], target, samp)

    for source in COEFS:
        @pl.when(band == source)
        def _():
            for i in range(len(COEFS[source])):
                coef_copy(source, i).start()
            for i in range(len(SENDS[source])):
                if i not in late.get(source, []) and i not in EARLY[source]:
                    panel_copy(source, i).start()

    chunk = 512

    def standard(x, mean, scale):
        x = x.astype(jnp.float32)
        return jnp.where(x >= 0.0, (x - mean) * scale, 0.0).astype(jnp.bfloat16)

    def twin_copy(j):
        place = pl.ds(pl.multiple_of(core * width + j * piece, piece), piece)
        return remote(lhs.at[place, :], lhs.at[place, :], twin_s, twin_r, twin, samp)

    def twin_wait():
        place = pl.ds(pl.multiple_of((1 - core) * width, width), width)
        return remote(lhs.at[place, :], lhs.at[place, :], twin_s, twin_r, twin, samp)

    def scale_own(j, _):
        place = pl.ds(pl.multiple_of(core * width + j * piece, piece), piece)
        mean, scale = coef[pl.ds(j, 1), :], coef[pl.ds(pieces + j, 1), :]

        def part(i, _):
            span = pl.ds(pl.multiple_of(i * chunk, chunk), chunk)
            scaled = standard(raw[j, span, :], mean, scale)
            rhs[j, span, :] = scaled
            lhs[place, span] = scaled.T
            return 0

        lax.fori_loop(0, depth // chunk, part, 0)
        twin_copy(j).start()
        return 0

    lax.fori_loop(0, pieces, scale_own, 0)

    def relay_copy(w):
        target = jnp.where(w < 4, pick((2, 2, 6, 0, 0, 1, 0, 3)), pick((2, 2, 6, 0, 0, 1, 0, 5)))
        slot = jnp.clip(w + pick((-4, -2, 0, 0, 0, -2, 0, 0)), 0, 5)
        return remote(window.at[w], window.at[slot], relay_s.at[w], panel_r.at[slot], target, samp)

    def arrival(w):
        return remote(window.at[w], window.at[w], relay_s.at[w], panel_r.at[w], twin, samp)

    def relayed(w):
        return (among(0, 1, 5) & (w >= 4)) | ((band == 2) & (w < 2)) | ((band == 7) & (w < 6))

    def job(n):
        w = lookup(ORDER, n - pieces)
        own = n < pieces
        active = own | (w != NONE)
        w = jnp.minimum(w, 7)
        both = jnp.logical_not(own) & (w < 4)
        single = jnp.logical_not(own) & (w >= 4)
        q = jnp.where(own, n, jnp.where(both, w, lax.rem(jnp.maximum(2 * core + w - 4, 0), pieces)))
        return w, own, both, single, active, q

    def needs(n, r):
        w, own, both, single, active, q = job(n)
        return active & (both | (own & ((r == 0) | (core == 1))) | (single & (r == jnp.where(upper, 0, 1))))

    def block_of(n, r):
        w, own, both, single, active, q = job(n)
        return jnp.clip(jnp.where(single, 3, jnp.where(own, 0, 2) + core - r), 0, 3)

    def lower(n):
        return (n < pieces) | jnp.logical_not(upper)

    def part_copy(n, r, k, q, i):
        columns = pl.ds(pl.multiple_of(k * width + q * piece, piece), piece)
        target = (near, middle, far, samp)[i]
        slot = (0, jnp.where(outer, 2, 1), 1, 3)[i]
        source = parts.at[pl.ds(pl.multiple_of(n * 2 * width + r * width + target * rows, rows), rows), :]
        return remote(source, land.at[slot, :, columns], part_s, part_r.at[k, slot],
                      even + r, target)

    def carry_copy(n, r):
        source = parts.at[pl.ds(pl.multiple_of(n * 2 * width + r * width + far * rows, rows), rows), :]
        return remote(source, carry_in.at[n, r], part_s, carry_r.at[n], band, near)

    def turned_copy(n, r, single, q, held):
        k = jnp.clip(jnp.where(single, 3, 2 - core + r), 0, 3)
        source = turned.at[n - pieces, :, pl.ds(pl.multiple_of(r * width, width), width)]
        to = jnp.where(single, 3, jnp.maximum(band - 2, 0))
        if held:
            return remote(source, hold.at[q, r], part_s, hold_r.at[q], to, samp)
        return remote(source, land.at[samp, :, pl.ds(pl.multiple_of(k * width, width), width)],
                      part_s, part_r.at[k, samp], to, q)

    def hold_copy(r, q):
        return remote(hold.at[q, r], land.at[samp, :, (1 + r) * width:(2 + r) * width], hold_s,
                      part_r.at[1 + r, samp], band, q)

    def hold_wait(q):
        return remote(hold.at[q], hold.at[q], hold_s, hold_r.at[q], twin, samp)

    def is_held(both, q):
        return (band == 7) & both & (q != samp)

    def carry_on(n):
        first, second = needs(n, 0), needs(n, 1)

        @pl.when((first | second) & lower(n) & inner)
        def _():
            @pl.when(first & second)
            def _():
                remote(carry_in.at[n], carry_in.at[n], part_s, carry_r.at[n], twin, samp).wait_recv()

            @pl.when(jnp.logical_not(first & second))
            def _():
                remote(carry_in.at[n, 0], carry_in.at[n, 0], part_s, carry_r.at[n], twin, samp).wait_recv()

            def one(r, _):
                @pl.when(needs(n, r))
                def _():
                    w, own, both, single, active, q = job(n)
                    place = pl.ds(pl.multiple_of(n * 2 * width + r * width + far * rows, rows), rows)
                    parts[place, :] = (keep[n, r] + carry_in[n, r].astype(jnp.float32)).astype(jnp.bfloat16)
                    part_copy(n, r, block_of(n, r), q, 2).start()

                return 0

            lax.fori_loop(0, 2, one, 0)

    jobs = pieces + len(ORDER[0])

    def run(n, _):
        event = lookup(RELAYS, n)

        @pl.when(event != NONE)
        def _():
            w = jnp.minimum(event, 5)
            arrival(w).wait_recv()
            relay_copy(w).start()

        @pl.when((n == pieces) & (core == 0))
        def _():
            twin_wait().wait_recv()

        for when, q in HOLD.items():
            @pl.when((band == 5) & (n == when) & (samp != q))
            def _():
                hold_wait(q).wait_recv()
                for r in range(2):
                    hold_copy(r, q).start()

        for source, events in LATE.items():
            for when, (waits, starts) in events.items():
                @pl.when((band == source) & (n == when))
                def _():
                    for i in waits:
                        panel_copy(source, i).wait_send()
                    for i in starts:
                        panel_copy(source, i).start()

        w, own, both, single, active, q = job(n)

        @pl.when(active)
        def _():
            @pl.when(jnp.logical_not(own))
            def _():
                @pl.when(jnp.logical_not(relayed(w)))
                def _():
                    arrival(w).wait_recv()

                slot = jnp.where(both, 0, 1)

                @pl.when((w == 0) | (w == 4))
                def _():
                    remote(coef, coef_in.at[slot], coef_s.at[0], coef_r.at[slot], twin, samp).wait_recv()

                mean, scale = coef_in[slot, pl.ds(q, 1), :], coef_in[slot, pl.ds(pieces + q, 1), :]

                def rescale(i, _):
                    span = pl.ds(pl.multiple_of(i * chunk, chunk), chunk)
                    rhs[pieces, span, :] = standard(window[w, span, :], mean, scale)
                    return 0

                lax.fori_loop(0, depth // chunk, rescale, 0)

            index = jnp.where(own, q, pieces)

            def multiply(i, _):
                r = lax.rem(core + i, 2)

                @pl.when(needs(n, r))
                def _():
                    @pl.when((i == 1) & (n == jnp.where(core == 1, 0, NONE)))
                    def _():
                        twin_wait().wait_recv()

                    place = pl.ds(pl.multiple_of(r * width, width), width)
                    total[...] = jnp.dot(lhs[place, :], rhs[index], preferred_element_type=jnp.float32)

                    @pl.when(lower(n))
                    def _():
                        k = block_of(n, r)
                        parts[pl.ds(pl.multiple_of(n * 2 * width + r * width, width), width), :] = total[...].astype(jnp.bfloat16)

                        @pl.when(outer)
                        def _():
                            carry_copy(n, r).start()

                        part_copy(n, r, k, q, 1).start()
                        part_copy(n, r, k, q, 0).start()

                        @pl.when(core != r)
                        def _():
                            part_copy(n, r, k, q, 3).start()

                        @pl.when(inner)
                        def _():
                            keep[n, r] = total[pl.ds(pl.multiple_of(far * rows, rows), rows), :]

                        @pl.when(core == r)
                        def _():
                            columns = pl.ds(pl.multiple_of(k * width + q * piece, piece), piece)
                            out_ref[:, columns] = total[pl.ds(pl.multiple_of(samp * rows, rows), rows), :]

                    @pl.when(jnp.logical_not(lower(n)))
                    def _():
                        m = jnp.maximum(n, pieces)
                        turned[m - pieces, :, place] = total[...].T.astype(jnp.bfloat16)

                        @pl.when(is_held(both, q))
                        def _():
                            turned_copy(m, r, single, q, True).start()

                        @pl.when(jnp.logical_not(is_held(both, q)))
                        def _():
                            turned_copy(m, r, single, q, False).start()

                return 0

            lax.fori_loop(0, 2, multiply, 0)

        @pl.when(n >= LAG)
        def _():
            carry_on(jnp.maximum(n - LAG, 0))

        return 0

    lax.fori_loop(0, jobs, run, 0)
    for n in range(jobs - LAG, jobs):
        carry_on(n)

    def landed(k, slot):
        place = slice(k * width, (k + 1) * width)
        remote(land.at[slot, :, place], land.at[slot, :, place], part_s, part_r.at[k, slot], twin, samp).wait_recv()

    def finish(k):
        kind = pick([row[k] for row in SOURCES])
        place = slice(k * width, (k + 1) * width)

        @pl.when((kind != 2) & (kind != 3))
        def _():
            landed(k, 0)
            landed(k, 1)

            @pl.when(inner)
            def _():
                landed(k, 2)

            def close(spot, slots):
                result = out_ref[:, spot] if 3 not in slots else land[3, :, spot].astype(jnp.float32)
                for slot in slots[:2]:
                    result = result + land[slot, :, spot].astype(jnp.float32)
                out_ref[:, spot] = result / samples

            @pl.when(kind == 0)
            def _():
                close(place, (0, 1))

            @pl.when(kind == 1)
            def _():
                landed(k, 3)
                close(place, (0, 1, 3))

            @pl.when(kind == 4)
            def _():
                mid = k * width + width // 2
                spot = slice(k * width, mid)
                remote(land.at[3, :, spot], land.at[3, :, spot], part_s, part_r.at[k, 3], twin, samp).wait_recv()
                close(spot, (0, 1, 3))
                close(slice(mid, (k + 1) * width), (0, 1))

            @pl.when(inner)
            def _():
                out_ref[:, place] += land[2, :, place].astype(jnp.float32) / samples

        @pl.when(kind == 3)
        def _():
            out_ref[:, place] = jnp.zeros((rows, width), jnp.float32)

    def gather(k):
        place = slice(k * width, (k + 1) * width)
        for z in range(shards):
            landed(k, z)
        result = land[0, :, place].astype(jnp.float32)
        for z in range(1, shards):
            result = result + land[z, :, place].astype(jnp.float32)
        out_ref[:, place] = result / samples

    for k in range(4):
        finish(k)
    for b, k in ((3, 3), (4, 2), (4, 3), (5, 1), (5, 2)):
        @pl.when(band == b)
        def _():
            gather(k)

    for source in SENDS:
        @pl.when(band == source)
        def _():
            for i in range(len(SENDS[source])):
                if i not in waited.get(source, []):
                    panel_copy(source, i).wait_send()
            for i in range(len(COEFS[source])):
                coef_copy(source, i).wait_send()
    for w in range(6):
        @pl.when(relayed(w))
        def _():
            relay_copy(jnp.int32(w)).wait_send()
    twin_wait().wait_send()

    @pl.when(band == 5)
    def _():
        remote(hold.at[0:shards - 1], hold.at[0:shards - 1], hold_s, hold_r.at[0], twin, samp).wait_send()

    for b in range(bands):
        odd = b % 2
        sent = pieces * (3 + 4 * odd)
        if b >= 6:
            sent += sum(pieces * (2 if w < 4 else 1) for w in ORDER[b] if w != NONE)
        else:
            sent += sum(7 if w < 4 else 4 - odd for w in ORDER[b] if w != NONE)

        @pl.when(band == b)
        def _():
            span = pl.ds(0, sent * rows)
            remote(parts.at[span, :], parts.at[span, :], part_s, part_r.at[0, 0], twin, samp).wait_send()


def ladder(bands, shards, dosage):
    depth, width = dosage.shape
    pieces = shards
    piece = width // pieces
    rows = width // shards
    jobs = pieces + len(ORDER[0])
    f32, b16 = jnp.float32, jnp.bfloat16
    dma = pltpu.SemaphoreType.DMA
    return pl.pallas_call(
        functools.partial(ladder_kernel, bands, shards, depth * shards),
        out_shape=jax.ShapeDtypeStruct((rows, WIN), f32),
        in_specs=[pl.BlockSpec(memory_space=pltpu.HBM)],
        out_specs=pl.BlockSpec(memory_space=pltpu.VMEM),
        scratch_shapes=[
            pltpu.VMEM((pieces, depth, piece), b16),
            pltpu.VMEM((pieces + 1, depth, piece), b16),
            pltpu.VMEM((2 * width, depth), b16),
            pltpu.VMEM((8, depth, piece), b16),
            pltpu.VMEM((jobs * 2 * width, piece), b16),
            pltpu.VMEM((jobs - pieces, rows, 2 * width), b16),
            pltpu.VMEM((width, piece), f32),
            pltpu.VMEM((4, rows, WIN), b16),
            pltpu.VMEM((jobs, 2, rows, piece), b16),
            pltpu.VMEM((4 * pieces, piece), f32),
            pltpu.VMEM((shards - 1, 4 * pieces, piece), f32),
            pltpu.VMEM((2 * pieces, piece), f32),
            pltpu.VMEM((2, 2 * pieces, piece), f32),
            dma((pieces,)),
            dma((6,)), dma((8,)), dma((6,)),
            dma(()), dma(()),
            dma((4,)), dma((2,)),
            dma(()), dma(()),
            dma(()), dma((4, 4)), dma((jobs,)),
            pltpu.VMEM((pieces, 2, rows, width), b16),
            dma(()), dma((pieces,)),
            pltpu.VMEM((jobs, 2, rows, piece), f32),
        ],
        compiler_params=pltpu.CompilerParams(
            collective_id=0, has_side_effects=True, vmem_limit_bytes=52 * 1024 * 1024
        ),
    )(dosage)


def on_device(bands, shards, dosage):
    if bands == len(ORDER) and shards == 4 and dosage.shape[1] == TILE:
        return ladder(bands, shards, dosage)
    return general(bands, shards, dosage)


def solution(mesh):
    return jax.shard_map(
        functools.partial(on_device, mesh.shape["band"], mesh.shape["samp"]),
        mesh=mesh,
        in_specs=(P("samp", "band"),),
        out_specs=P(("band", "samp"), None),
        check_vma=False,
    )
```

```python
import functools

import jax
import jax.numpy as jnp
from jax import lax
from jax.experimental import pallas as pl
from jax.experimental.pallas import tpu as pltpu
from jax.sharding import PartitionSpec as P

TILE = 512
WIN = 2048
PIECES = 4
MESH = pl.DeviceIdType.MESH


def remote(src, dst, send, recv, band, samp):
    return pltpu.make_async_remote_copy(
        src_ref=src, dst_ref=dst, send_sem=send, recv_sem=recv,
        device_id=(band, samp), device_id_type=MESH,
    )


def kernel(bands, shards, reach, samples, dosage_ref, out_ref, own_t, window, stats, stats_in, coef,
           coef_in, parts, far_parts, near_in, far_in, panel_s, panel_r, stat_s, stat_r, coef_s, coef_r,
           part_s, part_r, relay_s, work, raw_ref, load_s):
    band = lax.axis_index("band")
    samp = lax.axis_index("samp")
    depth, width = raw_ref.shape
    load = pltpu.make_async_copy(dosage_ref, raw_ref, load_s)
    load.start()
    rows = width // shards
    piece = width // PIECES
    half = shards // 2
    side, seat = samp // half, lax.rem(samp, half)
    near = [side * half + lax.rem(seat + d, half) for d in range(1, half)]
    far = [(1 - side) * half + lax.rem(seat + d, half) for d in range(half)]
    peers = far + near

    barrier = pltpu.get_barrier_semaphore()
    for peer in peers:
        pl.semaphore_signal(barrier, inc=1, device_id=(band, peer), device_id_type=MESH)
    expected = shards - 1
    for k in range(1, reach + 1):
        @pl.when(band >= k)
        def _():
            pl.semaphore_signal(barrier, inc=1, device_id=(band - k, samp), device_id_type=MESH)

        @pl.when(band + k < bands)
        def _():
            pl.semaphore_signal(barrier, inc=1, device_id=(band + k, samp), device_id_type=MESH)
    expected = expected + jnp.minimum(band, reach) + jnp.minimum(bands - 1 - band, reach)
    pl.semaphore_wait(barrier, expected)
    load.wait()

    def panel_copy(k, j):
        columns = pl.ds(pl.multiple_of(j * piece, piece), piece)
        return remote(raw_ref.at[:, columns], window.at[k - 1, :, columns],
                      panel_s.at[k - 1, j], panel_r.at[k - 1, j], jnp.maximum(band - k, 0), samp)

    even = lax.rem(band, 2) == 0
    turn = lax.rem(band, 4)

    def sends(k):
        if k == 1:
            return jnp.logical_not(even)
        if k == 2:
            return (band >= 2) & (turn != 0)
        return even & (band >= 3)

    def relay_copy(k, j):
        columns = pl.ds(pl.multiple_of(j * piece, piece), piece)
        onward = (k == 2) & jnp.logical_not(even)
        target = jnp.clip(jnp.where(onward, band - 1, band + 1), 0, bands - 1)
        slot = jnp.where(k == 3, 1, jnp.where(even, 0, 2))
        return remote(window.at[k - 1, :, columns], window.at[slot, :, columns],
                      relay_s.at[k - 2, j], panel_r.at[slot, j], target, samp)

    def coef_copy(k):
        return remote(coef, coef_in.at[k - 1], coef_s.at[k - 1], coef_r.at[k - 1],
                      jnp.maximum(band - k, 0), samp)

    def part_copy(k, j, d):
        columns = pl.ds(pl.multiple_of(k * width + j * piece, piece), piece)
        source, landing, slot = (far_parts, far_in, d) if d < half else (parts, near_in, d - half)
        return remote(source.at[pl.ds(pl.multiple_of(peers[d] * rows, rows), rows), columns],
                      landing.at[slot, :, columns],
                      part_s.at[k, j, d], part_r.at[k, j, d], band, peers[d])

    def start_panel(k, j):
        @pl.when(sends(k))
        def _():
            panel_copy(k, j).start()

    early = [(k, 0) for k in range(1, reach + 1)]
    later = [(k, j) for j in range(PIECES) for k in range(1, reach + 1) if (k, j) not in early]
    for k, j in early:
        start_panel(k, j)

    step = 64

    def add(i, carry):
        x = raw_ref[pl.ds(pl.multiple_of(i * step, step), step), :].astype(jnp.float32)
        seen = jnp.where(x >= 0.0, 1.0, 0.0)
        value = jnp.where(x >= 0.0, x, 0.0)
        fold = lambda a: jnp.sum(a.reshape(step // 8, 8, width), axis=0)
        return carry[0] + fold(seen), carry[1] + fold(value), carry[2] + fold(value * value)

    zero = jnp.zeros((8, width), jnp.float32)
    sums = lax.fori_loop(0, depth // step, add, (zero, zero, zero))
    stats[...] = jnp.concatenate(
        [jnp.sum(a, axis=0, keepdims=True) for a in sums] + [jnp.zeros((5, width), jnp.float32)], axis=0
    )
    stat_copies = [
        remote(stats, stats_in.at[d], stat_s.at[d], stat_r.at[d], band, peers[d])
        for d in range(shards - 1)
    ]
    for copy in stat_copies:
        copy.start()
    for copy in stat_copies:
        copy.wait()
    sums = stats[...]
    for d in range(shards - 1):
        sums = sums + stats_in[d]
    count, total, square = sums[0:1], sums[1:2], sums[2:3]
    mean = (total + 1.0) / (count + 1.0)
    spread = (square - 2.0 * mean * total + count * mean * mean + 0.5) / (count + 1.0)
    coef[...] = jnp.concatenate(
        [mean, lax.rsqrt(spread), jnp.zeros((6, width), jnp.float32)], axis=0
    )
    for k in range(1, reach + 1):
        @pl.when(band >= k)
        def _():
            coef_copy(k).start()
    for k, j in later:
        start_panel(k, j)

    chunk = 256

    def standard(x, mean, scale):
        x = x.astype(jnp.float32)
        return jnp.where(x >= 0.0, (x - mean) * scale, 0.0).astype(jnp.bfloat16)

    own = window.at[reach]

    def scale_own(i, _):
        span = pl.ds(pl.multiple_of(i * chunk, chunk), chunk)
        scaled = standard(raw_ref[span, :], coef[0:1, :], coef[1:2, :])
        own[span, :] = scaled
        own_t[:, span] = scaled.T
        return 0

    lax.fori_loop(0, depth // chunk, scale_own, 0)

    def correlate(k, j, panel):
        place = pl.ds(pl.multiple_of(k * width + j * piece, piece), piece)

        def block(i, _):
            span = pl.ds(pl.multiple_of(i * 256, 256), 256)
            total = jnp.dot(own_t[span, :], panel[...], preferred_element_type=jnp.float32)
            parts[span, place] = total
            far_parts[span, place] = total.astype(jnp.bfloat16)
            return 0

        lax.fori_loop(0, width // 256, block, 0)
        for d in range(shards - 1):
            part_copy(k, j, d).start()
        out_ref[:, place] = parts[pl.ds(pl.multiple_of(samp * rows, rows), rows), place]

    def finish(k, j):
        place = slice(k * width + j * piece, k * width + (j + 1) * piece)
        total = out_ref[:, place]
        for d in range(shards - 1):
            part_copy(k, j, d).wait()
            landed = far_in[d, :, place] if d < half else near_in[d - half, :, place]
            total = total + landed.astype(jnp.float32)
        out_ref[:, place] = total / samples

    for j in range(PIECES):
        correlate(0, j, own.at[:, pl.ds(j * piece, piece)])
    ahead = [(1, 0)]
    for j in range(PIECES):
        ahead += [(1, j + 1)] if j + 1 < PIECES else []
        ahead += [(k, j) for k in range(2, reach + 1)]
    level = [(k, j) for j in range(PIECES) for k in range(reach, 0, -1)]
    for (k_even, j_even), (k_odd, j_odd) in zip(ahead, level):
        k_last = k_odd if k_odd == 1 else reach + 2 - k_odd
        k = jnp.where(even, k_even, jnp.where(turn == 3, k_last, k_odd))
        j = jnp.where(even, j_even, j_odd)
        columns = pl.ds(pl.multiple_of(j * piece, piece), piece)

        @pl.when(band + k < bands)
        def _():
            panel_copy(k, j).wait_recv()

            @pl.when((k == 2) | ((k == 3) & (turn == 1)))
            def _():
                relay_copy(k, j).start()

            @pl.when(j == 0)
            def _():
                coef_copy(k).wait_recv()

            mean, scale = coef_in[k - 1, 0:1, columns], coef_in[k - 1, 1:2, columns]

            def rescale(i, _):
                span = pl.ds(pl.multiple_of(i * chunk, chunk), chunk)
                work[span, :] = standard(window[k - 1, span, columns], mean, scale)
                return 0

            lax.fori_loop(0, depth // chunk, rescale, 0)
            correlate(k, j, work)

    for j in range(PIECES):
        finish(0, j)
    for j in range(PIECES):
        for k in range(1, reach + 1):
            @pl.when(band + k < bands)
            def _():
                finish(k, j)

            @pl.when(band + k >= bands)
            def _():
                place = slice(k * width + j * piece, k * width + (j + 1) * piece)
                out_ref[:, place] = jnp.zeros((rows, piece), jnp.float32)
    for k in range(1, reach + 1):
        @pl.when(band >= k)
        def _():
            coef_copy(k).wait_send()

        for j in range(PIECES):
            @pl.when(sends(k))
            def _():
                panel_copy(k, j).wait_send()

            if k > 1:
                @pl.when((band + k < bands) & ((k == 2) | (turn == 1)))
                def _():
                    relay_copy(k, j).wait_send()


def general(bands, shards, dosage):
    depth, width = dosage.shape
    reach = (WIN - TILE + width - 1) // width
    rows = width // shards
    f32 = jnp.float32
    dma = pltpu.SemaphoreType.DMA
    return pl.pallas_call(
        functools.partial(kernel, bands, shards, reach, depth * shards),
        out_shape=jax.ShapeDtypeStruct((rows, WIN), f32),
        in_specs=[pl.BlockSpec(memory_space=pltpu.HBM)],
        out_specs=pl.BlockSpec(memory_space=pltpu.VMEM),
        scratch_shapes=[
            pltpu.VMEM((width, depth), jnp.bfloat16),
            pltpu.VMEM((reach + 1, depth, width), jnp.bfloat16),
            pltpu.VMEM((8, width), f32),
            pltpu.VMEM((shards - 1, 8, width), f32),
            pltpu.VMEM((8, width), f32),
            pltpu.VMEM((reach, 8, width), f32),
            pltpu.VMEM((width, WIN), f32),
            pltpu.VMEM((width, WIN), jnp.bfloat16),
            pltpu.VMEM((max(shards // 2 - 1, 1), rows, WIN), f32),
            pltpu.VMEM((shards // 2, rows, WIN), jnp.bfloat16),
            dma((reach, PIECES)), dma((reach, PIECES)),
            dma((shards - 1,)), dma((shards - 1,)),
            dma((reach,)), dma((reach,)),
            dma((reach + 1, PIECES, shards - 1)), dma((reach + 1, PIECES, shards - 1)),
            dma((reach - 1, PIECES)),
            pltpu.VMEM((depth, width // PIECES), jnp.bfloat16),
            pltpu.VMEM((depth, width), jnp.bfloat16),
            dma(()),
        ],
        compiler_params=pltpu.CompilerParams(
            collective_id=0, has_side_effects=True, vmem_limit_bytes=48 * 1024 * 1024
        ),
    )(dosage)


ORDER = (
    (4, 5, 0, 1, 2, 3, 15, 15),
    (4, 0, 5, 1, 2, 3, 15, 15),
    (0, 1, 2, 3, 15, 15, 15, 15),
    (0, 1, 2, 3, 15, 15, 15, 15),
    (15, 15, 15, 15, 15, 15, 15, 15),
    (15, 15, 15, 15, 15, 15, 15, 15),
    (0, 2, 1, 3, 15, 15, 15, 15),
    (4, 0, 5, 1, 2, 3, 6, 7),
)
RELAYS = (
    {0: 4, 3: 5},
    {4: 4, 6: 5},
    {4: 0, 5: 1},
    {},
    {},
    {7: 4, 8: 5},
    {},
    {0: 4, 1: 0, 3: 5, 4: 1, 6: 2, 9: 3},
)
SENDS = {
    2: [(0, 0, 0), (1, 0, 1), (2, 0, 2), (3, 0, 3)],
    3: [(2, 7, 4), (3, 7, 5), (0, 1, 0), (1, 1, 1), (0, 7, 6), (1, 7, 7)],
    4: [(0, 0, 4), (1, 0, 5), (2, 1, 4), (3, 1, 5), (2, 6, 2), (3, 6, 3)],
    5: [(0, 7, 0), (1, 7, 1), (2, 7, 2), (3, 7, 3)],
}
EARLY = {2: (0,), 3: (0, 2), 4: (0,), 5: (0,)}
LATE = {3: {6: ((0,), (4, 5))}, 4: {0: ((0,), (2, 3)), 2: ((2,), (4, 5))}}
COEFS = {2: [(0, 0)], 3: [(1, 0), (7, 1)], 4: [(0, 1), (1, 1), (2, 0), (6, 0)], 5: [(7, 0), (3, 0)]}
SOURCES = ((0, 1, 0, 1), (0, 1, 0, 4), (0, 1, 0, 1), (0, 1, 0, 2), (0, 1, 2, 2), (0, 2, 2, 3), (0, 1, 3, 3), (0, 3, 3, 3))
CROSS = {3: (7,), 4: (6,), 6: (4,), 7: (3,)}
HOLD = {6: 0, 7: 1, 8: 2, 9: 3}
LAG = 3
NONE = 15


def peers(bands):
    plane = {b: {b + 1 - 2 * (b % 2)} for b in range(bands)}
    pairs = [(b, target) for b in SENDS for _, target, _ in SENDS[b]] + [(b, target) for b in COEFS for target, _ in COEFS[b]]
    pairs += [(0, 2), (1, 2), (2, 6), (5, 1), (7, 3), (7, 5)] + [(b, target) for b in CROSS for target in CROSS[b]]
    for a, b in pairs:
        plane[a].add(b)
        plane[b].add(a)
    line = {b: {b, b + 1 - 2 * (b % 2), *CROSS.get(b, ())} for b in range(bands)}
    return plane, line


def ladder_kernel(bands, shards, samples, dosage_ref, out_ref, raw, rhs, lhs, window, parts, turned, total,
                  land, carry_in, stats, stats_in, coef, coef_in, load_s, panel_s, panel_r, relay_s, stat_s,
                  stat_r, coef_s, coef_r, twin_s, twin_r, part_s, part_r, carry_r, hold, hold_s, hold_r, keep):
    band = lax.axis_index("band")
    samp = lax.axis_index("samp")
    pieces, depth, piece = raw.shape
    width = pieces * piece
    rows = width // shards
    core = lax.rem(band, 2)
    even = band - core
    twin = band + 1 - 2 * core
    upper = band >= 6
    outer = (samp == 0) | (samp == 3)
    inner = jnp.logical_not(outer)
    near = samp + 1 - 2 * lax.rem(samp, 2)
    middle = jnp.where(samp < 2, 2, 1)
    far = jnp.where(samp < 2, 3, 0)

    def pick(values):
        result = jnp.int32(values[0])
        for i, value in enumerate(values[1:], 1):
            result = jnp.where(band == i, jnp.int32(value), result)
        return result

    def among(*which):
        result = band == which[0]
        for i in which[1:]:
            result = result | (band == i)
        return result

    def lookup(table, n):
        result = jnp.int32(NONE)
        for b in range(bands):
            for i, value in (table[b].items() if isinstance(table[b], dict) else enumerate(table[b])):
                if value != NONE:
                    result = jnp.where((band == b) & (n == i), jnp.int32(value), result)
        return result

    loads = [
        pltpu.make_async_copy(dosage_ref.at[:, pl.ds(j * piece, piece)], raw.at[j], load_s.at[j])
        for j in range(pieces)
    ]
    for load in loads:
        load.start()
    barrier = pltpu.get_barrier_semaphore()
    plane, line = peers(bands)
    for b in range(bands):
        @pl.when(band == b)
        def _():
            for peer in sorted(plane[b]):
                pl.semaphore_signal(barrier, inc=1, device_id=(peer, samp), device_id_type=MESH)
            for peer in sorted(line[b]):
                for d in range(1, shards):
                    pl.semaphore_signal(barrier, inc=1, device_id=(peer, lax.rem(samp + d, shards)),
                                        device_id_type=MESH)

    step = 256

    def measure(j, _):
        def add(i, carry):
            x = raw[j, pl.ds(pl.multiple_of(i * step, step), step), :].astype(jnp.float32)
            seen = jnp.where(x >= 0.0, 1.0, 0.0)
            value = jnp.maximum(x, 0.0)
            fold = lambda a: jnp.sum(a.reshape(step // 8, 8, piece), axis=0)
            return carry[0] + fold(seen), carry[1] + fold(value), carry[2] + fold(value * value)

        zero = jnp.zeros((8, piece), jnp.float32)
        sums = lax.fori_loop(0, depth // step, add, (zero, zero, zero))
        for i, a in enumerate(sums):
            stats[pl.ds(pieces * i + j, 1), :] = jnp.sum(a, axis=0, keepdims=True)
        return 0

    for load in loads:
        load.wait()
    stats[3 * pieces:, :] = jnp.zeros((pieces, piece), jnp.float32)
    lax.fori_loop(0, pieces, measure, 0)
    pl.semaphore_wait(barrier, pick([len(plane[b]) + (shards - 1) * len(line[b]) for b in range(bands)]))

    def panel_copy(source, i):
        j, target, slot = SENDS[source][i]
        return remote(raw.at[j], window.at[slot], panel_s.at[i], panel_r.at[slot], target, samp)

    late = {source: [i for _, (_, starts) in events.items() for i in starts] for source, events in LATE.items()}
    waited = {source: [i for _, (waits, _) in events.items() for i in waits] for source, events in LATE.items()}
    for source in SENDS:
        @pl.when(band == source)
        def _():
            for i in EARLY[source]:
                panel_copy(source, i).start()

    stat_copies = [
        remote(stats, stats_in.at[d - 1], stat_s, stat_r, band, lax.rem(samp + d, shards))
        for d in range(1, shards)
    ]
    for copy in stat_copies:
        copy.start()
    remote(stats_in, stats_in, stat_s, stat_r, twin, samp).wait()
    sums = stats[...]
    for d in range(shards - 1):
        sums = sums + stats_in[d]
    count, sum1, square = (sums[pieces * i:pieces * (i + 1)] for i in range(3))
    mean = (sum1 + 1.0) / (count + 1.0)
    spread = (square - 2.0 * mean * sum1 + count * mean * mean + 0.5) / (count + 1.0)
    coef[0:pieces, :] = mean
    coef[pieces:2 * pieces, :] = lax.rsqrt(spread)

    def coef_copy(source, i):
        target, slot = COEFS[source][i]
        return remote(coef, coef_in.at[slot], coef_s.at[i], coef_r.at[slot], target, samp)

    for source in COEFS:
        @pl.when(band == source)
        def _():
            for i in range(len(COEFS[source])):
                coef_copy(source, i).start()
            for i in range(len(SENDS[source])):
                if i not in late.get(source, []) and i not in EARLY[source]:
                    panel_copy(source, i).start()

    chunk = 512

    def standard(x, mean, scale):
        x = x.astype(jnp.float32)
        return jnp.where(x >= 0.0, (x - mean) * scale, 0.0).astype(jnp.bfloat16)

    def twin_copy(j):
        place = pl.ds(pl.multiple_of(core * width + j * piece, piece), piece)
        return remote(lhs.at[place, :], lhs.at[place, :], twin_s, twin_r, twin, samp)

    def twin_wait():
        place = pl.ds(pl.multiple_of((1 - core) * width, width), width)
        return remote(lhs.at[place, :], lhs.at[place, :], twin_s, twin_r, twin, samp)

    def scale_own(j, _):
        place = pl.ds(pl.multiple_of(core * width + j * piece, piece), piece)
        mean, scale = coef[pl.ds(j, 1), :], coef[pl.ds(pieces + j, 1), :]

        def part(i, _):
            span = pl.ds(pl.multiple_of(i * chunk, chunk), chunk)
            scaled = standard(raw[j, span, :], mean, scale)
            rhs[j, span, :] = scaled
            lhs[place, span] = scaled.T
            return 0

        lax.fori_loop(0, depth // chunk, part, 0)
        twin_copy(j).start()
        return 0

    lax.fori_loop(0, pieces, scale_own, 0)

    def relay_copy(w):
        target = jnp.where(w < 4, pick((2, 2, 6, 0, 0, 1, 0, 3)), pick((2, 2, 6, 0, 0, 1, 0, 5)))
        slot = jnp.clip(w + pick((-4, -2, 0, 0, 0, -2, 0, 0)), 0, 5)
        return remote(window.at[w], window.at[slot], relay_s.at[w], panel_r.at[slot], target, samp)

    def arrival(w):
        return remote(window.at[w], window.at[w], relay_s.at[w], panel_r.at[w], twin, samp)

    def relayed(w):
        return (among(0, 1, 5) & (w >= 4)) | ((band == 2) & (w < 2)) | ((band == 7) & (w < 6))

    def job(n):
        w = lookup(ORDER, n - pieces)
        own = n < pieces
        active = own | (w != NONE)
        w = jnp.minimum(w, 7)
        both = jnp.logical_not(own) & (w < 4)
        single = jnp.logical_not(own) & (w >= 4)
        q = jnp.where(own, n, jnp.where(both, w, lax.rem(jnp.maximum(2 * core + w - 4, 0), pieces)))
        return w, own, both, single, active, q

    def needs(n, r):
        w, own, both, single, active, q = job(n)
        return active & (both | (own & ((r == 0) | (core == 1))) | (single & (r == jnp.where(upper, 0, 1))))

    def block_of(n, r):
        w, own, both, single, active, q = job(n)
        return jnp.clip(jnp.where(single, 3, jnp.where(own, 0, 2) + core - r), 0, 3)

    def lower(n):
        return (n < pieces) | jnp.logical_not(upper)

    def part_copy(n, r, k, q, i):
        columns = pl.ds(pl.multiple_of(k * width + q * piece, piece), piece)
        target = (near, middle, far, samp)[i]
        slot = (0, jnp.where(outer, 2, 1), 1, 3)[i]
        source = parts.at[pl.ds(pl.multiple_of(n * 2 * width + r * width + target * rows, rows), rows), :]
        return remote(source, land.at[slot, :, columns], part_s, part_r.at[k, slot],
                      even + r, target)

    def carry_copy(n, r):
        source = parts.at[pl.ds(pl.multiple_of(n * 2 * width + r * width + far * rows, rows), rows), :]
        return remote(source, carry_in.at[n, r], part_s, carry_r.at[n], band, near)

    def turned_copy(n, r, single, q, held):
        k = jnp.clip(jnp.where(single, 3, 2 - core + r), 0, 3)
        source = turned.at[n - pieces, :, pl.ds(pl.multiple_of(r * width, width), width)]
        to = jnp.where(single, 3, jnp.maximum(band - 2, 0))
        if held:
            return remote(source, hold.at[q, r], part_s, hold_r.at[q], to, samp)
        return remote(source, land.at[samp, :, pl.ds(pl.multiple_of(k * width, width), width)],
                      part_s, part_r.at[k, samp], to, q)

    def hold_copy(r, q):
        return remote(hold.at[q, r], land.at[samp, :, (1 + r) * width:(2 + r) * width], hold_s,
                      part_r.at[1 + r, samp], band, q)

    def hold_wait(q):
        return remote(hold.at[q], hold.at[q], hold_s, hold_r.at[q], twin, samp)

    def is_held(both, q):
        return (band == 7) & both & (q != samp)

    def carry_on(n):
        first, second = needs(n, 0), needs(n, 1)

        @pl.when((first | second) & lower(n) & inner)
        def _():
            @pl.when(first & second)
            def _():
                remote(carry_in.at[n], carry_in.at[n], part_s, carry_r.at[n], twin, samp).wait_recv()

            @pl.when(jnp.logical_not(first & second))
            def _():
                remote(carry_in.at[n, 0], carry_in.at[n, 0], part_s, carry_r.at[n], twin, samp).wait_recv()

            def one(r, _):
                @pl.when(needs(n, r))
                def _():
                    w, own, both, single, active, q = job(n)
                    place = pl.ds(pl.multiple_of(n * 2 * width + r * width + far * rows, rows), rows)
                    parts[place, :] = (keep[n, r] + carry_in[n, r].astype(jnp.float32)).astype(jnp.bfloat16)
                    part_copy(n, r, block_of(n, r), q, 2).start()

                return 0

            lax.fori_loop(0, 2, one, 0)

    jobs = pieces + len(ORDER[0])

    def run(n, _):
        event = lookup(RELAYS, n)

        @pl.when(event != NONE)
        def _():
            w = jnp.minimum(event, 5)
            arrival(w).wait_recv()
            relay_copy(w).start()

        @pl.when((n == pieces) & (core == 0))
        def _():
            twin_wait().wait_recv()

        for when, q in HOLD.items():
            @pl.when((band == 5) & (n == when) & (samp != q))
            def _():
                hold_wait(q).wait_recv()
                for r in range(2):
                    hold_copy(r, q).start()

        for source, events in LATE.items():
            for when, (waits, starts) in events.items():
                @pl.when((band == source) & (n == when))
                def _():
                    for i in waits:
                        panel_copy(source, i).wait_send()
                    for i in starts:
                        panel_copy(source, i).start()

        w, own, both, single, active, q = job(n)

        @pl.when(active)
        def _():
            @pl.when(jnp.logical_not(own))
            def _():
                @pl.when(jnp.logical_not(relayed(w)))
                def _():
                    arrival(w).wait_recv()

                slot = jnp.where(both, 0, 1)

                @pl.when((w == 0) | (w == 4))
                def _():
                    remote(coef, coef_in.at[slot], coef_s.at[0], coef_r.at[slot], twin, samp).wait_recv()

                mean, scale = coef_in[slot, pl.ds(q, 1), :], coef_in[slot, pl.ds(pieces + q, 1), :]

                def rescale(i, _):
                    span = pl.ds(pl.multiple_of(i * chunk, chunk), chunk)
                    rhs[pieces, span, :] = standard(window[w, span, :], mean, scale)
                    return 0

                lax.fori_loop(0, depth // chunk, rescale, 0)

            index = jnp.where(own, q, pieces)

            def multiply(i, _):
                r = lax.rem(core + i, 2)

                @pl.when(needs(n, r))
                def _():
                    @pl.when((i == 1) & (n == jnp.where(core == 1, 0, NONE)))
                    def _():
                        twin_wait().wait_recv()

                    place = pl.ds(pl.multiple_of(r * width, width), width)
                    total[...] = jnp.dot(lhs[place, :], rhs[index], preferred_element_type=jnp.float32)

                    @pl.when(lower(n))
                    def _():
                        k = block_of(n, r)
                        parts[pl.ds(pl.multiple_of(n * 2 * width + r * width, width), width), :] = total[...].astype(jnp.bfloat16)

                        @pl.when(outer)
                        def _():
                            carry_copy(n, r).start()

                        part_copy(n, r, k, q, 1).start()
                        part_copy(n, r, k, q, 0).start()

                        @pl.when(core != r)
                        def _():
                            part_copy(n, r, k, q, 3).start()

                        @pl.when(inner)
                        def _():
                            keep[n, r] = total[pl.ds(pl.multiple_of(far * rows, rows), rows), :]

                        @pl.when(core == r)
                        def _():
                            columns = pl.ds(pl.multiple_of(k * width + q * piece, piece), piece)
                            out_ref[:, columns] = total[pl.ds(pl.multiple_of(samp * rows, rows), rows), :]

                    @pl.when(jnp.logical_not(lower(n)))
                    def _():
                        m = jnp.maximum(n, pieces)
                        turned[m - pieces, :, place] = total[...].T.astype(jnp.bfloat16)

                        @pl.when(is_held(both, q))
                        def _():
                            turned_copy(m, r, single, q, True).start()

                        @pl.when(jnp.logical_not(is_held(both, q)))
                        def _():
                            turned_copy(m, r, single, q, False).start()

                return 0

            lax.fori_loop(0, 2, multiply, 0)

        @pl.when(n >= LAG)
        def _():
            carry_on(jnp.maximum(n - LAG, 0))

        return 0

    lax.fori_loop(0, jobs, run, 0)
    for n in range(jobs - LAG, jobs):
        carry_on(n)

    def landed(k, slot):
        place = slice(k * width, (k + 1) * width)
        remote(land.at[slot, :, place], land.at[slot, :, place], part_s, part_r.at[k, slot], twin, samp).wait_recv()

    def finish(k):
        kind = pick([row[k] for row in SOURCES])
        place = slice(k * width, (k + 1) * width)

        @pl.when((kind != 2) & (kind != 3))
        def _():
            landed(k, 0)
            landed(k, 1)

            @pl.when(inner)
            def _():
                landed(k, 2)

            def close(spot, slots):
                result = out_ref[:, spot] if 3 not in slots else land[3, :, spot].astype(jnp.float32)
                for slot in slots[:2]:
                    result = result + land[slot, :, spot].astype(jnp.float32)
                out_ref[:, spot] = result / samples

            @pl.when(kind == 0)
            def _():
                close(place, (0, 1))

            @pl.when(kind == 1)
            def _():
                landed(k, 3)
                close(place, (0, 1, 3))

            @pl.when(kind == 4)
            def _():
                mid = k * width + width // 2
                spot = slice(k * width, mid)
                remote(land.at[3, :, spot], land.at[3, :, spot], part_s, part_r.at[k, 3], twin, samp).wait_recv()
                close(spot, (0, 1, 3))
                close(slice(mid, (k + 1) * width), (0, 1))

            @pl.when(inner)
            def _():
                out_ref[:, place] += land[2, :, place].astype(jnp.float32) / samples

        @pl.when(kind == 3)
        def _():
            out_ref[:, place] = jnp.zeros((rows, width), jnp.float32)

    def gather(k):
        place = slice(k * width, (k + 1) * width)
        for z in range(shards):
            landed(k, z)
        result = land[0, :, place].astype(jnp.float32)
        for z in range(1, shards):
            result = result + land[z, :, place].astype(jnp.float32)
        out_ref[:, place] = result / samples

    for k in range(4):
        finish(k)
    for b, k in ((3, 3), (4, 2), (4, 3), (5, 1), (5, 2)):
        @pl.when(band == b)
        def _():
            gather(k)

    for source in SENDS:
        @pl.when(band == source)
        def _():
            for i in range(len(SENDS[source])):
                if i not in waited.get(source, []):
                    panel_copy(source, i).wait_send()
            for i in range(len(COEFS[source])):
                coef_copy(source, i).wait_send()
    for w in range(6):
        @pl.when(relayed(w))
        def _():
            relay_copy(jnp.int32(w)).wait_send()
    twin_wait().wait_send()

    @pl.when(band == 5)
    def _():
        remote(hold.at[0:shards - 1], hold.at[0:shards - 1], hold_s, hold_r.at[0], twin, samp).wait_send()

    for b in range(bands):
        odd = b % 2
        sent = pieces * (3 + 4 * odd)
        if b >= 6:
            sent += sum(pieces * (2 if w < 4 else 1) for w in ORDER[b] if w != NONE)
        else:
            sent += sum(7 if w < 4 else 4 - odd for w in ORDER[b] if w != NONE)

        @pl.when(band == b)
        def _():
            span = pl.ds(0, sent * rows)
            remote(parts.at[span, :], parts.at[span, :], part_s, part_r.at[0, 0], twin, samp).wait_send()


def ladder(bands, shards, dosage):
    depth, width = dosage.shape
    pieces = shards
    piece = width // pieces
    rows = width // shards
    jobs = pieces + len(ORDER[0])
    f32, b16 = jnp.float32, jnp.bfloat16
    dma = pltpu.SemaphoreType.DMA
    return pl.pallas_call(
        functools.partial(ladder_kernel, bands, shards, depth * shards),
        out_shape=jax.ShapeDtypeStruct((rows, WIN), f32),
        in_specs=[pl.BlockSpec(memory_space=pltpu.HBM)],
        out_specs=pl.BlockSpec(memory_space=pltpu.VMEM),
        scratch_shapes=[
            pltpu.VMEM((pieces, depth, piece), b16),
            pltpu.VMEM((pieces + 1, depth, piece), b16),
            pltpu.VMEM((2 * width, depth), b16),
            pltpu.VMEM((8, depth, piece), b16),
            pltpu.VMEM((jobs * 2 * width, piece), b16),
            pltpu.VMEM((jobs - pieces, rows, 2 * width), b16),
            pltpu.VMEM((width, piece), f32),
            pltpu.VMEM((4, rows, WIN), b16),
            pltpu.VMEM((jobs, 2, rows, piece), b16),
            pltpu.VMEM((4 * pieces, piece), f32),
            pltpu.VMEM((shards - 1, 4 * pieces, piece), f32),
            pltpu.VMEM((2 * pieces, piece), f32),
            pltpu.VMEM((2, 2 * pieces, piece), f32),
            dma((pieces,)),
            dma((6,)), dma((8,)), dma((6,)),
            dma(()), dma(()),
            dma((4,)), dma((2,)),
            dma(()), dma(()),
            dma(()), dma((4, 4)), dma((jobs,)),
            pltpu.VMEM((pieces, 2, rows, width), b16),
            dma(()), dma((pieces,)),
            pltpu.VMEM((jobs, 2, rows, piece), f32),
        ],
        compiler_params=pltpu.CompilerParams(
            collective_id=0, has_side_effects=True, vmem_limit_bytes=52 * 1024 * 1024
        ),
    )(dosage)


def on_device(bands, shards, dosage):
    if bands == len(ORDER) and shards == 4 and dosage.shape[1] == TILE:
        return ladder(bands, shards, dosage)
    return general(bands, shards, dosage)


def solution(mesh):
    return jax.shard_map(
        functools.partial(on_device, mesh.shape["band"], mesh.shape["samp"]),
        mesh=mesh,
        in_specs=(P("samp", "band"),),
        out_specs=P(("band", "samp"), None),
        check_vma=False,
    )
```

```python
import functools

import jax
import jax.numpy as jnp
from jax import lax
from jax.experimental import pallas as pl
from jax.experimental.pallas import tpu as pltpu
from jax.sharding import PartitionSpec as P

TILE = 512
WIN = 2048
PIECES = 4
MESH = pl.DeviceIdType.MESH


def remote(src, dst, send, recv, band, samp):
    return pltpu.make_async_remote_copy(
        src_ref=src, dst_ref=dst, send_sem=send, recv_sem=recv,
        device_id=(band, samp), device_id_type=MESH,
    )


def kernel(bands, shards, reach, samples, dosage_ref, out_ref, own_t, window, stats, stats_in, coef,
           coef_in, parts, far_parts, near_in, far_in, panel_s, panel_r, stat_s, stat_r, coef_s, coef_r,
           part_s, part_r, relay_s, work, raw_ref, load_s):
    band = lax.axis_index("band")
    samp = lax.axis_index("samp")
    depth, width = raw_ref.shape
    load = pltpu.make_async_copy(dosage_ref, raw_ref, load_s)
    load.start()
    rows = width // shards
    piece = width // PIECES
    half = shards // 2
    side, seat = samp // half, lax.rem(samp, half)
    near = [side * half + lax.rem(seat + d, half) for d in range(1, half)]
    far = [(1 - side) * half + lax.rem(seat + d, half) for d in range(half)]
    peers = far + near

    barrier = pltpu.get_barrier_semaphore()
    for peer in peers:
        pl.semaphore_signal(barrier, inc=1, device_id=(band, peer), device_id_type=MESH)
    expected = shards - 1
    for k in range(1, reach + 1):
        @pl.when(band >= k)
        def _():
            pl.semaphore_signal(barrier, inc=1, device_id=(band - k, samp), device_id_type=MESH)

        @pl.when(band + k < bands)
        def _():
            pl.semaphore_signal(barrier, inc=1, device_id=(band + k, samp), device_id_type=MESH)
    expected = expected + jnp.minimum(band, reach) + jnp.minimum(bands - 1 - band, reach)
    pl.semaphore_wait(barrier, expected)
    load.wait()

    def panel_copy(k, j):
        columns = pl.ds(pl.multiple_of(j * piece, piece), piece)
        return remote(raw_ref.at[:, columns], window.at[k - 1, :, columns],
                      panel_s.at[k - 1, j], panel_r.at[k - 1, j], jnp.maximum(band - k, 0), samp)

    even = lax.rem(band, 2) == 0
    turn = lax.rem(band, 4)

    def sends(k):
        if k == 1:
            return jnp.logical_not(even)
        if k == 2:
            return (band >= 2) & (turn != 0)
        return even & (band >= 3)

    def relay_copy(k, j):
        columns = pl.ds(pl.multiple_of(j * piece, piece), piece)
        onward = (k == 2) & jnp.logical_not(even)
        target = jnp.clip(jnp.where(onward, band - 1, band + 1), 0, bands - 1)
        slot = jnp.where(k == 3, 1, jnp.where(even, 0, 2))
        return remote(window.at[k - 1, :, columns], window.at[slot, :, columns],
                      relay_s.at[k - 2, j], panel_r.at[slot, j], target, samp)

    def coef_copy(k):
        return remote(coef, coef_in.at[k - 1], coef_s.at[k - 1], coef_r.at[k - 1],
                      jnp.maximum(band - k, 0), samp)

    def part_copy(k, j, d):
        columns = pl.ds(pl.multiple_of(k * width + j * piece, piece), piece)
        source, landing, slot = (far_parts, far_in, d) if d < half else (parts, near_in, d - half)
        return remote(source.at[pl.ds(pl.multiple_of(peers[d] * rows, rows), rows), columns],
                      landing.at[slot, :, columns],
                      part_s.at[k, j, d], part_r.at[k, j, d], band, peers[d])

    def start_panel(k, j):
        @pl.when(sends(k))
        def _():
            panel_copy(k, j).start()

    early = [(k, 0) for k in range(1, reach + 1)]
    later = [(k, j) for j in range(PIECES) for k in range(1, reach + 1) if (k, j) not in early]
    for k, j in early:
        start_panel(k, j)

    step = 64

    def add(i, carry):
        x = raw_ref[pl.ds(pl.multiple_of(i * step, step), step), :].astype(jnp.float32)
        seen = jnp.where(x >= 0.0, 1.0, 0.0)
        value = jnp.where(x >= 0.0, x, 0.0)
        fold = lambda a: jnp.sum(a.reshape(step // 8, 8, width), axis=0)
        return carry[0] + fold(seen), carry[1] + fold(value), carry[2] + fold(value * value)

    zero = jnp.zeros((8, width), jnp.float32)
    sums = lax.fori_loop(0, depth // step, add, (zero, zero, zero))
    stats[...] = jnp.concatenate(
        [jnp.sum(a, axis=0, keepdims=True) for a in sums] + [jnp.zeros((5, width), jnp.float32)], axis=0
    )
    stat_copies = [
        remote(stats, stats_in.at[d], stat_s.at[d], stat_r.at[d], band, peers[d])
        for d in range(shards - 1)
    ]
    for copy in stat_copies:
        copy.start()
    for copy in stat_copies:
        copy.wait()
    sums = stats[...]
    for d in range(shards - 1):
        sums = sums + stats_in[d]
    count, total, square = sums[0:1], sums[1:2], sums[2:3]
    mean = (total + 1.0) / (count + 1.0)
    spread = (square - 2.0 * mean * total + count * mean * mean + 0.5) / (count + 1.0)
    coef[...] = jnp.concatenate(
        [mean, lax.rsqrt(spread), jnp.zeros((6, width), jnp.float32)], axis=0
    )
    for k in range(1, reach + 1):
        @pl.when(band >= k)
        def _():
            coef_copy(k).start()
    for k, j in later:
        start_panel(k, j)

    chunk = 256

    def standard(x, mean, scale):
        x = x.astype(jnp.float32)
        return jnp.where(x >= 0.0, (x - mean) * scale, 0.0).astype(jnp.bfloat16)

    own = window.at[reach]

    def scale_own(i, _):
        span = pl.ds(pl.multiple_of(i * chunk, chunk), chunk)
        scaled = standard(raw_ref[span, :], coef[0:1, :], coef[1:2, :])
        own[span, :] = scaled
        own_t[:, span] = scaled.T
        return 0

    lax.fori_loop(0, depth // chunk, scale_own, 0)

    def correlate(k, j, panel):
        place = pl.ds(pl.multiple_of(k * width + j * piece, piece), piece)

        def block(i, _):
            span = pl.ds(pl.multiple_of(i * 256, 256), 256)
            total = jnp.dot(own_t[span, :], panel[...], preferred_element_type=jnp.float32)
            parts[span, place] = total
            far_parts[span, place] = total.astype(jnp.bfloat16)
            return 0

        lax.fori_loop(0, width // 256, block, 0)
        for d in range(shards - 1):
            part_copy(k, j, d).start()
        out_ref[:, place] = parts[pl.ds(pl.multiple_of(samp * rows, rows), rows), place]

    def finish(k, j):
        place = slice(k * width + j * piece, k * width + (j + 1) * piece)
        total = out_ref[:, place]
        for d in range(shards - 1):
            part_copy(k, j, d).wait()
            landed = far_in[d, :, place] if d < half else near_in[d - half, :, place]
            total = total + landed.astype(jnp.float32)
        out_ref[:, place] = total / samples

    for j in range(PIECES):
        correlate(0, j, own.at[:, pl.ds(j * piece, piece)])
    ahead = [(1, 0)]
    for j in range(PIECES):
        ahead += [(1, j + 1)] if j + 1 < PIECES else []
        ahead += [(k, j) for k in range(2, reach + 1)]
    level = [(k, j) for j in range(PIECES) for k in range(reach, 0, -1)]
    for (k_even, j_even), (k_odd, j_odd) in zip(ahead, level):
        k_last = k_odd if k_odd == 1 else reach + 2 - k_odd
        k = jnp.where(even, k_even, jnp.where(turn == 3, k_last, k_odd))
        j = jnp.where(even, j_even, j_odd)
        columns = pl.ds(pl.multiple_of(j * piece, piece), piece)

        @pl.when(band + k < bands)
        def _():
            panel_copy(k, j).wait_recv()

            @pl.when((k == 2) | ((k == 3) & (turn == 1)))
            def _():
                relay_copy(k, j).start()

            @pl.when(j == 0)
            def _():
                coef_copy(k).wait_recv()

            mean, scale = coef_in[k - 1, 0:1, columns], coef_in[k - 1, 1:2, columns]

            def rescale(i, _):
                span = pl.ds(pl.multiple_of(i * chunk, chunk), chunk)
                work[span, :] = standard(window[k - 1, span, columns], mean, scale)
                return 0

            lax.fori_loop(0, depth // chunk, rescale, 0)
            correlate(k, j, work)

    for j in range(PIECES):
        finish(0, j)
    for j in range(PIECES):
        for k in range(1, reach + 1):
            @pl.when(band + k < bands)
            def _():
                finish(k, j)

            @pl.when(band + k >= bands)
            def _():
                place = slice(k * width + j * piece, k * width + (j + 1) * piece)
                out_ref[:, place] = jnp.zeros((rows, piece), jnp.float32)
    for k in range(1, reach + 1):
        @pl.when(band >= k)
        def _():
            coef_copy(k).wait_send()

        for j in range(PIECES):
            @pl.when(sends(k))
            def _():
                panel_copy(k, j).wait_send()

            if k > 1:
                @pl.when((band + k < bands) & ((k == 2) | (turn == 1)))
                def _():
                    relay_copy(k, j).wait_send()


def general(bands, shards, dosage):
    depth, width = dosage.shape
    reach = (WIN - TILE + width - 1) // width
    rows = width // shards
    f32 = jnp.float32
    dma = pltpu.SemaphoreType.DMA
    return pl.pallas_call(
        functools.partial(kernel, bands, shards, reach, depth * shards),
        out_shape=jax.ShapeDtypeStruct((rows, WIN), f32),
        in_specs=[pl.BlockSpec(memory_space=pltpu.HBM)],
        out_specs=pl.BlockSpec(memory_space=pltpu.VMEM),
        scratch_shapes=[
            pltpu.VMEM((width, depth), jnp.bfloat16),
            pltpu.VMEM((reach + 1, depth, width), jnp.bfloat16),
            pltpu.VMEM((8, width), f32),
            pltpu.VMEM((shards - 1, 8, width), f32),
            pltpu.VMEM((8, width), f32),
            pltpu.VMEM((reach, 8, width), f32),
            pltpu.VMEM((width, WIN), f32),
            pltpu.VMEM((width, WIN), jnp.bfloat16),
            pltpu.VMEM((max(shards // 2 - 1, 1), rows, WIN), f32),
            pltpu.VMEM((shards // 2, rows, WIN), jnp.bfloat16),
            dma((reach, PIECES)), dma((reach, PIECES)),
            dma((shards - 1,)), dma((shards - 1,)),
            dma((reach,)), dma((reach,)),
            dma((reach + 1, PIECES, shards - 1)), dma((reach + 1, PIECES, shards - 1)),
            dma((reach - 1, PIECES)),
            pltpu.VMEM((depth, width // PIECES), jnp.bfloat16),
            pltpu.VMEM((depth, width), jnp.bfloat16),
            dma(()),
        ],
        compiler_params=pltpu.CompilerParams(
            collective_id=0, has_side_effects=True, vmem_limit_bytes=48 * 1024 * 1024
        ),
    )(dosage)


ORDER = (
    (4, 5, 0, 1, 2, 3, 15, 15),
    (4, 0, 5, 1, 2, 3, 15, 15),
    (0, 1, 2, 3, 15, 15, 15, 15),
    (0, 1, 2, 3, 15, 15, 15, 15),
    (15, 15, 15, 15, 15, 15, 15, 15),
    (15, 15, 15, 15, 15, 15, 15, 15),
    (0, 2, 1, 3, 15, 15, 15, 15),
    (4, 0, 5, 1, 2, 3, 6, 7),
)
RELAYS = (
    {0: 4, 2: 5},
    {4: 4, 6: 5},
    {4: 0, 5: 1},
    {},
    {},
    {7: 4, 8: 5},
    {},
    {0: 4, 1: 0, 3: 5, 4: 1, 6: 2, 9: 3},
)
SENDS = {
    2: [(0, 0, 0), (1, 0, 1), (2, 0, 2), (3, 0, 3)],
    3: [(2, 7, 4), (3, 7, 5), (0, 1, 0), (1, 1, 1), (0, 7, 6), (1, 7, 7)],
    4: [(0, 0, 4), (1, 0, 5), (2, 1, 4), (3, 1, 5), (2, 6, 2), (3, 6, 3)],
    5: [(0, 7, 0), (1, 7, 1), (2, 7, 2), (3, 7, 3)],
}
EARLY = {2: (0,), 3: (0, 2), 4: (0,), 5: (0,)}
LATE = {3: {6: ((0,), (4, 5))}, 4: {0: ((0,), (2, 3)), 2: ((2,), (4, 5))}}
COEFS = {2: [(0, 0)], 3: [(1, 0), (7, 1)], 4: [(0, 1), (1, 1), (2, 0), (6, 0)], 5: [(7, 0), (3, 0)]}
SOURCES = ((0, 1, 0, 1), (0, 1, 0, 4), (0, 1, 0, 1), (0, 1, 0, 2), (0, 1, 2, 2), (0, 2, 2, 3), (0, 1, 3, 3), (0, 3, 3, 3))
CROSS = {3: (7,), 4: (6,), 6: (4,), 7: (3,)}
HOLD = {6: 0, 7: 1, 8: 2, 9: 3}
LAG = 3
NONE = 15


def peers(bands):
    plane = {b: {b + 1 - 2 * (b % 2)} for b in range(bands)}
    pairs = [(b, target) for b in SENDS for _, target, _ in SENDS[b]] + [(b, target) for b in COEFS for target, _ in COEFS[b]]
    pairs += [(0, 2), (1, 2), (2, 6), (5, 1), (7, 3), (7, 5)] + [(b, target) for b in CROSS for target in CROSS[b]]
    for a, b in pairs:
        plane[a].add(b)
        plane[b].add(a)
    line = {b: {b, b + 1 - 2 * (b % 2), *CROSS.get(b, ())} for b in range(bands)}
    return plane, line


def ladder_kernel(bands, shards, samples, dosage_ref, out_ref, raw, rhs, lhs, window, parts, turned, total,
                  land, carry_in, stats, stats_in, coef, coef_in, load_s, panel_s, panel_r, relay_s, stat_s,
                  stat_r, coef_s, coef_r, twin_s, twin_r, part_s, part_r, carry_r, hold, hold_s, hold_r, keep):
    band = lax.axis_index("band")
    samp = lax.axis_index("samp")
    pieces, depth, piece = raw.shape
    width = pieces * piece
    rows = width // shards
    core = lax.rem(band, 2)
    even = band - core
    twin = band + 1 - 2 * core
    upper = band >= 6
    outer = (samp == 0) | (samp == 3)
    inner = jnp.logical_not(outer)
    near = samp + 1 - 2 * lax.rem(samp, 2)
    middle = jnp.where(samp < 2, 2, 1)
    far = jnp.where(samp < 2, 3, 0)

    def pick(values):
        result = jnp.int32(values[0])
        for i, value in enumerate(values[1:], 1):
            result = jnp.where(band == i, jnp.int32(value), result)
        return result

    def among(*which):
        result = band == which[0]
        for i in which[1:]:
            result = result | (band == i)
        return result

    def lookup(table, n):
        result = jnp.int32(NONE)
        for b in range(bands):
            for i, value in (table[b].items() if isinstance(table[b], dict) else enumerate(table[b])):
                if value != NONE:
                    result = jnp.where((band == b) & (n == i), jnp.int32(value), result)
        return result

    loads = [
        pltpu.make_async_copy(dosage_ref.at[:, pl.ds(j * piece, piece)], raw.at[j], load_s.at[j])
        for j in range(pieces)
    ]
    for load in loads:
        load.start()
    barrier = pltpu.get_barrier_semaphore()
    plane, line = peers(bands)
    for b in range(bands):
        @pl.when(band == b)
        def _():
            for peer in sorted(plane[b]):
                pl.semaphore_signal(barrier, inc=1, device_id=(peer, samp), device_id_type=MESH)
            for peer in sorted(line[b]):
                for d in range(1, shards):
                    pl.semaphore_signal(barrier, inc=1, device_id=(peer, lax.rem(samp + d, shards)),
                                        device_id_type=MESH)

    step = 256

    def measure(j, _):
        def add(i, carry):
            x = raw[j, pl.ds(pl.multiple_of(i * step, step), step), :].astype(jnp.float32)
            seen = jnp.where(x >= 0.0, 1.0, 0.0)
            value = jnp.maximum(x, 0.0)
            fold = lambda a: jnp.sum(a.reshape(step // 8, 8, piece), axis=0)
            return carry[0] + fold(seen), carry[1] + fold(value), carry[2] + fold(value * value)

        zero = jnp.zeros((8, piece), jnp.float32)
        sums = lax.fori_loop(0, depth // step, add, (zero, zero, zero))
        for i, a in enumerate(sums):
            stats[pl.ds(pieces * i + j, 1), :] = jnp.sum(a, axis=0, keepdims=True)
        return 0

    for load in loads:
        load.wait()
    stats[3 * pieces:, :] = jnp.zeros((pieces, piece), jnp.float32)
    lax.fori_loop(0, pieces, measure, 0)
    pl.semaphore_wait(barrier, pick([len(plane[b]) + (shards - 1) * len(line[b]) for b in range(bands)]))

    def panel_copy(source, i):
        j, target, slot = SENDS[source][i]
        return remote(raw.at[j], window.at[slot], panel_s.at[i], panel_r.at[slot], target, samp)

    late = {source: [i for _, (_, starts) in events.items() for i in starts] for source, events in LATE.items()}
    waited = {source: [i for _, (waits, _) in events.items() for i in waits] for source, events in LATE.items()}
    for source in SENDS:
        @pl.when(band == source)
        def _():
            for i in EARLY[source]:
                panel_copy(source, i).start()

    stat_copies = [
        remote(stats, stats_in.at[d - 1], stat_s, stat_r, band, lax.rem(samp + d, shards))
        for d in range(1, shards)
    ]
    for copy in stat_copies:
        copy.start()
    remote(stats_in, stats_in, stat_s, stat_r, twin, samp).wait()
    sums = stats[...]
    for d in range(shards - 1):
        sums = sums + stats_in[d]
    count, sum1, square = (sums[pieces * i:pieces * (i + 1)] for i in range(3))
    mean = (sum1 + 1.0) / (count + 1.0)
    spread = (square - 2.0 * mean * sum1 + count * mean * mean + 0.5) / (count + 1.0)
    coef[0:pieces, :] = mean
    coef[pieces:2 * pieces, :] = lax.rsqrt(spread)

    def coef_copy(source, i):
        target, slot = COEFS[source][i]
        return remote(coef, coef_in.at[slot], coef_s.at[i], coef_r.at[slot], target, samp)

    for source in COEFS:
        @pl.when(band == source)
        def _():
            for i in range(len(COEFS[source])):
                coef_copy(source, i).start()
            for i in range(len(SENDS[source])):
                if i not in late.get(source, []) and i not in EARLY[source]:
                    panel_copy(source, i).start()

    chunk = 512

    def standard(x, mean, scale):
        x = x.astype(jnp.float32)
        return jnp.where(x >= 0.0, (x - mean) * scale, 0.0).astype(jnp.bfloat16)

    def twin_copy(j):
        place = pl.ds(pl.multiple_of(core * width + j * piece, piece), piece)
        return remote(lhs.at[place, :], lhs.at[place, :], twin_s, twin_r, twin, samp)

    def twin_wait():
        place = pl.ds(pl.multiple_of((1 - core) * width, width), width)
        return remote(lhs.at[place, :], lhs.at[place, :], twin_s, twin_r, twin, samp)

    def scale_own(j, _):
        place = pl.ds(pl.multiple_of(core * width + j * piece, piece), piece)
        mean, scale = coef[pl.ds(j, 1), :], coef[pl.ds(pieces + j, 1), :]

        def part(i, _):
            span = pl.ds(pl.multiple_of(i * chunk, chunk), chunk)
            scaled = standard(raw[j, span, :], mean, scale)
            rhs[j, span, :] = scaled
            lhs[place, span] = scaled.T
            return 0

        lax.fori_loop(0, depth // chunk, part, 0)
        twin_copy(j).start()
        return 0

    lax.fori_loop(0, pieces, scale_own, 0)

    def relay_copy(w):
        target = jnp.where(w < 4, pick((2, 2, 6, 0, 0, 1, 0, 3)), pick((2, 2, 6, 0, 0, 1, 0, 5)))
        slot = jnp.clip(w + pick((-4, -2, 0, 0, 0, -2, 0, 0)), 0, 5)
        return remote(window.at[w], window.at[slot], relay_s.at[w], panel_r.at[slot], target, samp)

    def arrival(w):
        return remote(window.at[w], window.at[w], relay_s.at[w], panel_r.at[w], twin, samp)

    def relayed(w):
        return (among(0, 1, 5) & (w >= 4)) | ((band == 2) & (w < 2)) | ((band == 7) & (w < 6))

    def job(n):
        w = lookup(ORDER, n - pieces)
        own = n < pieces
        active = own | (w != NONE)
        w = jnp.minimum(w, 7)
        both = jnp.logical_not(own) & (w < 4)
        single = jnp.logical_not(own) & (w >= 4)
        q = jnp.where(own, n, jnp.where(both, w, lax.rem(jnp.maximum(2 * core + w - 4, 0), pieces)))
        return w, own, both, single, active, q

    def needs(n, r):
        w, own, both, single, active, q = job(n)
        return active & (both | (own & ((r == 0) | (core == 1))) | (single & (r == jnp.where(upper, 0, 1))))

    def block_of(n, r):
        w, own, both, single, active, q = job(n)
        return jnp.clip(jnp.where(single, 3, jnp.where(own, 0, 2) + core - r), 0, 3)

    def lower(n):
        return (n < pieces) | jnp.logical_not(upper)

    def part_copy(n, r, k, q, i):
        columns = pl.ds(pl.multiple_of(k * width + q * piece, piece), piece)
        target = (near, middle, far, samp)[i]
        slot = (0, jnp.where(outer, 2, 1), 1, 3)[i]
        source = parts.at[pl.ds(pl.multiple_of(n * 2 * width + r * width + target * rows, rows), rows), :]
        return remote(source, land.at[slot, :, columns], part_s, part_r.at[k, slot],
                      even + r, target)

    def carry_copy(n, r):
        source = parts.at[pl.ds(pl.multiple_of(n * 2 * width + r * width + far * rows, rows), rows), :]
        return remote(source, carry_in.at[n, r], part_s, carry_r.at[n], band, near)

    def turned_copy(n, r, single, q, held):
        k = jnp.clip(jnp.where(single, 3, 2 - core + r), 0, 3)
        source = turned.at[n - pieces, :, pl.ds(pl.multiple_of(r * width, width), width)]
        to = jnp.where(single, 3, jnp.maximum(band - 2, 0))
        if held:
            return remote(source, hold.at[q, r], part_s, hold_r.at[q], to, samp)
        return remote(source, land.at[samp, :, pl.ds(pl.multiple_of(k * width, width), width)],
                      part_s, part_r.at[k, samp], to, q)

    def hold_copy(r, q):
        return remote(hold.at[q, r], land.at[samp, :, (1 + r) * width:(2 + r) * width], hold_s,
                      part_r.at[1 + r, samp], band, q)

    def hold_wait(q):
        return remote(hold.at[q], hold.at[q], hold_s, hold_r.at[q], twin, samp)

    def is_held(both, q):
        return (band == 7) & both & (q != samp)

    def carry_on(n):
        first, second = needs(n, 0), needs(n, 1)

        @pl.when((first | second) & lower(n) & inner)
        def _():
            @pl.when(first & second)
            def _():
                remote(carry_in.at[n], carry_in.at[n], part_s, carry_r.at[n], twin, samp).wait_recv()

            @pl.when(jnp.logical_not(first & second))
            def _():
                remote(carry_in.at[n, 0], carry_in.at[n, 0], part_s, carry_r.at[n], twin, samp).wait_recv()

            def one(r, _):
                @pl.when(needs(n, r))
                def _():
                    w, own, both, single, active, q = job(n)
                    place = pl.ds(pl.multiple_of(n * 2 * width + r * width + far * rows, rows), rows)
                    parts[place, :] = (keep[n, r] + carry_in[n, r].astype(jnp.float32)).astype(jnp.bfloat16)
                    part_copy(n, r, block_of(n, r), q, 2).start()

                return 0

            lax.fori_loop(0, 2, one, 0)

    jobs = pieces + len(ORDER[0])

    def run(n, _):
        event = lookup(RELAYS, n)

        @pl.when(event != NONE)
        def _():
            w = jnp.minimum(event, 5)
            arrival(w).wait_recv()
            relay_copy(w).start()

        @pl.when((n == pieces) & (core == 0))
        def _():
            twin_wait().wait_recv()

        for when, q in HOLD.items():
            @pl.when((band == 5) & (n == when) & (samp != q))
            def _():
                hold_wait(q).wait_recv()
                for r in range(2):
                    hold_copy(r, q).start()

        for source, events in LATE.items():
            for when, (waits, starts) in events.items():
                @pl.when((band == source) & (n == when))
                def _():
                    for i in waits:
                        panel_copy(source, i).wait_send()
                    for i in starts:
                        panel_copy(source, i).start()

        w, own, both, single, active, q = job(n)

        @pl.when(active)
        def _():
            @pl.when(jnp.logical_not(own))
            def _():
                @pl.when(jnp.logical_not(relayed(w)))
                def _():
                    arrival(w).wait_recv()

                slot = jnp.where(both, 0, 1)

                @pl.when((w == 0) | (w == 4))
                def _():
                    remote(coef, coef_in.at[slot], coef_s.at[0], coef_r.at[slot], twin, samp).wait_recv()

                mean, scale = coef_in[slot, pl.ds(q, 1), :], coef_in[slot, pl.ds(pieces + q, 1), :]

                def rescale(i, _):
                    span = pl.ds(pl.multiple_of(i * chunk, chunk), chunk)
                    rhs[pieces, span, :] = standard(window[w, span, :], mean, scale)
                    return 0

                lax.fori_loop(0, depth // chunk, rescale, 0)

            index = jnp.where(own, q, pieces)

            def multiply(i, _):
                r = lax.rem(core + i, 2)

                @pl.when(needs(n, r))
                def _():
                    @pl.when((i == 1) & (n == jnp.where(core == 1, 0, NONE)))
                    def _():
                        twin_wait().wait_recv()

                    place = pl.ds(pl.multiple_of(r * width, width), width)
                    total[...] = jnp.dot(lhs[place, :], rhs[index], preferred_element_type=jnp.float32)

                    @pl.when(lower(n))
                    def _():
                        k = block_of(n, r)
                        parts[pl.ds(pl.multiple_of(n * 2 * width + r * width, width), width), :] = total[...].astype(jnp.bfloat16)

                        @pl.when(outer)
                        def _():
                            carry_copy(n, r).start()

                        part_copy(n, r, k, q, 1).start()
                        part_copy(n, r, k, q, 0).start()

                        @pl.when(core != r)
                        def _():
                            part_copy(n, r, k, q, 3).start()

                        @pl.when(inner)
                        def _():
                            keep[n, r] = total[pl.ds(pl.multiple_of(far * rows, rows), rows), :]

                        @pl.when(core == r)
                        def _():
                            columns = pl.ds(pl.multiple_of(k * width + q * piece, piece), piece)
                            out_ref[:, columns] = total[pl.ds(pl.multiple_of(samp * rows, rows), rows), :]

                    @pl.when(jnp.logical_not(lower(n)))
                    def _():
                        m = jnp.maximum(n, pieces)
                        turned[m - pieces, :, place] = total[...].T.astype(jnp.bfloat16)

                        @pl.when(is_held(both, q))
                        def _():
                            turned_copy(m, r, single, q, True).start()

                        @pl.when(jnp.logical_not(is_held(both, q)))
                        def _():
                            turned_copy(m, r, single, q, False).start()

                return 0

            lax.fori_loop(0, 2, multiply, 0)

        @pl.when(n >= LAG)
        def _():
            carry_on(jnp.maximum(n - LAG, 0))

        return 0

    lax.fori_loop(0, jobs, run, 0)
    for n in range(jobs - LAG, jobs):
        carry_on(n)

    def landed(k, slot):
        place = slice(k * width, (k + 1) * width)
        remote(land.at[slot, :, place], land.at[slot, :, place], part_s, part_r.at[k, slot], twin, samp).wait_recv()

    def finish(k):
        kind = pick([row[k] for row in SOURCES])
        place = slice(k * width, (k + 1) * width)

        @pl.when((kind != 2) & (kind != 3))
        def _():
            landed(k, 0)
            landed(k, 1)

            @pl.when(inner)
            def _():
                landed(k, 2)

            def close(spot, slots):
                result = out_ref[:, spot] if 3 not in slots else land[3, :, spot].astype(jnp.float32)
                for slot in slots[:2]:
                    result = result + land[slot, :, spot].astype(jnp.float32)
                out_ref[:, spot] = result / samples

            @pl.when(kind == 0)
            def _():
                close(place, (0, 1))

            @pl.when(kind == 1)
            def _():
                landed(k, 3)
                close(place, (0, 1, 3))

            @pl.when(kind == 4)
            def _():
                mid = k * width + width // 2
                spot = slice(k * width, mid)
                remote(land.at[3, :, spot], land.at[3, :, spot], part_s, part_r.at[k, 3], twin, samp).wait_recv()
                close(spot, (0, 1, 3))
                close(slice(mid, (k + 1) * width), (0, 1))

            @pl.when(inner)
            def _():
                out_ref[:, place] += land[2, :, place].astype(jnp.float32) / samples

        @pl.when(kind == 3)
        def _():
            out_ref[:, place] = jnp.zeros((rows, width), jnp.float32)

    def gather(k):
        place = slice(k * width, (k + 1) * width)
        for z in range(shards):
            landed(k, z)
        result = land[0, :, place].astype(jnp.float32)
        for z in range(1, shards):
            result = result + land[z, :, place].astype(jnp.float32)
        out_ref[:, place] = result / samples

    for k in range(4):
        finish(k)
    for b, k in ((3, 3), (4, 2), (4, 3), (5, 1), (5, 2)):
        @pl.when(band == b)
        def _():
            gather(k)

    for source in SENDS:
        @pl.when(band == source)
        def _():
            for i in range(len(SENDS[source])):
                if i not in waited.get(source, []):
                    panel_copy(source, i).wait_send()
            for i in range(len(COEFS[source])):
                coef_copy(source, i).wait_send()
    for w in range(6):
        @pl.when(relayed(w))
        def _():
            relay_copy(jnp.int32(w)).wait_send()
    twin_wait().wait_send()

    @pl.when(band == 5)
    def _():
        remote(hold.at[0:shards - 1], hold.at[0:shards - 1], hold_s, hold_r.at[0], twin, samp).wait_send()

    for b in range(bands):
        odd = b % 2
        sent = pieces * (3 + 4 * odd)
        if b >= 6:
            sent += sum(pieces * (2 if w < 4 else 1) for w in ORDER[b] if w != NONE)
        else:
            sent += sum(7 if w < 4 else 4 - odd for w in ORDER[b] if w != NONE)

        @pl.when(band == b)
        def _():
            span = pl.ds(0, sent * rows)
            remote(parts.at[span, :], parts.at[span, :], part_s, part_r.at[0, 0], twin, samp).wait_send()


def ladder(bands, shards, dosage):
    depth, width = dosage.shape
    pieces = shards
    piece = width // pieces
    rows = width // shards
    jobs = pieces + len(ORDER[0])
    f32, b16 = jnp.float32, jnp.bfloat16
    dma = pltpu.SemaphoreType.DMA
    return pl.pallas_call(
        functools.partial(ladder_kernel, bands, shards, depth * shards),
        out_shape=jax.ShapeDtypeStruct((rows, WIN), f32),
        in_specs=[pl.BlockSpec(memory_space=pltpu.HBM)],
        out_specs=pl.BlockSpec(memory_space=pltpu.VMEM),
        scratch_shapes=[
            pltpu.VMEM((pieces, depth, piece), b16),
            pltpu.VMEM((pieces + 1, depth, piece), b16),
            pltpu.VMEM((2 * width, depth), b16),
            pltpu.VMEM((8, depth, piece), b16),
            pltpu.VMEM((jobs * 2 * width, piece), b16),
            pltpu.VMEM((jobs - pieces, rows, 2 * width), b16),
            pltpu.VMEM((width, piece), f32),
            pltpu.VMEM((4, rows, WIN), b16),
            pltpu.VMEM((jobs, 2, rows, piece), b16),
            pltpu.VMEM((4 * pieces, piece), f32),
            pltpu.VMEM((shards - 1, 4 * pieces, piece), f32),
            pltpu.VMEM((2 * pieces, piece), f32),
            pltpu.VMEM((2, 2 * pieces, piece), f32),
            dma((pieces,)),
            dma((6,)), dma((8,)), dma((6,)),
            dma(()), dma(()),
            dma((4,)), dma((2,)),
            dma(()), dma(()),
            dma(()), dma((4, 4)), dma((jobs,)),
            pltpu.VMEM((pieces, 2, rows, width), b16),
            dma(()), dma((pieces,)),
            pltpu.VMEM((jobs, 2, rows, piece), f32),
        ],
        compiler_params=pltpu.CompilerParams(
            collective_id=0, has_side_effects=True, vmem_limit_bytes=52 * 1024 * 1024
        ),
    )(dosage)


def on_device(bands, shards, dosage):
    if bands == len(ORDER) and shards == 4 and dosage.shape[1] == TILE:
        return ladder(bands, shards, dosage)
    return general(bands, shards, dosage)


def solution(mesh):
    return jax.shard_map(
        functools.partial(on_device, mesh.shape["band"], mesh.shape["samp"]),
        mesh=mesh,
        in_specs=(P("samp", "band"),),
        out_specs=P(("band", "samp"), None),
        check_vma=False,
    )
```
